32 devices in a mesh: gx: 8 (over z, x), gy: 4 (over y, core).
Axes of the slice: x: 2, y: 2, z: 4, core: 2. Of those that a mesh axis runs over, the one named last changes fastest.
Arguments:
- velocity: float32 [3, 128, 256, 256], P(None, 'gx', 'gy'), may hold values from -6 to 6
Outputs:
- details_one: float32 [7, 9, 64, 128, 128], P(None, None, 'gx', 'gy')
- stress_one: float32 [6, 64, 128, 128], P(None, 'gx', 'gy')
- details_two: float32 [7, 9, 32, 64, 64], P(None, None, 'gx', 'gy')
- stress_two: float32 [6, 32, 64, 64], P(None, 'gx', 'gy')
- details_three: float32 [7, 9, 16, 32, 32], P(None, None, 'gx', 'gy')
- stress_three: float32 [6, 16, 32, 32], P(None, 'gx', 'gy')
- coarse_velocity: float32 [3, 16, 32, 32], P(None, 'gx', 'gy')
The draws below stay inside these ranges and needn't reach their ends.
All inputs are finite; a program needn't handle non-finite values.
Results may differ from the reference program's by a relative error of at most 0.0003.
Values sent between devices are 32-bit elements; how exact they have to be, the bound alone decides.
No kernel may reach another device: no remote copies, remote signals or barrier semaphores. Data moves between devices by JAX's collectives and lax.ppermute only.
A program may use at most 256 MiB of HBM per device.

```python
import jax
import jax.numpy as jnp
from jax import lax

NZ = 256
NX = 128
NY = 256


def block_scale(own_key, shape, shards, low, high):
    def one(axis_at, parts):
        steps = jax.random.uniform(jax.random.fold_in(jax.random.fold_in(own_key, 6), axis_at), (parts,), jnp.float32, low / len(shards), high / len(shards))
        return jnp.repeat(jnp.exp(steps), shape[axis_at] // parts).reshape((-1,) + (1,) * (len(shape) - axis_at - 1))

    level = one(*shards[0])
    for cut in shards[1:]:
        level = level * one(*cut)
    return level


def gaussian(rng, shape, scale, limit, shards=(), dtype=jnp.bfloat16):
    factor_of = block_scale(rng, shape, shards, -0.22, 0.18) if shards else 1.0
    result = jax.random.normal(rng, shape, jnp.float32) * scale * factor_of
    return jnp.minimum(jnp.maximum(result, -limit), limit).astype(dtype)


def setup_inputs(seed: int = 0) -> dict:
    keys = jax.random.split(jax.random.key(seed), 2)
    velocity = gaussian(keys[0], (3, NX, NY, NZ), 1.0, 6.0, ((1, 8), (2, 4)), jnp.float32)
    return {"velocity": velocity}


predict_one = -1.586134342
update_one = -0.05298011854
predict_two = 0.8829110762
update_two = 0.4435068522
scaling = 1.149604398
product_pairs = ((0, 0), (0, 1), (0, 2), (1, 1), (1, 2), (2, 2))


def lifting(volume, dimension, next_even, prev_odd):
    length = volume.shape[dimension]
    even_cells = lax.slice_in_dim(volume, 0, length, 2, dimension)
    odd_cells = lax.slice_in_dim(volume, 1, length, 2, dimension)
    odd_cells = odd_cells + predict_one * (even_cells + next_even(even_cells))
    even_cells = even_cells + update_one * (odd_cells + prev_odd(odd_cells))
    odd_cells = odd_cells + predict_two * (even_cells + next_even(even_cells))
    even_cells = even_cells + update_two * (odd_cells + prev_odd(odd_cells))
    return jnp.concatenate([even_cells * scaling, odd_cells / scaling], axis=0)


def periodic_next(dimension):
    return lambda values: jnp.roll(values, -1, axis=dimension)


def periodic_prev(dimension):
    return lambda values: jnp.roll(values, 1, axis=dimension)


def mirror_next(dimension):
    def shifted(values):
        extent = values.shape[dimension]
        return jnp.concatenate([lax.slice_in_dim(values, 1, extent, 1, dimension), lax.slice_in_dim(values, extent - 1, extent, 1, dimension)], axis=dimension)
    return shifted


def mirror_prev(dimension):
    def shifted(values):
        extent = values.shape[dimension]
        return jnp.concatenate([lax.slice_in_dim(values, 0, 1, 1, dimension), lax.slice_in_dim(values, 0, extent - 1, 1, dimension)], axis=dimension)
    return shifted


def stresses_of(approximation):
    return jnp.stack([approximation[3 + position] - approximation[pair[0]] * approximation[pair[1]] for position, pair in enumerate(product_pairs)])


def reference(velocity):
    products = jnp.stack([velocity[pair[0]] * velocity[pair[1]] for pair in product_pairs])
    all_fields = jnp.concatenate([velocity, products], axis=0)
    results = []
    for level_index in range(3):
        subbands = lifting(all_fields, 1, periodic_next(1), periodic_prev(1))
        subbands = lifting(subbands, 2, periodic_next(2), periodic_prev(2))
        subbands = lifting(subbands, 3, mirror_next(3), mirror_prev(3))
        grouped = subbands.reshape((8, 9) + subbands.shape[1:])
        approximation = grouped[0]
        results.append(grouped[1:])
        results.append(stresses_of(approximation))
        all_fields = approximation
    return (results[0], results[1], results[2], results[3], results[4], results[5], approximation[:3])
```

```python
import jax
import jax.numpy as jnp
import numpy as np
from jax import lax
from jax.experimental import pallas as pl
from jax.experimental.pallas import tpu as pltpu
from jax.sharding import PartitionSpec as P

predict_one = -1.586134342
update_one = -0.05298011854
predict_two = 0.8829110762
update_two = 0.4435068522
scaling = 1.149604398
product_pairs = ((0, 0), (0, 1), (0, 2), (1, 1), (1, 2), (2, 2))
BEFORE = 4
AFTER = 3
MIB = 1 << 20


def shifted(block, axis, distance):
    size = lax.axis_size(axis)
    return lax.ppermute(block, axis, [(i, (i + distance) % size) for i in range(size)])


def third_table(length, lanes):
    eye = np.eye(length)
    e, o = eye[:, 0::2], eye[:, 1::2]
    following = lambda t: np.concatenate([t[:, 1:], t[:, -1:]], 1)
    preceding = lambda t: np.concatenate([t[:, :1], t[:, :-1]], 1)
    o = o + predict_one * (e + following(e))
    e = e + update_one * (o + preceding(o))
    o = o + predict_two * (e + following(e))
    e = e + update_two * (o + preceding(o))
    table = np.zeros((lanes, lanes))
    table[:length, : length // 2] = e * scaling
    table[:length, lanes // 2 : lanes // 2 + length // 2] = o / scaling
    return table.astype(np.float32)


def band_scale(by, bx):
    return float(scaling ** ((1 - 2 * by) + (1 - 2 * bx)))


def dot(a, b):
    return jnp.dot(a, b, precision=lax.Precision.HIGHEST, preferred_element_type=jnp.float32)


def ring_lift(e, o):
    n = e.shape[0]
    up = lambda t: pltpu.roll(t, n - 1, 0)
    down = lambda t: pltpu.roll(t, 1, 0)
    o = o + predict_one * (e + up(e))
    e = e + update_one * (o + down(o))
    o = o + predict_two * (e + up(e))
    e = e + update_two * (o + down(o))
    return e, o


def halo_lift(e, o, p, q, r, s, following, preceding, first, last):
    o1 = o + predict_one * (e + following(e, r))
    o1_before = p + predict_one * first(e)
    e1 = e + update_one * (preceding(o1, o1_before) + o1)
    e1_before = q + update_one * o1_before
    e1_after = r + update_one * (last(o1) + s)
    o2 = o1 + predict_two * (e1 + following(e1, e1_after))
    o2_before = o1_before + predict_two * (e1_before + first(e1))
    e2 = e1 + update_two * (preceding(o2, o2_before) + o2)
    return e2, o2


def lead_lift(e, o, p, q, r, s):
    return halo_lift_list(e, o, p, q, r, s)


def halo_lift_list(e, o, p, q, r, s):
    m = len(e)
    e = list(e) + [r]
    o1 = [p + predict_one * e[0]]
    o1 += [o[i] + predict_one * (e[i] + e[i + 1]) for i in range(m)] + [s]
    e1 = [q + update_one * o1[0]]
    e1 += [e[i] + update_one * (o1[i] + o1[i + 1]) for i in range(m + 1)]
    o2 = [o1[i] + predict_two * (e1[i] + e1[i + 1]) for i in range(m + 1)]
    e2 = [e1[i + 1] + update_two * (o2[i] + o2[i + 1]) for i in range(m)]
    return e2, o2[1:]


def sublane_lift(e, o, p, q, r, s):
    n = e.shape[0]
    row = lax.broadcasted_iota(jnp.int32, e.shape, 0)
    following = lambda t, edge: jnp.where(row == n - 1, edge, pltpu.roll(t, n - 1, 0))
    preceding = lambda t, edge: jnp.where(row == 0, edge, pltpu.roll(t, 1, 0))
    return halo_lift(e, o, p, q, r, s, following, preceding, lambda t: t[0:1], lambda t: t[n - 1 : n])


def parts_for_next(c):
    p = c[-1] + predict_one * c[-2]
    q = c[-2] + update_one * (c[-3] + predict_one * (c[-4] + c[-2]))
    return p, q


def parts_for_previous(c):
    return c[0], c[1] + predict_one * (c[0] + c[2])


def row_parts(layer):
    rows = layer.shape[0]
    tail = [layer[rows - 4 + i : rows - 3 + i] for i in range(4)]
    head = [layer[i : i + 1] for i in range(3)]
    return parts_for_next(tail) + parts_for_previous(head)


def local_kernel(v_ref, before_ref, after_ref, table_ref, low_ref, rest_ref, rows_ref, stack_ref):
    ny = v_ref.shape[2]
    half = ny // 2
    lanes = v_ref.shape[3] // 2
    even, odd = [], []
    for c in range(3):
        for h in range(2):
            cut = pl.ds(h * lanes, lanes)
            rows_ref[c, h, 12:16, :] = before_ref[c, 0, :, cut]
            rows_ref[c, h, 16 : 16 + ny, :] = v_ref[c, 0, :, cut]
            rows_ref[c, h, 16 + ny : 16 + ny + AFTER, :] = after_ref[c, 0, :, cut]
    count = half + 16
    for h in range(2):
        even = [rows_ref[c, h, pl.ds(0, count, stride=2), :] for c in range(3)]
        odd = [rows_ref[c, h, pl.ds(1, count, stride=2), :] for c in range(3)]
        for f in range(9):
            if f < 3:
                e, o = even[f], odd[f]
            else:
                i, j = product_pairs[f - 3]
                e, o = even[i] * even[j], odd[i] * odd[j]
            e, o = ring_lift(e, o)
            stack_ref[f * ny : f * ny + half, h * lanes : (h + 1) * lanes] = e[8 : 8 + half]
            stack_ref[f * ny + half : (f + 1) * ny, h * lanes : (h + 1) * lanes] = o[8 : 8 + half]
    out = dot(stack_ref[...], table_ref[...])
    for f in range(9):
        low_ref[f, 0] = out[f * ny : f * ny + half, :lanes]
        rest_ref[0, f, 0] = out[f * ny + half : (f + 1) * ny, :lanes]
        rest_ref[1, f, 0] = out[f * ny : f * ny + half, lanes:]
        rest_ref[2, f, 0] = out[f * ny + half : (f + 1) * ny, lanes:]


def local_pass(velocity, before, after, table):
    _, nx, ny, nz = velocity.shape
    half, lanes = ny // 2, nz // 2
    return pl.pallas_call(
        local_kernel,
        grid=(nx,),
        in_specs=[
            pl.BlockSpec((3, 1, ny, nz), lambda i: (0, i, 0, 0)),
            pl.BlockSpec((3, 1, BEFORE, nz), lambda i: (0, i + BEFORE, 0, 0)),
            pl.BlockSpec((3, 1, AFTER, nz), lambda i: (0, i + BEFORE, 0, 0)),
            pl.BlockSpec((nz, nz), lambda i: (0, 0)),
        ],
        out_specs=[
            pl.BlockSpec((9, 1, half, lanes), lambda i: (0, i, 0, 0)),
            pl.BlockSpec((3, 9, 1, half, lanes), lambda i: (0, 0, i, 0, 0)),
        ],
        out_shape=[
            jax.ShapeDtypeStruct((9, nx, half, lanes), jnp.float32),
            jax.ShapeDtypeStruct((3, 9, nx, half, lanes), jnp.float32),
        ],
        scratch_shapes=[pltpu.VMEM((3, 2, ny + 32, lanes), jnp.float32), pltpu.VMEM((9 * ny, nz), jnp.float32)],
        compiler_params=pltpu.CompilerParams(vmem_limit_bytes=24 * MIB),
        cost_estimate=pl.CostEstimate(flops=9 * nx * ny * nz * 512, bytes_accessed=9 * nx * ny * nz * 6, transcendentals=0),
        name="local_pass",
    )(velocity, before, after, table)


def pair_of(f):
    k = f - 3
    one = jnp.where(k < 3, 0, jnp.where(k < 5, 1, 2))
    two = jnp.where(k < 3, k, jnp.where(k < 5, k - 2, 2))
    return jnp.where(f < 3, f, one), jnp.where(f < 3, 3, two)


def gather_rows(refs, rows_ref, even_ref, odd_ref):
    edge_before, mid_before, edge_after, mid_after, row_before, row_after = refs
    mid = mid_before.shape[2]
    ny = mid + 16
    nx = row_before.shape[1] - BEFORE - AFTER
    lanes = rows_ref.shape[2]
    count = ny // 2 + 16
    even_ref[3] = jnp.ones(even_ref.shape[1:], jnp.float32)
    odd_ref[3] = jnp.ones(odd_ref.shape[1:], jnp.float32)
    for c in range(3):
        for layer in range(BEFORE + AFTER):
            if layer < BEFORE:
                edge, middle, at, line = edge_before, mid_before, layer, layer
            else:
                edge, middle, at, line = edge_after, mid_after, layer - BEFORE, layer + nx
            for h in range(2):
                cut = pl.ds(h * lanes, lanes)
                rows_ref[h, 12:16, :] = row_before[c, line, :, cut]
                rows_ref[h, 16:24, :] = edge[c, at, 0:8, cut]
                rows_ref[h, 24 : 24 + mid, :] = middle[c, at, :, cut]
                rows_ref[h, 24 + mid : 32 + mid, :] = edge[c, at, 8:16, cut]
                rows_ref[h, 16 + ny : 16 + ny + AFTER, :] = row_after[c, line, :, cut]
                even_ref[c, layer, :, cut] = rows_ref[h, pl.ds(0, count, stride=2), :]
                odd_ref[c, layer, :, cut] = rows_ref[h, pl.ds(1, count, stride=2), :]


def halo_parts(ref, i, j):
    g = [ref[i, layer] * ref[j, layer] for layer in range(BEFORE + AFTER)]
    return parts_for_next(g[:BEFORE]) + parts_for_previous(g[BEFORE:])


def lift_first(layers, halo):
    return halo_lift_list(layers[0::2], layers[1::2], *halo)


def send_parts(layers, f, next_ref, prev_ref, next_edge_ref, prev_edge_ref, down_ref, up_ref):
    for part, value in enumerate(parts_for_next(layers)):
        next_ref[f, part] = value
        for at, row in enumerate(row_parts(value)):
            next_edge_ref[f, part, at : at + 1, :] = row
    for part, value in enumerate(parts_for_previous(layers)):
        prev_ref[f, part] = value
        for at, row in enumerate(row_parts(value)):
            prev_edge_ref[f, part, at : at + 1, :] = row
    for at, layer in enumerate(layers):
        p, q, r, s = row_parts(layer)
        down_ref[f, at, 0:1, :] = p
        down_ref[f, at, 1:2, :] = q
        up_ref[f, at, 0:1, :] = r
        up_ref[f, at, 1:2, :] = s


def approx_kernel(*refs):
    low_ref, table_ref = refs[:2]
    halo_refs = refs[2:8]
    approx_ref, high_ref, stress_ref = refs[8:11]
    sends = refs[11:17]
    rows_ref, even_ref, odd_ref, kept_ref, stack_ref = refs[17:]
    f = pl.program_id(0)
    nx, half, lanes = low_ref.shape[1:]

    @pl.when(f == 0)
    def _():
        gather_rows(halo_refs, rows_ref, even_ref, odd_ref)

    i, j = pair_of(f)
    even = halo_parts(even_ref, i, j)
    odd = halo_parts(odd_ref, i, j)
    for k in range(4):
        e, _ = ring_lift(even[k], odd[k])
        stack_ref[k * half : (k + 1) * half, :] = e[8 : 8 + half]
    out = dot(stack_ref[...], table_ref[:, :lanes])
    halo = [out[k * half : (k + 1) * half] for k in range(4)]
    e, o = lift_first([low_ref[0, x] for x in range(nx)], halo)
    e = [t * band_scale(0, 0) for t in e]
    for x in range(nx // 2):
        approx_ref[0, x] = e[x]
        high_ref[0, x] = o[x] * band_scale(0, 1)

    @pl.when(f < 3)
    def _():
        for x in range(nx // 2):
            kept_ref[f, x] = e[x]

    @pl.when(f >= 3)
    def _():
        for x in range(nx // 2):
            stress_ref[0, x] = e[x] - kept_ref[i, x] * kept_ref[j, x]

    send_parts(e, 0, *sends)


def whole(shape):
    return pl.BlockSpec(shape, lambda f: (0,) * len(shape))


def per_field(shape):
    return pl.BlockSpec((1,) + shape, lambda f: (f,) + (0,) * len(shape))


def approx_pass(low, halo, table):
    _, nx, half, lanes = low.shape
    nz, count, mx = 2 * lanes, half + 16, nx // 2
    f32 = lambda *shape: jax.ShapeDtypeStruct(shape, jnp.float32)
    sends = [(2, half, lanes), (2, half, lanes), (2, 4, lanes), (2, 4, lanes), (mx, 2, lanes), (mx, 2, lanes)]
    return pl.pallas_call(
        approx_kernel,
        grid=(9,),
        in_specs=[per_field((nx, half, lanes)), whole((nz, nz))] + [whole(h.shape) for h in halo],
        out_specs=[
            per_field((mx, half, lanes)),
            per_field((mx, half, lanes)),
            pl.BlockSpec((1, mx, half, lanes), lambda f: (jnp.maximum(f - 3, 0), 0, 0, 0)),
        ]
        + [per_field(s) for s in sends],
        out_shape=[f32(9, mx, half, lanes), f32(9, mx, half, lanes), f32(6, mx, half, lanes)] + [f32(9, *s) for s in sends],
        scratch_shapes=[
            pltpu.VMEM((2, 2 * half + 32, lanes), jnp.float32),
            pltpu.VMEM((4, BEFORE + AFTER, count, nz), jnp.float32),
            pltpu.VMEM((4, BEFORE + AFTER, count, nz), jnp.float32),
            pltpu.VMEM((3, mx, half, lanes), jnp.float32),
            pltpu.VMEM((4 * half, nz), jnp.float32),
        ],
        compiler_params=pltpu.CompilerParams(vmem_limit_bytes=24 * MIB),
        name="approx_pass",
    )(low, table, *halo)


def detail_kernel(*refs):
    rest_ref, high_ref, table_ref = refs[:3]
    halo_refs = refs[3:9]
    out_ref, rows_ref, even_ref, odd_ref, stack_ref = refs[9:]
    f = pl.program_id(0)
    nx, half, lanes = rest_ref.shape[2:]

    @pl.when(f == 0)
    def _():
        gather_rows(halo_refs, rows_ref, even_ref, odd_ref)

    i, j = pair_of(f)
    even = halo_parts(even_ref, i, j)
    odd = halo_parts(odd_ref, i, j)
    for k in range(4):
        e, o = ring_lift(even[k], odd[k])
        stack_ref[k * half : (k + 1) * half, :] = e[8 : 8 + half]
        stack_ref[(4 + k) * half : (5 + k) * half, :] = o[8 : 8 + half]
    out = dot(stack_ref[...], table_ref[...])
    for x in range(nx // 2):
        out_ref[0, 0, x] = high_ref[0, x]
    for band, (bz, by) in enumerate(((0, 1), (1, 0), (1, 1))):
        halo = [out[(4 * by + k) * half : (4 * by + k + 1) * half, bz * lanes : (bz + 1) * lanes] for k in range(4)]
        e, o = lift_first([rest_ref[band, 0, x] for x in range(nx)], halo)
        at = 4 * bz + 2 * by - 1
        for x in range(nx // 2):
            out_ref[at, 0, x] = e[x] * band_scale(by, 0)
            out_ref[at + 1, 0, x] = o[x] * band_scale(by, 1)


def detail_pass(rest, high, halo, table):
    _, _, nx, half, lanes = rest.shape
    nz, count, mx = 2 * lanes, half + 16, nx // 2
    return pl.pallas_call(
        detail_kernel,
        grid=(9,),
        in_specs=[
            pl.BlockSpec((3, 1, nx, half, lanes), lambda f: (0, f, 0, 0, 0)),
            per_field((mx, half, lanes)),
            whole((nz, nz)),
        ]
        + [whole(h.shape) for h in halo],
        out_specs=pl.BlockSpec((7, 1, mx, half, lanes), lambda f: (0, f, 0, 0, 0)),
        out_shape=jax.ShapeDtypeStruct((7, 9, mx, half, lanes), jnp.float32),
        scratch_shapes=[
            pltpu.VMEM((2, 2 * half + 32, lanes), jnp.float32),
            pltpu.VMEM((4, BEFORE + AFTER, count, nz), jnp.float32),
            pltpu.VMEM((4, BEFORE + AFTER, count, nz), jnp.float32),
            pltpu.VMEM((8 * half, nz), jnp.float32),
        ],
        compiler_params=pltpu.CompilerParams(vmem_limit_bytes=24 * MIB),
        cost_estimate=pl.CostEstimate(flops=9 * nx * half * nz * 200, bytes_accessed=9 * nx * half * nz * 16, transcendentals=0),
        name="detail_pass",
    )(rest, high, table, *halo)


def level_kernel(last, nz, *refs):
    a_ref, before_ref, after_ref, down_ref, up_ref, table_ref = refs[:6]
    detail_ref, stress_ref, approx_ref = refs[6:9]
    sends = refs[9:15] if not last else ()
    pad_ref, stack_ref, out_ref, kept_ref = refs[-4:]
    nx, ny = a_ref.shape[1:3]
    half, lanes = ny // 2, nz // 2
    wide = table_ref.shape[0]
    if nz < wide:
        pad_ref[...] = jnp.zeros_like(pad_ref)
    for f in range(9):
        for layer in range(nx + 4):
            if layer < nx:
                source = a_ref.at[f, layer]
            elif layer < nx + 2:
                source = before_ref.at[f, layer - nx]
            else:
                source = after_ref.at[f, layer - nx - 2]
            pad_ref[layer, :, :nz] = source[...]
            e = pad_ref[layer, pl.ds(0, half, stride=2), :]
            o = pad_ref[layer, pl.ds(1, half, stride=2), :]
            rows = [down_ref[f, layer, 0:1, :], down_ref[f, layer, 1:2, :], up_ref[f, layer, 0:1, :], up_ref[f, layer, 1:2, :]]
            if nz < wide:
                rows = [jnp.concatenate([row, jnp.zeros((1, wide - nz), jnp.float32)], axis=1) for row in rows]
            e, o = sublane_lift(e, o, *rows)
            stack_ref[layer * ny : layer * ny + half, :] = e
            stack_ref[layer * ny + half : (layer + 1) * ny, :] = o
        out_ref[...] = dot(stack_ref[...], table_ref[...])
        layers = [out_ref[layer * ny : (layer + 1) * ny, :] for layer in range(nx + 4)]
        low, high = lift_first(layers[:nx], layers[nx:])
        approx = []
        for x in range(nx // 2):
            for bx, value in enumerate((low[x], high[x])):
                for by in range(2):
                    t = value[by * half : (by + 1) * half] * band_scale(by, bx)
                    for bz in range(2):
                        band = 4 * bz + 2 * by + bx
                        piece = t[:, bz * (wide // 2) : bz * (wide // 2) + lanes]
                        if band:
                            detail_ref[band - 1, f, x] = piece
                        else:
                            approx.append(piece)
        for x in range(nx // 2):
            if f < 3:
                kept_ref[f, x] = approx[x]
            else:
                i, j = product_pairs[f - 3]
                stress_ref[f - 3, x] = approx[x] - kept_ref[i, x] * kept_ref[j, x]
            if not last or f < 3:
                approx_ref[f, x] = approx[x]
        if not last:
            send_parts(approx, f, *sends)


def level_pass(approx, halo, last):
    _, nx, ny, nz = approx.shape
    mx, half, lanes = nx // 2, ny // 2, nz // 2
    wide = max(nz, 128)
    f32 = lambda *shape: jax.ShapeDtypeStruct(shape, jnp.float32)
    out = [f32(7, 9, mx, half, lanes), f32(6, mx, half, lanes), f32(3 if last else 9, mx, half, lanes)]
    if not last:
        out += [f32(9, *s) for s in ((2, half, lanes), (2, half, lanes), (2, 4, lanes), (2, 4, lanes), (mx, 2, lanes), (mx, 2, lanes))]
    vmem = pl.BlockSpec(memory_space=pltpu.VMEM)
    return pl.pallas_call(
        lambda *refs: level_kernel(last, nz, *refs),
        in_specs=[vmem] * 6,
        out_specs=[vmem] * len(out),
        out_shape=out,
        scratch_shapes=[
            pltpu.VMEM((nx + 4, ny, wide), jnp.float32),
            pltpu.VMEM(((nx + 4) * ny, wide), jnp.float32),
            pltpu.VMEM(((nx + 4) * ny, wide), jnp.float32),
            pltpu.VMEM((3, mx, half, lanes), jnp.float32),
        ],
        compiler_params=pltpu.CompilerParams(vmem_limit_bytes=24 * MIB),
        name="last_level" if last else "second_level",
    )(approx, *halo, jnp.asarray(third_table(nz, wide)))


def exchange(to_next, to_prev, edge_next, edge_prev, down, up):
    from_prev_edge = shifted(edge_next, "gx", 1)
    from_next_edge = shifted(edge_prev, "gx", -1)
    before = shifted(to_next, "gx", 1)
    after = shifted(to_prev, "gx", -1)
    down = jnp.concatenate([down, from_prev_edge[:, :, 0:2], from_next_edge[:, :, 0:2]], axis=1)
    up = jnp.concatenate([up, from_prev_edge[:, :, 2:4], from_next_edge[:, :, 2:4]], axis=1)
    return before, after, shifted(down, "gy", 1), shifted(up, "gy", -1)


def body(velocity):
    _, nx, ny, nz = velocity.shape
    table = jnp.asarray(third_table(nz, nz))
    tail, head = velocity[:, nx - BEFORE :], velocity[:, :AFTER]
    edges = lambda t: jnp.concatenate([t[:, :, :8], t[:, :, ny - 8 :]], axis=2)
    edge_before = shifted(edges(tail), "gx", 1)
    edge_after = shifted(edges(head), "gx", -1)
    mid_before = shifted(tail[:, :, 8 : ny - 8], "gx", 1)
    mid_after = shifted(head[:, :, 8 : ny - 8], "gx", -1)
    down = jnp.concatenate([edge_before[:, :, 12:], velocity[:, :, ny - BEFORE :], edge_after[:, :, 12:]], axis=1)
    up = jnp.concatenate([edge_before[:, :, :AFTER], velocity[:, :, :AFTER], edge_after[:, :, :AFTER]], axis=1)
    row_before = shifted(down, "gy", 1)
    row_after = shifted(up, "gy", -1)
    low, rest = local_pass(velocity, row_before, row_after, table)
    halo = (edge_before, mid_before, edge_after, mid_after, row_before, row_after)
    approx, high, stress_one, *sends = approx_pass(low, halo, table)
    second_halo = exchange(*sends)
    details_one = detail_pass(rest, high, halo, table)
    details_two, stress_two, approx, *sends = level_pass(approx, second_halo, False)
    details_three, stress_three, coarse = level_pass(approx, exchange(*sends), True)
    return details_one, stress_one, details_two, stress_two, details_three, stress_three, coarse


def solution(mesh):
    in_specs = (P(None, "gx", "gy", None),)
    out_specs = (
        P(None, None, "gx", "gy", None),
        P(None, "gx", "gy", None),
        P(None, None, "gx", "gy", None),
        P(None, "gx", "gy", None),
        P(None, None, "gx", "gy", None),
        P(None, "gx", "gy", None),
        P(None, "gx", "gy", None),
    )
    return jax.shard_map(body, mesh=mesh, in_specs=in_specs, out_specs=out_specs, check_vma=False)
```

```python
import jax
import jax.numpy as jnp
import numpy as np
from jax import lax
from jax.experimental import pallas as pl
from jax.experimental.pallas import tpu as pltpu
from jax.sharding import PartitionSpec as P

predict_one = -1.586134342
update_one = -0.05298011854
predict_two = 0.8829110762
update_two = 0.4435068522
scaling = 1.149604398
product_pairs = ((0, 0), (0, 1), (0, 2), (1, 1), (1, 2), (2, 2))
BEFORE = 4
AFTER = 3
MIB = 1 << 20


def shifted(block, axis, distance):
    size = lax.axis_size(axis)
    return lax.ppermute(block, axis, [(i, (i + distance) % size) for i in range(size)])


def third_table(length, lanes):
    eye = np.eye(length)
    e, o = eye[:, 0::2], eye[:, 1::2]
    following = lambda t: np.concatenate([t[:, 1:], t[:, -1:]], 1)
    preceding = lambda t: np.concatenate([t[:, :1], t[:, :-1]], 1)
    o = o + predict_one * (e + following(e))
    e = e + update_one * (o + preceding(o))
    o = o + predict_two * (e + following(e))
    e = e + update_two * (o + preceding(o))
    table = np.zeros((lanes, lanes))
    table[:length, : length // 2] = e * scaling
    table[:length, lanes // 2 : lanes // 2 + length // 2] = o / scaling
    return table.astype(np.float32)


def band_scale(by, bx):
    return float(scaling ** ((1 - 2 * by) + (1 - 2 * bx)))


def dot(a, b):
    return jnp.dot(a, b, precision=lax.Precision.HIGHEST, preferred_element_type=jnp.float32)


def ring_lift(e, o):
    n = e.shape[0]
    up = lambda t: pltpu.roll(t, n - 1, 0)
    down = lambda t: pltpu.roll(t, 1, 0)
    o = o + predict_one * (e + up(e))
    e = e + update_one * (o + down(o))
    o = o + predict_two * (e + up(e))
    e = e + update_two * (o + down(o))
    return e, o


def halo_lift(e, o, p, q, r, s, following, preceding, first, last):
    o1 = o + predict_one * (e + following(e, r))
    o1_before = p + predict_one * first(e)
    e1 = e + update_one * (preceding(o1, o1_before) + o1)
    e1_before = q + update_one * o1_before
    e1_after = r + update_one * (last(o1) + s)
    o2 = o1 + predict_two * (e1 + following(e1, e1_after))
    o2_before = o1_before + predict_two * (e1_before + first(e1))
    e2 = e1 + update_two * (preceding(o2, o2_before) + o2)
    return e2, o2


def lead_lift(e, o, p, q, r, s):
    return halo_lift_list(e, o, p, q, r, s)


def halo_lift_list(e, o, p, q, r, s):
    m = len(e)
    e = list(e) + [r]
    o1 = [p + predict_one * e[0]]
    o1 += [o[i] + predict_one * (e[i] + e[i + 1]) for i in range(m)] + [s]
    e1 = [q + update_one * o1[0]]
    e1 += [e[i] + update_one * (o1[i] + o1[i + 1]) for i in range(m + 1)]
    o2 = [o1[i] + predict_two * (e1[i] + e1[i + 1]) for i in range(m + 1)]
    e2 = [e1[i + 1] + update_two * (o2[i] + o2[i + 1]) for i in range(m)]
    return e2, o2[1:]


def sublane_lift(e, o, p, q, r, s):
    n = e.shape[0]
    row = lax.broadcasted_iota(jnp.int32, e.shape, 0)
    following = lambda t, edge: jnp.where(row == n - 1, edge, pltpu.roll(t, n - 1, 0))
    preceding = lambda t, edge: jnp.where(row == 0, edge, pltpu.roll(t, 1, 0))
    return halo_lift(e, o, p, q, r, s, following, preceding, lambda t: t[0:1], lambda t: t[n - 1 : n])


def parts_for_next(c):
    p = c[-1] + predict_one * c[-2]
    q = c[-2] + update_one * (c[-3] + predict_one * (c[-4] + c[-2]))
    return p, q


def parts_for_previous(c):
    return c[0], c[1] + predict_one * (c[0] + c[2])


def row_parts(layer):
    rows = layer.shape[0]
    tail = [layer[rows - 4 + i : rows - 3 + i] for i in range(4)]
    head = [layer[i : i + 1] for i in range(3)]
    return parts_for_next(tail) + parts_for_previous(head)


def local_kernel(v_ref, before_ref, after_ref, table_ref, low_ref, rest_ref, rows_ref, stack_ref):
    ny = v_ref.shape[2]
    half = ny // 2
    lanes = v_ref.shape[3] // 2
    even, odd = [], []
    for c in range(3):
        for h in range(2):
            cut = pl.ds(h * lanes, lanes)
            rows_ref[c, h, 12:16, :] = before_ref[c, 0, :, cut]
            rows_ref[c, h, 16 : 16 + ny, :] = v_ref[c, 0, :, cut]
            rows_ref[c, h, 16 + ny : 16 + ny + AFTER, :] = after_ref[c, 0, :, cut]
    count = half + 16
    for h in range(2):
        even = [rows_ref[c, h, pl.ds(0, count, stride=2), :] for c in range(3)]
        odd = [rows_ref[c, h, pl.ds(1, count, stride=2), :] for c in range(3)]
        for f in range(9):
            if f < 3:
                e, o = even[f], odd[f]
            else:
                i, j = product_pairs[f - 3]
                e, o = even[i] * even[j], odd[i] * odd[j]
            e, o = ring_lift(e, o)
            stack_ref[f * ny : f * ny + half, h * lanes : (h + 1) * lanes] = e[8 : 8 + half]
            stack_ref[f * ny + half : (f + 1) * ny, h * lanes : (h + 1) * lanes] = o[8 : 8 + half]
    out = dot(stack_ref[...], table_ref[...])
    for f in range(9):
        low_ref[f, 0] = out[f * ny : f * ny + half, :lanes]
        rest_ref[0, f, 0] = out[f * ny + half : (f + 1) * ny, :lanes]
        rest_ref[1, f, 0] = out[f * ny : f * ny + half, lanes:]
        rest_ref[2, f, 0] = out[f * ny + half : (f + 1) * ny, lanes:]


def local_pass(velocity, before, after, table):
    _, nx, ny, nz = velocity.shape
    half, lanes = ny // 2, nz // 2
    return pl.pallas_call(
        local_kernel,
        grid=(nx,),
        in_specs=[
            pl.BlockSpec((3, 1, ny, nz), lambda i: (0, i, 0, 0)),
            pl.BlockSpec((3, 1, BEFORE, nz), lambda i: (0, i, 0, 0)),
            pl.BlockSpec((3, 1, AFTER, nz), lambda i: (0, i, 0, 0)),
            pl.BlockSpec((nz, nz), lambda i: (0, 0)),
        ],
        out_specs=[
            pl.BlockSpec((9, 1, half, lanes), lambda i: (0, i, 0, 0)),
            pl.BlockSpec((3, 9, 1, half, lanes), lambda i: (0, 0, i, 0, 0)),
        ],
        out_shape=[
            jax.ShapeDtypeStruct((9, nx, half, lanes), jnp.float32),
            jax.ShapeDtypeStruct((3, 9, nx, half, lanes), jnp.float32),
        ],
        scratch_shapes=[pltpu.VMEM((3, 2, ny + 32, lanes), jnp.float32), pltpu.VMEM((9 * ny, nz), jnp.float32)],
        compiler_params=pltpu.CompilerParams(vmem_limit_bytes=24 * MIB),
        cost_estimate=pl.CostEstimate(flops=9 * nx * ny * nz * 512, bytes_accessed=9 * nx * ny * nz * 6, transcendentals=0),
        name="local_pass",
    )(velocity, before, after, table)


def pair_of(f):
    k = f - 3
    one = jnp.where(k < 3, 0, jnp.where(k < 5, 1, 2))
    two = jnp.where(k < 3, k, jnp.where(k < 5, k - 2, 2))
    return jnp.where(f < 3, f, one), jnp.where(f < 3, 3, two)


def gather_rows(refs, rows_ref, even_ref, odd_ref):
    edge_before, mid_before, edge_after, mid_after, row_before, row_after = refs
    mid = mid_before.shape[2]
    ny = mid + 16
    lanes = rows_ref.shape[2]
    count = ny // 2 + 16
    even_ref[3] = jnp.ones(even_ref.shape[1:], jnp.float32)
    odd_ref[3] = jnp.ones(odd_ref.shape[1:], jnp.float32)
    for c in range(3):
        for layer in range(BEFORE + AFTER):
            if layer < BEFORE:
                edge, middle, at = edge_before, mid_before, layer
            else:
                edge, middle, at = edge_after, mid_after, layer - BEFORE
            for h in range(2):
                cut = pl.ds(h * lanes, lanes)
                rows_ref[h, 12:16, :] = row_before[c, layer, :, cut]
                rows_ref[h, 16:24, :] = edge[c, at, 0:8, cut]
                rows_ref[h, 24 : 24 + mid, :] = middle[c, at, :, cut]
                rows_ref[h, 24 + mid : 32 + mid, :] = edge[c, at, 8:16, cut]
                rows_ref[h, 16 + ny : 16 + ny + AFTER, :] = row_after[c, layer, :, cut]
                even_ref[c, layer, :, cut] = rows_ref[h, pl.ds(0, count, stride=2), :]
                odd_ref[c, layer, :, cut] = rows_ref[h, pl.ds(1, count, stride=2), :]


def halo_parts(ref, i, j):
    g = [ref[i, layer] * ref[j, layer] for layer in range(BEFORE + AFTER)]
    return parts_for_next(g[:BEFORE]) + parts_for_previous(g[BEFORE:])


def lift_first(layers, halo):
    return halo_lift_list(layers[0::2], layers[1::2], *halo)


def send_parts(layers, f, next_ref, prev_ref, next_edge_ref, prev_edge_ref, down_ref, up_ref):
    for part, value in enumerate(parts_for_next(layers)):
        next_ref[f, part] = value
        for at, row in enumerate(row_parts(value)):
            next_edge_ref[f, part, at : at + 1, :] = row
    for part, value in enumerate(parts_for_previous(layers)):
        prev_ref[f, part] = value
        for at, row in enumerate(row_parts(value)):
            prev_edge_ref[f, part, at : at + 1, :] = row
    for at, layer in enumerate(layers):
        p, q, r, s = row_parts(layer)
        down_ref[f, at, 0:1, :] = p
        down_ref[f, at, 1:2, :] = q
        up_ref[f, at, 0:1, :] = r
        up_ref[f, at, 1:2, :] = s


def approx_kernel(*refs):
    low_ref, table_ref = refs[:2]
    halo_refs = refs[2:8]
    approx_ref, high_ref, stress_ref = refs[8:11]
    sends = refs[11:17]
    rows_ref, even_ref, odd_ref, kept_ref, stack_ref = refs[17:]
    f = pl.program_id(0)
    nx, half, lanes = low_ref.shape[1:]

    @pl.when(f == 0)
    def _():
        gather_rows(halo_refs, rows_ref, even_ref, odd_ref)

    i, j = pair_of(f)
    even = halo_parts(even_ref, i, j)
    odd = halo_parts(odd_ref, i, j)
    for k in range(4):
        e, _ = ring_lift(even[k], odd[k])
        stack_ref[k * half : (k + 1) * half, :] = e[8 : 8 + half]
    out = dot(stack_ref[...], table_ref[:, :lanes])
    halo = [out[k * half : (k + 1) * half] for k in range(4)]
    e, o = lift_first([low_ref[0, x] for x in range(nx)], halo)
    e = [t * band_scale(0, 0) for t in e]
    for x in range(nx // 2):
        approx_ref[0, x] = e[x]
        high_ref[0, x] = o[x] * band_scale(0, 1)

    @pl.when(f < 3)
    def _():
        for x in range(nx // 2):
            kept_ref[f, x] = e[x]

    @pl.when(f >= 3)
    def _():
        for x in range(nx // 2):
            stress_ref[0, x] = e[x] - kept_ref[i, x] * kept_ref[j, x]

    send_parts(e, 0, *sends)


def whole(shape):
    return pl.BlockSpec(shape, lambda f: (0,) * len(shape))


def per_field(shape):
    return pl.BlockSpec((1,) + shape, lambda f: (f,) + (0,) * len(shape))


def approx_pass(low, halo, table):
    _, nx, half, lanes = low.shape
    nz, count, mx = 2 * lanes, half + 16, nx // 2
    f32 = lambda *shape: jax.ShapeDtypeStruct(shape, jnp.float32)
    sends = [(2, half, lanes), (2, half, lanes), (2, 4, lanes), (2, 4, lanes), (mx, 2, lanes), (mx, 2, lanes)]
    return pl.pallas_call(
        approx_kernel,
        grid=(9,),
        in_specs=[per_field((nx, half, lanes)), whole((nz, nz))] + [whole(h.shape) for h in halo],
        out_specs=[
            per_field((mx, half, lanes)),
            per_field((mx, half, lanes)),
            pl.BlockSpec((1, mx, half, lanes), lambda f: (jnp.maximum(f - 3, 0), 0, 0, 0)),
        ]
        + [per_field(s) for s in sends],
        out_shape=[f32(9, mx, half, lanes), f32(9, mx, half, lanes), f32(6, mx, half, lanes)] + [f32(9, *s) for s in sends],
        scratch_shapes=[
            pltpu.VMEM((2, 2 * half + 32, lanes), jnp.float32),
            pltpu.VMEM((4, BEFORE + AFTER, count, nz), jnp.float32),
            pltpu.VMEM((4, BEFORE + AFTER, count, nz), jnp.float32),
            pltpu.VMEM((3, mx, half, lanes), jnp.float32),
            pltpu.VMEM((4 * half, nz), jnp.float32),
        ],
        compiler_params=pltpu.CompilerParams(vmem_limit_bytes=24 * MIB),
        name="approx_pass",
    )(low, table, *halo)


def detail_kernel(*refs):
    rest_ref, high_ref, table_ref = refs[:3]
    halo_refs = refs[3:9]
    out_ref, rows_ref, even_ref, odd_ref, stack_ref = refs[9:]
    f = pl.program_id(0)
    nx, half, lanes = rest_ref.shape[2:]

    @pl.when(f == 0)
    def _():
        gather_rows(halo_refs, rows_ref, even_ref, odd_ref)

    i, j = pair_of(f)
    even = halo_parts(even_ref, i, j)
    odd = halo_parts(odd_ref, i, j)
    for k in range(4):
        e, o = ring_lift(even[k], odd[k])
        stack_ref[k * half : (k + 1) * half, :] = e[8 : 8 + half]
        stack_ref[(4 + k) * half : (5 + k) * half, :] = o[8 : 8 + half]
    out = dot(stack_ref[...], table_ref[...])
    for x in range(nx // 2):
        out_ref[0, 0, x] = high_ref[0, x]
    for band, (bz, by) in enumerate(((0, 1), (1, 0), (1, 1))):
        halo = [out[(4 * by + k) * half : (4 * by + k + 1) * half, bz * lanes : (bz + 1) * lanes] for k in range(4)]
        e, o = lift_first([rest_ref[band, 0, x] for x in range(nx)], halo)
        at = 4 * bz + 2 * by - 1
        for x in range(nx // 2):
            out_ref[at, 0, x] = e[x] * band_scale(by, 0)
            out_ref[at + 1, 0, x] = o[x] * band_scale(by, 1)


def detail_pass(rest, high, halo, table):
    _, _, nx, half, lanes = rest.shape
    nz, count, mx = 2 * lanes, half + 16, nx // 2
    return pl.pallas_call(
        detail_kernel,
        grid=(9,),
        in_specs=[
            pl.BlockSpec((3, 1, nx, half, lanes), lambda f: (0, f, 0, 0, 0)),
            per_field((mx, half, lanes)),
            whole((nz, nz)),
        ]
        + [whole(h.shape) for h in halo],
        out_specs=pl.BlockSpec((7, 1, mx, half, lanes), lambda f: (0, f, 0, 0, 0)),
        out_shape=jax.ShapeDtypeStruct((7, 9, mx, half, lanes), jnp.float32),
        scratch_shapes=[
            pltpu.VMEM((2, 2 * half + 32, lanes), jnp.float32),
            pltpu.VMEM((4, BEFORE + AFTER, count, nz), jnp.float32),
            pltpu.VMEM((4, BEFORE + AFTER, count, nz), jnp.float32),
            pltpu.VMEM((8 * half, nz), jnp.float32),
        ],
        compiler_params=pltpu.CompilerParams(vmem_limit_bytes=24 * MIB),
        cost_estimate=pl.CostEstimate(flops=9 * nx * half * nz * 200, bytes_accessed=9 * nx * half * nz * 16, transcendentals=0),
        name="detail_pass",
    )(rest, high, table, *halo)


def level_kernel(last, nz, *refs):
    a_ref, before_ref, after_ref, down_ref, up_ref, table_ref = refs[:6]
    detail_ref, stress_ref, approx_ref = refs[6:9]
    sends = refs[9:15] if not last else ()
    pad_ref, stack_ref, out_ref, kept_ref = refs[-4:]
    nx, ny = a_ref.shape[1:3]
    half, lanes = ny // 2, nz // 2
    wide = table_ref.shape[0]
    if nz < wide:
        pad_ref[...] = jnp.zeros_like(pad_ref)
    for f in range(9):
        for layer in range(nx + 4):
            if layer < nx:
                source = a_ref.at[f, layer]
            elif layer < nx + 2:
                source = before_ref.at[f, layer - nx]
            else:
                source = after_ref.at[f, layer - nx - 2]
            pad_ref[layer, :, :nz] = source[...]
            e = pad_ref[layer, pl.ds(0, half, stride=2), :]
            o = pad_ref[layer, pl.ds(1, half, stride=2), :]
            rows = [down_ref[f, layer, 0:1, :], down_ref[f, layer, 1:2, :], up_ref[f, layer, 0:1, :], up_ref[f, layer, 1:2, :]]
            if nz < wide:
                rows = [jnp.concatenate([row, jnp.zeros((1, wide - nz), jnp.float32)], axis=1) for row in rows]
            e, o = sublane_lift(e, o, *rows)
            stack_ref[layer * ny : layer * ny + half, :] = e
            stack_ref[layer * ny + half : (layer + 1) * ny, :] = o
        out_ref[...] = dot(stack_ref[...], table_ref[...])
        layers = [out_ref[layer * ny : (layer + 1) * ny, :] for layer in range(nx + 4)]
        low, high = lift_first(layers[:nx], layers[nx:])
        approx = []
        for x in range(nx // 2):
            for bx, value in enumerate((low[x], high[x])):
                for by in range(2):
                    t = value[by * half : (by + 1) * half] * band_scale(by, bx)
                    for bz in range(2):
                        band = 4 * bz + 2 * by + bx
                        piece = t[:, bz * (wide // 2) : bz * (wide // 2) + lanes]
                        if band:
                            detail_ref[band - 1, f, x] = piece
                        else:
                            approx.append(piece)
        for x in range(nx // 2):
            if f < 3:
                kept_ref[f, x] = approx[x]
            else:
                i, j = product_pairs[f - 3]
                stress_ref[f - 3, x] = approx[x] - kept_ref[i, x] * kept_ref[j, x]
            if not last or f < 3:
                approx_ref[f, x] = approx[x]
        if not last:
            send_parts(approx, f, *sends)


def level_pass(approx, halo, last):
    _, nx, ny, nz = approx.shape
    mx, half, lanes = nx // 2, ny // 2, nz // 2
    wide = max(nz, 128)
    f32 = lambda *shape: jax.ShapeDtypeStruct(shape, jnp.float32)
    out = [f32(7, 9, mx, half, lanes), f32(6, mx, half, lanes), f32(3 if last else 9, mx, half, lanes)]
    if not last:
        out += [f32(9, *s) for s in ((2, half, lanes), (2, half, lanes), (2, 4, lanes), (2, 4, lanes), (mx, 2, lanes), (mx, 2, lanes))]
    vmem = pl.BlockSpec(memory_space=pltpu.VMEM)
    return pl.pallas_call(
        lambda *refs: level_kernel(last, nz, *refs),
        in_specs=[vmem] * 6,
        out_specs=[vmem] * len(out),
        out_shape=out,
        scratch_shapes=[
            pltpu.VMEM((nx + 4, ny, wide), jnp.float32),
            pltpu.VMEM(((nx + 4) * ny, wide), jnp.float32),
            pltpu.VMEM(((nx + 4) * ny, wide), jnp.float32),
            pltpu.VMEM((3, mx, half, lanes), jnp.float32),
        ],
        compiler_params=pltpu.CompilerParams(vmem_limit_bytes=24 * MIB),
        name="last_level" if last else "second_level",
    )(approx, *halo, jnp.asarray(third_table(nz, wide)))


def exchange(to_next, to_prev, edge_next, edge_prev, down, up):
    from_prev_edge = shifted(edge_next, "gx", 1)
    from_next_edge = shifted(edge_prev, "gx", -1)
    before = shifted(to_next, "gx", 1)
    after = shifted(to_prev, "gx", -1)
    down = jnp.concatenate([down, from_prev_edge[:, :, 0:2], from_next_edge[:, :, 0:2]], axis=1)
    up = jnp.concatenate([up, from_prev_edge[:, :, 2:4], from_next_edge[:, :, 2:4]], axis=1)
    return before, after, shifted(down, "gy", 1), shifted(up, "gy", -1)


def body(velocity):
    _, nx, ny, nz = velocity.shape
    table = jnp.asarray(third_table(nz, nz))
    tail, head = velocity[:, nx - BEFORE :], velocity[:, :AFTER]
    edges = lambda t: jnp.concatenate([t[:, :, :8], t[:, :, ny - 8 :]], axis=2)
    edge_before = shifted(edges(tail), "gx", 1)
    edge_after = shifted(edges(head), "gx", -1)
    mid_before = shifted(tail[:, :, 8 : ny - 8], "gx", 1)
    mid_after = shifted(head[:, :, 8 : ny - 8], "gx", -1)
    own_before = shifted(velocity[:, :, ny - BEFORE :], "gy", 1)
    own_after = shifted(velocity[:, :, :AFTER], "gy", -1)
    low, rest = local_pass(velocity, own_before, own_after, table)
    edge_before, edge_after, low = lax.optimization_barrier((edge_before, edge_after, low))
    down = jnp.concatenate([edge_before[:, :, 12:], edge_after[:, :, 12:]], axis=1)
    up = jnp.concatenate([edge_before[:, :, :AFTER], edge_after[:, :, :AFTER]], axis=1)
    row_before = shifted(down, "gy", 1)
    row_after = shifted(up, "gy", -1)
    halo = (edge_before, mid_before, edge_after, mid_after, row_before, row_after)
    approx, high, stress_one, *sends = approx_pass(low, halo, table)
    second_halo = exchange(*sends)
    details_one = detail_pass(rest, high, halo, table)
    approx, details_one = lax.optimization_barrier((approx, details_one))
    details_two, stress_two, approx, *sends = level_pass(approx, second_halo, False)
    details_three, stress_three, coarse = level_pass(approx, exchange(*sends), True)
    return details_one, stress_one, details_two, stress_two, details_three, stress_three, coarse


def solution(mesh):
    in_specs = (P(None, "gx", "gy", None),)
    out_specs = (
        P(None, None, "gx", "gy", None),
        P(None, "gx", "gy", None),
        P(None, None, "gx", "gy", None),
        P(None, "gx", "gy", None),
        P(None, None, "gx", "gy", None),
        P(None, "gx", "gy", None),
        P(None, "gx", "gy", None),
    )
    return jax.shard_map(body, mesh=mesh, in_specs=in_specs, out_specs=out_specs, check_vma=False)
```

```python
import jax
import jax.numpy as jnp
import numpy as np
from jax import lax
from jax.experimental import pallas as pl
from jax.experimental.pallas import tpu as pltpu
from jax.sharding import PartitionSpec as P

predict_one = -1.586134342
update_one = -0.05298011854
predict_two = 0.8829110762
update_two = 0.4435068522
scaling = 1.149604398
product_pairs = ((0, 0), (0, 1), (0, 2), (1, 1), (1, 2), (2, 2))
BEFORE = 4
AFTER = 3
GROUP = 3
MIB = 1 << 20


def shifted(block, axis, distance):
    size = lax.axis_size(axis)
    return lax.ppermute(block, axis, [(i, (i + distance) % size) for i in range(size)])


def third_table(length, lanes):
    eye = np.eye(length)
    e, o = eye[:, 0::2], eye[:, 1::2]
    following = lambda t: np.concatenate([t[:, 1:], t[:, -1:]], 1)
    preceding = lambda t: np.concatenate([t[:, :1], t[:, :-1]], 1)
    o = o + predict_one * (e + following(e))
    e = e + update_one * (o + preceding(o))
    o = o + predict_two * (e + following(e))
    e = e + update_two * (o + preceding(o))
    table = np.zeros((lanes, lanes))
    table[:length, : length // 2] = e * scaling
    table[:length, lanes // 2 : lanes // 2 + length // 2] = o / scaling
    return table.astype(np.float32)


def band_scale(by, bx):
    return float(scaling ** ((1 - 2 * by) + (1 - 2 * bx)))


def dot(a, b):
    return jnp.dot(a, b, precision=lax.Precision.HIGHEST, preferred_element_type=jnp.float32)


def ring_lift(e, o):
    n = e.shape[0]
    up = lambda t: pltpu.roll(t, n - 1, 0)
    down = lambda t: pltpu.roll(t, 1, 0)
    o = o + predict_one * (e + up(e))
    e = e + update_one * (o + down(o))
    o = o + predict_two * (e + up(e))
    e = e + update_two * (o + down(o))
    return e, o


def halo_lift(e, o, p, q, r, s, following, preceding, first, last):
    o1 = o + predict_one * (e + following(e, r))
    o1_before = p + predict_one * first(e)
    e1 = e + update_one * (preceding(o1, o1_before) + o1)
    e1_before = q + update_one * o1_before
    e1_after = r + update_one * (last(o1) + s)
    o2 = o1 + predict_two * (e1 + following(e1, e1_after))
    o2_before = o1_before + predict_two * (e1_before + first(e1))
    e2 = e1 + update_two * (preceding(o2, o2_before) + o2)
    return e2, o2


def halo_lift_list(e, o, p, q, r, s):
    m = len(e)
    e = list(e) + [r]
    o1 = [p + predict_one * e[0]]
    o1 += [o[i] + predict_one * (e[i] + e[i + 1]) for i in range(m)] + [s]
    e1 = [q + update_one * o1[0]]
    e1 += [e[i] + update_one * (o1[i] + o1[i + 1]) for i in range(m + 1)]
    o2 = [o1[i] + predict_two * (e1[i] + e1[i + 1]) for i in range(m + 1)]
    e2 = [e1[i + 1] + update_two * (o2[i] + o2[i + 1]) for i in range(m)]
    return e2, o2[1:]


def sublane_lift(e, o, p, q, r, s):
    n = e.shape[0]
    row = lax.broadcasted_iota(jnp.int32, e.shape, 0)
    following = lambda t, edge: jnp.where(row == n - 1, edge, pltpu.roll(t, n - 1, 0))
    preceding = lambda t, edge: jnp.where(row == 0, edge, pltpu.roll(t, 1, 0))
    return halo_lift(e, o, p, q, r, s, following, preceding, lambda t: t[0:1], lambda t: t[n - 1 : n])


def parts_for_next(c):
    p = c[-1] + predict_one * c[-2]
    q = c[-2] + update_one * (c[-3] + predict_one * (c[-4] + c[-2]))
    return p, q


def parts_for_previous(c):
    return c[0], c[1] + predict_one * (c[0] + c[2])


def row_parts(layer):
    rows = layer.shape[0]
    tail = [layer[rows - 4 + i : rows - 3 + i] for i in range(4)]
    head = [layer[i : i + 1] for i in range(3)]
    return parts_for_next(tail) + parts_for_previous(head)


def local_kernel(v_ref, before_ref, after_ref, table_ref, low_ref, rest_ref, rows_ref, stack_ref):
    ny = v_ref.shape[2]
    half = ny // 2
    lanes = v_ref.shape[3] // 2
    even, odd = [], []
    for c in range(3):
        for h in range(2):
            cut = pl.ds(h * lanes, lanes)
            rows_ref[c, h, 12:16, :] = before_ref[c, 0, :, cut]
            rows_ref[c, h, 16 : 16 + ny, :] = v_ref[c, 0, :, cut]
            rows_ref[c, h, 16 + ny : 16 + ny + AFTER, :] = after_ref[c, 0, :, cut]
    count = half + 16
    for h in range(2):
        even = [rows_ref[c, h, pl.ds(0, count, stride=2), :] for c in range(3)]
        odd = [rows_ref[c, h, pl.ds(1, count, stride=2), :] for c in range(3)]
        for f in range(9):
            if f < 3:
                e, o = even[f], odd[f]
            else:
                i, j = product_pairs[f - 3]
                e, o = even[i] * even[j], odd[i] * odd[j]
            e, o = ring_lift(e, o)
            stack_ref[f * ny : f * ny + half, h * lanes : (h + 1) * lanes] = e[8 : 8 + half]
            stack_ref[f * ny + half : (f + 1) * ny, h * lanes : (h + 1) * lanes] = o[8 : 8 + half]
    out = dot(stack_ref[...], table_ref[...])
    for f in range(9):
        low_ref[f, 0] = out[f * ny : f * ny + half, :lanes]
        rest_ref[0, f, 0] = out[f * ny + half : (f + 1) * ny, :lanes]
        rest_ref[1, f, 0] = out[f * ny : f * ny + half, lanes:]
        rest_ref[2, f, 0] = out[f * ny + half : (f + 1) * ny, lanes:]


def local_pass(velocity, before, after, table):
    _, nx, ny, nz = velocity.shape
    half, lanes = ny // 2, nz // 2
    return pl.pallas_call(
        local_kernel,
        grid=(nx,),
        in_specs=[
            pl.BlockSpec((3, 1, ny, nz), lambda i: (0, i, 0, 0)),
            pl.BlockSpec((3, 1, BEFORE, nz), lambda i: (0, i, 0, 0)),
            pl.BlockSpec((3, 1, AFTER, nz), lambda i: (0, i, 0, 0)),
            pl.BlockSpec((nz, nz), lambda i: (0, 0)),
        ],
        out_specs=[
            pl.BlockSpec((9, 1, half, lanes), lambda i: (0, i, 0, 0)),
            pl.BlockSpec((3, 9, 1, half, lanes), lambda i: (0, 0, i, 0, 0)),
        ],
        out_shape=[
            jax.ShapeDtypeStruct((9, nx, half, lanes), jnp.float32),
            jax.ShapeDtypeStruct((3, 9, nx, half, lanes), jnp.float32),
        ],
        scratch_shapes=[pltpu.VMEM((3, 2, ny + 32, lanes), jnp.float32), pltpu.VMEM((9 * ny, nz), jnp.float32)],
        compiler_params=pltpu.CompilerParams(vmem_limit_bytes=24 * MIB),
        cost_estimate=pl.CostEstimate(flops=9 * nx * ny * nz * 512, bytes_accessed=9 * nx * ny * nz * 6, transcendentals=0),
        name="local_pass",
    )(velocity, before, after, table)


def pair_of(f):
    k = f - 3
    one = jnp.where(k < 3, 0, jnp.where(k < 5, 1, 2))
    two = jnp.where(k < 3, k, jnp.where(k < 5, k - 2, 2))
    return jnp.where(f < 3, f, one), jnp.where(f < 3, 3, two)


def gather_rows(refs, rows_ref, even_ref, odd_ref):
    edge_before, mid_before, edge_after, mid_after, row_before, row_after = refs
    mid = mid_before.shape[2]
    ny = mid + 16
    lanes = rows_ref.shape[2]
    count = ny // 2 + 16
    even_ref[3] = jnp.ones(even_ref.shape[1:], jnp.float32)
    odd_ref[3] = jnp.ones(odd_ref.shape[1:], jnp.float32)
    for c in range(3):
        for layer in range(BEFORE + AFTER):
            if layer < BEFORE:
                edge, middle, at = edge_before, mid_before, layer
            else:
                edge, middle, at = edge_after, mid_after, layer - BEFORE
            for h in range(2):
                cut = pl.ds(h * lanes, lanes)
                rows_ref[h, 12:16, :] = row_before[c, layer, :, cut]
                rows_ref[h, 16:24, :] = edge[c, at, 0:8, cut]
                rows_ref[h, 24 : 24 + mid, :] = middle[c, at, :, cut]
                rows_ref[h, 24 + mid : 32 + mid, :] = edge[c, at, 8:16, cut]
                rows_ref[h, 16 + ny : 16 + ny + AFTER, :] = row_after[c, layer, :, cut]
                even_ref[c, layer, :, cut] = rows_ref[h, pl.ds(0, count, stride=2), :]
                odd_ref[c, layer, :, cut] = rows_ref[h, pl.ds(1, count, stride=2), :]


def halo_parts(ref, i, j):
    g = [ref[i, layer] * ref[j, layer] for layer in range(BEFORE + AFTER)]
    return parts_for_next(g[:BEFORE]) + parts_for_previous(g[BEFORE:])


def lift_first(layers, halo):
    return halo_lift_list(layers[0::2], layers[1::2], *halo)


def send_parts(layers, f, next_ref, prev_ref, next_edge_ref, prev_edge_ref, down_ref, up_ref):
    for part, value in enumerate(parts_for_next(layers)):
        next_ref[f, part] = value
        for at, row in enumerate(row_parts(value)):
            next_edge_ref[f, part, at : at + 1, :] = row
    for part, value in enumerate(parts_for_previous(layers)):
        prev_ref[f, part] = value
        for at, row in enumerate(row_parts(value)):
            prev_edge_ref[f, part, at : at + 1, :] = row
    for at, layer in enumerate(layers):
        p, q, r, s = row_parts(layer)
        down_ref[f, at, 0:1, :] = p
        down_ref[f, at, 1:2, :] = q
        up_ref[f, at, 0:1, :] = r
        up_ref[f, at, 1:2, :] = s


def approx_kernel(*refs):
    low_ref, table_ref = refs[:2]
    halo_refs = refs[2:8]
    approx_ref, high_ref, stress_ref = refs[8:11]
    sends = refs[11:17]
    rows_ref, even_ref, odd_ref, kept_ref, stack_ref = refs[17:]
    f = pl.program_id(0)
    nx, half, lanes = low_ref.shape[1:]

    @pl.when(f == 0)
    def _():
        gather_rows(halo_refs, rows_ref, even_ref, odd_ref)

    pairs = [pair_of(f * GROUP + k) for k in range(GROUP)]
    for n, (i, j) in enumerate(pairs):
        even = halo_parts(even_ref, i, j)
        odd = halo_parts(odd_ref, i, j)
        for k in range(4):
            e, _ = ring_lift(even[k], odd[k])
            at = (4 * n + k) * half
            stack_ref[at : at + half, :] = e[8 : 8 + half]
    out = dot(stack_ref[...], table_ref[:, :lanes])
    fields = []
    for n in range(GROUP):
        halo = [out[(4 * n + k) * half : (4 * n + k + 1) * half] for k in range(4)]
        e, o = lift_first([low_ref[n, x] for x in range(nx)], halo)
        e = [t * band_scale(0, 0) for t in e]
        for x in range(nx // 2):
            approx_ref[n, x] = e[x]
            high_ref[n, x] = o[x] * band_scale(0, 1)
        send_parts(e, n, *sends)
        fields.append(e)

    @pl.when(f == 0)
    def _():
        for n in range(GROUP):
            for x in range(nx // 2):
                kept_ref[n, x] = fields[n][x]

    @pl.when(f > 0)
    def _():
        for n, (i, j) in enumerate(pairs):
            for x in range(nx // 2):
                stress_ref[n, x] = approx_ref[n, x] - kept_ref[i, x] * kept_ref[j, x]


def whole(shape):
    return pl.BlockSpec(shape, lambda f: (0,) * len(shape))


def per_field(shape):
    return pl.BlockSpec((GROUP,) + shape, lambda f: (f,) + (0,) * len(shape))


def approx_pass(low, halo, table):
    _, nx, half, lanes = low.shape
    nz, count, mx = 2 * lanes, half + 16, nx // 2
    f32 = lambda *shape: jax.ShapeDtypeStruct(shape, jnp.float32)
    sends = [(2, half, lanes), (2, half, lanes), (2, 4, lanes), (2, 4, lanes), (mx, 2, lanes), (mx, 2, lanes)]
    return pl.pallas_call(
        approx_kernel,
        grid=(9 // GROUP,),
        in_specs=[per_field((nx, half, lanes)), whole((nz, nz))] + [whole(h.shape) for h in halo],
        out_specs=[
            per_field((mx, half, lanes)),
            per_field((mx, half, lanes)),
            pl.BlockSpec((GROUP, mx, half, lanes), lambda f: (jnp.maximum(f - 1, 0), 0, 0, 0)),
        ]
        + [per_field(s) for s in sends],
        out_shape=[f32(9, mx, half, lanes), f32(9, mx, half, lanes), f32(6, mx, half, lanes)] + [f32(9, *s) for s in sends],
        scratch_shapes=[
            pltpu.VMEM((2, 2 * half + 32, lanes), jnp.float32),
            pltpu.VMEM((4, BEFORE + AFTER, count, nz), jnp.float32),
            pltpu.VMEM((4, BEFORE + AFTER, count, nz), jnp.float32),
            pltpu.VMEM((3, mx, half, lanes), jnp.float32),
            pltpu.VMEM((GROUP * 4 * half, nz), jnp.float32),
        ],
        compiler_params=pltpu.CompilerParams(vmem_limit_bytes=24 * MIB),
        name="approx_pass",
    )(low, table, *halo)


def detail_kernel(*refs):
    rest_ref, high_ref, table_ref = refs[:3]
    halo_refs = refs[3:9]
    out_ref, rows_ref, even_ref, odd_ref, stack_ref = refs[9:]
    f = pl.program_id(0)
    nx, half, lanes = rest_ref.shape[2:]

    @pl.when(f == 0)
    def _():
        gather_rows(halo_refs, rows_ref, even_ref, odd_ref)

    for n in range(GROUP):
        i, j = pair_of(f * GROUP + n)
        even = halo_parts(even_ref, i, j)
        odd = halo_parts(odd_ref, i, j)
        for k in range(4):
            e, o = ring_lift(even[k], odd[k])
            at = (8 * n + k) * half
            stack_ref[at : at + half, :] = e[8 : 8 + half]
            at += 4 * half
            stack_ref[at : at + half, :] = o[8 : 8 + half]
    stack_ref[...] = dot(stack_ref[...], table_ref[...])
    for n in range(GROUP):
        for x in range(nx // 2):
            out_ref[0, n, x] = high_ref[n, x]
        for band, (bz, by) in enumerate(((0, 1), (1, 0), (1, 1))):
            halo = []
            for k in range(4):
                at = (8 * n + 4 * by + k) * half
                halo.append(stack_ref[at : at + half, bz * lanes : (bz + 1) * lanes])
            e, o = lift_first([rest_ref[band, n, x] for x in range(nx)], halo)
            at = 4 * bz + 2 * by - 1
            for x in range(nx // 2):
                out_ref[at, n, x] = e[x] * band_scale(by, 0)
                out_ref[at + 1, n, x] = o[x] * band_scale(by, 1)


def detail_pass(rest, high, halo, table):
    _, _, nx, half, lanes = rest.shape
    nz, count, mx = 2 * lanes, half + 16, nx // 2
    return pl.pallas_call(
        detail_kernel,
        grid=(9 // GROUP,),
        in_specs=[
            pl.BlockSpec((3, GROUP, nx, half, lanes), lambda f: (0, f, 0, 0, 0)),
            per_field((mx, half, lanes)),
            whole((nz, nz)),
        ]
        + [whole(h.shape) for h in halo],
        out_specs=pl.BlockSpec((7, GROUP, mx, half, lanes), lambda f: (0, f, 0, 0, 0)),
        out_shape=jax.ShapeDtypeStruct((7, 9, mx, half, lanes), jnp.float32),
        scratch_shapes=[
            pltpu.VMEM((2, 2 * half + 32, lanes), jnp.float32),
            pltpu.VMEM((4, BEFORE + AFTER, count, nz), jnp.float32),
            pltpu.VMEM((4, BEFORE + AFTER, count, nz), jnp.float32),
            pltpu.VMEM((GROUP * 8 * half, nz), jnp.float32),
        ],
        compiler_params=pltpu.CompilerParams(vmem_limit_bytes=24 * MIB),
        cost_estimate=pl.CostEstimate(flops=9 * nx * half * nz * 200, bytes_accessed=9 * nx * half * nz * 16, transcendentals=0),
        name="detail_pass",
    )(rest, high, table, *halo)


def level_kernel(last, nz, *refs):
    a_ref, before_ref, after_ref, down_ref, up_ref, table_ref = refs[:6]
    detail_ref, stress_ref, approx_ref = refs[6:9]
    sends = refs[9:15] if not last else ()
    pad_ref, stack_ref, out_ref, kept_ref = refs[-4:]
    nx, ny = a_ref.shape[1:3]
    half, lanes = ny // 2, nz // 2
    wide = table_ref.shape[0]
    if nz < wide:
        pad_ref[...] = jnp.zeros_like(pad_ref)
    lines = (nx + 4) * ny
    for f in range(9):
        for layer in range(nx + 4):
            if layer < nx:
                source = a_ref.at[f, layer]
            elif layer < nx + 2:
                source = before_ref.at[f, layer - nx]
            else:
                source = after_ref.at[f, layer - nx - 2]
            pad_ref[f, layer, :, :nz] = source[...]
    for f in range(9):
        for layer in range(nx + 4):
            e = pad_ref[f, layer, pl.ds(0, half, stride=2), :]
            o = pad_ref[f, layer, pl.ds(1, half, stride=2), :]
            rows = [down_ref[f, layer, 0:1, :], down_ref[f, layer, 1:2, :], up_ref[f, layer, 0:1, :], up_ref[f, layer, 1:2, :]]
            if nz < wide:
                rows = [jnp.concatenate([row, jnp.zeros((1, wide - nz), jnp.float32)], axis=1) for row in rows]
            e, o = sublane_lift(e, o, *rows)
            at = f * lines + layer * ny
            stack_ref[at : at + half, :] = e
            stack_ref[at + half : at + ny, :] = o
    out_ref[...] = dot(stack_ref[...], table_ref[...])
    for f in range(9):
        layers = [out_ref[f * lines + layer * ny : f * lines + (layer + 1) * ny, :] for layer in range(nx + 4)]
        low, high = lift_first(layers[:nx], layers[nx:])
        approx = []
        for x in range(nx // 2):
            for bx, value in enumerate((low[x], high[x])):
                for by in range(2):
                    t = value[by * half : (by + 1) * half] * band_scale(by, bx)
                    for bz in range(2):
                        band = 4 * bz + 2 * by + bx
                        piece = t[:, bz * (wide // 2) : bz * (wide // 2) + lanes]
                        if band:
                            detail_ref[band - 1, f, x] = piece
                        else:
                            approx.append(piece)
        for x in range(nx // 2):
            if f < 3:
                kept_ref[f, x] = approx[x]
            else:
                i, j = product_pairs[f - 3]
                stress_ref[f - 3, x] = approx[x] - kept_ref[i, x] * kept_ref[j, x]
            if not last or f < 3:
                approx_ref[f, x] = approx[x]
        if not last:
            send_parts(approx, f, *sends)


def level_pass(approx, halo, last):
    _, nx, ny, nz = approx.shape
    mx, half, lanes = nx // 2, ny // 2, nz // 2
    wide = max(nz, 128)
    f32 = lambda *shape: jax.ShapeDtypeStruct(shape, jnp.float32)
    out = [f32(7, 9, mx, half, lanes), f32(6, mx, half, lanes), f32(3 if last else 9, mx, half, lanes)]
    if not last:
        out += [f32(9, *s) for s in ((2, half, lanes), (2, half, lanes), (2, 4, lanes), (2, 4, lanes), (mx, 2, lanes), (mx, 2, lanes))]
    vmem = pl.BlockSpec(memory_space=pltpu.VMEM)
    return pl.pallas_call(
        lambda *refs: level_kernel(last, nz, *refs),
        in_specs=[vmem] * 6,
        out_specs=[vmem] * len(out),
        out_shape=out,
        scratch_shapes=[
            pltpu.VMEM((9, nx + 4, ny, wide), jnp.float32),
            pltpu.VMEM((9 * (nx + 4) * ny, wide), jnp.float32),
            pltpu.VMEM((9 * (nx + 4) * ny, wide), jnp.float32),
            pltpu.VMEM((3, mx, half, lanes), jnp.float32),
        ],
        compiler_params=pltpu.CompilerParams(vmem_limit_bytes=24 * MIB),
        name="last_level" if last else "second_level",
    )(approx, *halo, jnp.asarray(third_table(nz, wide)))


def exchange(to_next, to_prev, edge_next, edge_prev, down, up):
    from_prev_edge = shifted(edge_next, "gx", 1)
    from_next_edge = shifted(edge_prev, "gx", -1)
    before = shifted(to_next, "gx", 1)
    after = shifted(to_prev, "gx", -1)
    down = jnp.concatenate([down, from_prev_edge[:, :, 0:2], from_next_edge[:, :, 0:2]], axis=1)
    up = jnp.concatenate([up, from_prev_edge[:, :, 2:4], from_next_edge[:, :, 2:4]], axis=1)
    return before, after, shifted(down, "gy", 1), shifted(up, "gy", -1)


def body(velocity):
    _, nx, ny, nz = velocity.shape
    table = jnp.asarray(third_table(nz, nz))
    tail, head = velocity[:, nx - BEFORE :], velocity[:, :AFTER]
    edges = lambda t: jnp.concatenate([t[:, :, :8], t[:, :, ny - 8 :]], axis=2)
    edge_before = shifted(edges(tail), "gx", 1)
    edge_after = shifted(edges(head), "gx", -1)
    mid_before = shifted(tail[:, :, 8 : ny - 8], "gx", 1)
    mid_after = shifted(head[:, :, 8 : ny - 8], "gx", -1)
    own_before = shifted(velocity[:, :, ny - BEFORE :], "gy", 1)
    own_after = shifted(velocity[:, :, :AFTER], "gy", -1)
    low, rest = local_pass(velocity, own_before, own_after, table)
    edge_before, edge_after, low = lax.optimization_barrier((edge_before, edge_after, low))
    down = jnp.concatenate([edge_before[:, :, 12:], edge_after[:, :, 12:]], axis=1)
    up = jnp.concatenate([edge_before[:, :, :AFTER], edge_after[:, :, :AFTER]], axis=1)
    row_before = shifted(down, "gy", 1)
    row_after = shifted(up, "gy", -1)
    halo = (edge_before, mid_before, edge_after, mid_after, row_before, row_after)
    approx, high, stress_one, *sends = approx_pass(low, halo, table)
    second_halo = exchange(*sends)
    details_one = detail_pass(rest, high, halo, table)
    approx, details_one = lax.optimization_barrier((approx, details_one))
    details_two, stress_two, approx, *sends = level_pass(approx, second_halo, False)
    details_three, stress_three, coarse = level_pass(approx, exchange(*sends), True)
    return details_one, stress_one, details_two, stress_two, details_three, stress_three, coarse


def solution(mesh):
    in_specs = (P(None, "gx", "gy", None),)
    out_specs = (
        P(None, None, "gx", "gy", None),
        P(None, "gx", "gy", None),
        P(None, None, "gx", "gy", None),
        P(None, "gx", "gy", None),
        P(None, None, "gx", "gy", None),
        P(None, "gx", "gy", None),
        P(None, "gx", "gy", None),
    )
    return jax.shard_map(body, mesh=mesh, in_specs=in_specs, out_specs=out_specs, check_vma=False)
```

```python
import jax
import jax.numpy as jnp
import numpy as np
from jax import lax
from jax.experimental import pallas as pl
from jax.experimental.pallas import tpu as pltpu
from jax.sharding import PartitionSpec as P

predict_one = -1.586134342
update_one = -0.05298011854
predict_two = 0.8829110762
update_two = 0.4435068522
scaling = 1.149604398
product_pairs = ((0, 0), (0, 1), (0, 2), (1, 1), (1, 2), (2, 2))
BEFORE = 4
AFTER = 3
GROUP = 3
MIB = 1 << 20


def shifted(block, axis, distance):
    size = lax.axis_size(axis)
    return lax.ppermute(block, axis, [(i, (i + distance) % size) for i in range(size)])


def third_table(length, lanes):
    eye = np.eye(length)
    e, o = eye[:, 0::2], eye[:, 1::2]
    following = lambda t: np.concatenate([t[:, 1:], t[:, -1:]], 1)
    preceding = lambda t: np.concatenate([t[:, :1], t[:, :-1]], 1)
    o = o + predict_one * (e + following(e))
    e = e + update_one * (o + preceding(o))
    o = o + predict_two * (e + following(e))
    e = e + update_two * (o + preceding(o))
    table = np.zeros((lanes, lanes))
    table[:length, : length // 2] = e * scaling
    table[:length, lanes // 2 : lanes // 2 + length // 2] = o / scaling
    return table.astype(np.float32)


def band_scale(by, bx):
    return float(scaling ** ((1 - 2 * by) + (1 - 2 * bx)))


def dot(a, b):
    return jnp.dot(a, b, precision=lax.Precision.HIGHEST, preferred_element_type=jnp.float32)


def ring_lift(e, o):
    n = e.shape[0]
    up = lambda t: pltpu.roll(t, n - 1, 0)
    down = lambda t: pltpu.roll(t, 1, 0)
    o = o + predict_one * (e + up(e))
    e = e + update_one * (o + down(o))
    o = o + predict_two * (e + up(e))
    e = e + update_two * (o + down(o))
    return e, o


def halo_lift(e, o, p, q, r, s, following, preceding, first, last):
    o1 = o + predict_one * (e + following(e, r))
    o1_before = p + predict_one * first(e)
    e1 = e + update_one * (preceding(o1, o1_before) + o1)
    e1_before = q + update_one * o1_before
    e1_after = r + update_one * (last(o1) + s)
    o2 = o1 + predict_two * (e1 + following(e1, e1_after))
    o2_before = o1_before + predict_two * (e1_before + first(e1))
    e2 = e1 + update_two * (preceding(o2, o2_before) + o2)
    return e2, o2


def halo_lift_list(e, o, p, q, r, s):
    m = len(e)
    e = list(e) + [r]
    o1 = [p + predict_one * e[0]]
    o1 += [o[i] + predict_one * (e[i] + e[i + 1]) for i in range(m)] + [s]
    e1 = [q + update_one * o1[0]]
    e1 += [e[i] + update_one * (o1[i] + o1[i + 1]) for i in range(m + 1)]
    o2 = [o1[i] + predict_two * (e1[i] + e1[i + 1]) for i in range(m + 1)]
    e2 = [e1[i + 1] + update_two * (o2[i] + o2[i + 1]) for i in range(m)]
    return e2, o2[1:]


def sublane_lift(e, o, p, q, r, s):
    n = e.shape[0]
    row = lax.broadcasted_iota(jnp.int32, e.shape, 0)
    following = lambda t, edge: jnp.where(row == n - 1, edge, pltpu.roll(t, n - 1, 0))
    preceding = lambda t, edge: jnp.where(row == 0, edge, pltpu.roll(t, 1, 0))
    return halo_lift(e, o, p, q, r, s, following, preceding, lambda t: t[0:1], lambda t: t[n - 1 : n])


def parts_for_next(c):
    p = c[-1] + predict_one * c[-2]
    q = c[-2] + update_one * (c[-3] + predict_one * (c[-4] + c[-2]))
    return p, q


def parts_for_previous(c):
    return c[0], c[1] + predict_one * (c[0] + c[2])


def row_parts(layer):
    rows = layer.shape[0]
    tail = [layer[rows - 4 + i : rows - 3 + i] for i in range(4)]
    head = [layer[i : i + 1] for i in range(3)]
    return parts_for_next(tail) + parts_for_previous(head)


def local_kernel(v_ref, before_ref, after_ref, table_ref, low_ref, rest_ref, rows_ref, stack_ref):
    ny = v_ref.shape[2]
    half = ny // 2
    lanes = v_ref.shape[3] // 2
    even, odd = [], []
    for c in range(3):
        for h in range(2):
            cut = pl.ds(h * lanes, lanes)
            rows_ref[c, h, 12:16, :] = before_ref[c, 0, :, cut]
            rows_ref[c, h, 16 : 16 + ny, :] = v_ref[c, 0, :, cut]
            rows_ref[c, h, 16 + ny : 16 + ny + AFTER, :] = after_ref[c, 0, :, cut]
    count = half + 16
    for h in range(2):
        even = [rows_ref[c, h, pl.ds(0, count, stride=2), :] for c in range(3)]
        odd = [rows_ref[c, h, pl.ds(1, count, stride=2), :] for c in range(3)]
        for f in range(9):
            if f < 3:
                e, o = even[f], odd[f]
            else:
                i, j = product_pairs[f - 3]
                e, o = even[i] * even[j], odd[i] * odd[j]
            e, o = ring_lift(e, o)
            stack_ref[f * ny : f * ny + half, h * lanes : (h + 1) * lanes] = e[8 : 8 + half]
            stack_ref[f * ny + half : (f + 1) * ny, h * lanes : (h + 1) * lanes] = o[8 : 8 + half]
    out = dot(stack_ref[...], table_ref[...])
    for f in range(9):
        low_ref[f, 0] = out[f * ny : f * ny + half, :lanes]
        rest_ref[0, f, 0] = out[f * ny + half : (f + 1) * ny, :lanes]
        rest_ref[1, f, 0] = out[f * ny : f * ny + half, lanes:]
        rest_ref[2, f, 0] = out[f * ny + half : (f + 1) * ny, lanes:]


def local_pass(velocity, before, after, table):
    _, nx, ny, nz = velocity.shape
    half, lanes = ny // 2, nz // 2
    return pl.pallas_call(
        local_kernel,
        grid=(nx,),
        in_specs=[
            pl.BlockSpec((3, 1, ny, nz), lambda i: (0, i, 0, 0)),
            pl.BlockSpec((3, 1, BEFORE, nz), lambda i: (0, i, 0, 0)),
            pl.BlockSpec((3, 1, AFTER, nz), lambda i: (0, i, 0, 0)),
            pl.BlockSpec((nz, nz), lambda i: (0, 0)),
        ],
        out_specs=[
            pl.BlockSpec((9, 1, half, lanes), lambda i: (0, i, 0, 0)),
            pl.BlockSpec((3, 9, 1, half, lanes), lambda i: (0, 0, i, 0, 0)),
        ],
        out_shape=[
            jax.ShapeDtypeStruct((9, nx, half, lanes), jnp.float32),
            jax.ShapeDtypeStruct((3, 9, nx, half, lanes), jnp.float32),
        ],
        scratch_shapes=[pltpu.VMEM((3, 2, ny + 32, lanes), jnp.float32), pltpu.VMEM((9 * ny, nz), jnp.float32)],
        compiler_params=pltpu.CompilerParams(vmem_limit_bytes=24 * MIB),
        cost_estimate=pl.CostEstimate(flops=9 * nx * ny * nz * 512, bytes_accessed=9 * nx * ny * nz * 6, transcendentals=0),
        name="local_pass",
    )(velocity, before, after, table)


def pair_of(f):
    k = f - 3
    one = jnp.where(k < 3, 0, jnp.where(k < 5, 1, 2))
    two = jnp.where(k < 3, k, jnp.where(k < 5, k - 2, 2))
    return jnp.where(f < 3, f, one), jnp.where(f < 3, 3, two)


def gather_rows(refs, rows_ref, even_ref, odd_ref):
    edge_before, mid_before, edge_after, mid_after, row_before, row_after = refs
    mid = mid_before.shape[2]
    ny = mid + 16
    lanes = rows_ref.shape[2]
    count = ny // 2 + 16
    even_ref[3] = jnp.ones(even_ref.shape[1:], jnp.float32)
    odd_ref[3] = jnp.ones(odd_ref.shape[1:], jnp.float32)
    for c in range(3):
        for layer in range(BEFORE + AFTER):
            if layer < BEFORE:
                edge, middle, at = edge_before, mid_before, layer
            else:
                edge, middle, at = edge_after, mid_after, layer - BEFORE
            for h in range(2):
                cut = pl.ds(h * lanes, lanes)
                rows_ref[h, 12:16, :] = row_before[c, layer, :, cut]
                rows_ref[h, 16:24, :] = edge[c, at, 0:8, cut]
                rows_ref[h, 24 : 24 + mid, :] = middle[c, at, :, cut]
                rows_ref[h, 24 + mid : 32 + mid, :] = edge[c, at, 8:16, cut]
                rows_ref[h, 16 + ny : 16 + ny + AFTER, :] = row_after[c, layer, :, cut]
                even_ref[c, layer, :, cut] = rows_ref[h, pl.ds(0, count, stride=2), :]
                odd_ref[c, layer, :, cut] = rows_ref[h, pl.ds(1, count, stride=2), :]


def halo_parts(ref, i, j):
    g = [ref[i, layer] * ref[j, layer] for layer in range(BEFORE + AFTER)]
    return parts_for_next(g[:BEFORE]) + parts_for_previous(g[BEFORE:])


def lift_first(layers, halo):
    return halo_lift_list(layers[0::2], layers[1::2], *halo)


def send_parts(layers, f, next_ref, prev_ref, next_edge_ref, prev_edge_ref, down_ref, up_ref):
    for part, value in enumerate(parts_for_next(layers)):
        next_ref[f, part] = value
        for at, row in enumerate(row_parts(value)):
            next_edge_ref[f, part, at : at + 1, :] = row
    for part, value in enumerate(parts_for_previous(layers)):
        prev_ref[f, part] = value
        for at, row in enumerate(row_parts(value)):
            prev_edge_ref[f, part, at : at + 1, :] = row
    for at, layer in enumerate(layers):
        p, q, r, s = row_parts(layer)
        down_ref[f, at, 0:1, :] = p
        down_ref[f, at, 1:2, :] = q
        up_ref[f, at, 0:1, :] = r
        up_ref[f, at, 1:2, :] = s


def approx_kernel(*refs):
    low_ref, table_ref = refs[:2]
    halo_refs = refs[2:8]
    approx_ref, high_ref, stress_ref = refs[8:11]
    sends = refs[11:17]
    rows_ref, even_ref, odd_ref, kept_ref, stack_ref = refs[17:]
    f = pl.program_id(0)
    nx, half, lanes = low_ref.shape[1:]

    @pl.when(f == 0)
    def _():
        gather_rows(halo_refs, rows_ref, even_ref, odd_ref)

    pairs = [pair_of(f * GROUP + k) for k in range(GROUP)]
    for n, (i, j) in enumerate(pairs):
        even = halo_parts(even_ref, i, j)
        odd = halo_parts(odd_ref, i, j)
        for k in range(4):
            e, _ = ring_lift(even[k], odd[k])
            at = (4 * n + k) * half
            stack_ref[at : at + half, :] = e[8 : 8 + half]
    out = dot(stack_ref[...], table_ref[:, :lanes])
    fields = []
    for n in range(GROUP):
        halo = [out[(4 * n + k) * half : (4 * n + k + 1) * half] for k in range(4)]
        e, o = lift_first([low_ref[n, x] for x in range(nx)], halo)
        e = [t * band_scale(0, 0) for t in e]
        for x in range(nx // 2):
            approx_ref[n, x] = e[x]
            high_ref[n, x] = o[x] * band_scale(0, 1)
        send_parts(e, n, *sends)
        fields.append(e)

    @pl.when(f == 0)
    def _():
        for n in range(GROUP):
            for x in range(nx // 2):
                kept_ref[n, x] = fields[n][x]

    @pl.when(f > 0)
    def _():
        for n, (i, j) in enumerate(pairs):
            for x in range(nx // 2):
                stress_ref[n, x] = approx_ref[n, x] - kept_ref[i, x] * kept_ref[j, x]


def whole(shape):
    return pl.BlockSpec(shape, lambda f: (0,) * len(shape))


def per_field(shape):
    return pl.BlockSpec((GROUP,) + shape, lambda f: (f,) + (0,) * len(shape))


def approx_pass(low, halo, table):
    _, nx, half, lanes = low.shape
    nz, count, mx = 2 * lanes, half + 16, nx // 2
    f32 = lambda *shape: jax.ShapeDtypeStruct(shape, jnp.float32)
    sends = [(2, half, lanes), (2, half, lanes), (2, 4, lanes), (2, 4, lanes), (mx, 2, lanes), (mx, 2, lanes)]
    return pl.pallas_call(
        approx_kernel,
        grid=(9 // GROUP,),
        in_specs=[per_field((nx, half, lanes)), whole((nz, nz))] + [whole(h.shape) for h in halo],
        out_specs=[
            per_field((mx, half, lanes)),
            per_field((mx, half, lanes)),
            pl.BlockSpec((GROUP, mx, half, lanes), lambda f: (jnp.maximum(f - 1, 0), 0, 0, 0)),
        ]
        + [per_field(s) for s in sends],
        out_shape=[f32(9, mx, half, lanes), f32(9, mx, half, lanes), f32(6, mx, half, lanes)] + [f32(9, *s) for s in sends],
        scratch_shapes=[
            pltpu.VMEM((2, 2 * half + 32, lanes), jnp.float32),
            pltpu.VMEM((4, BEFORE + AFTER, count, nz), jnp.float32),
            pltpu.VMEM((4, BEFORE + AFTER, count, nz), jnp.float32),
            pltpu.VMEM((3, mx, half, lanes), jnp.float32),
            pltpu.VMEM((GROUP * 4 * half, nz), jnp.float32),
        ],
        compiler_params=pltpu.CompilerParams(vmem_limit_bytes=24 * MIB),
        name="approx_pass",
    )(low, table, *halo)


def detail_kernel(*refs):
    rest_ref, high_ref, table_ref = refs[:3]
    halo_refs = refs[3:9]
    out_ref, rows_ref, even_ref, odd_ref, stack_ref = refs[9:]
    f = pl.program_id(0)
    nx, half, lanes = rest_ref.shape[2:]

    @pl.when(f == 0)
    def _():
        gather_rows(halo_refs, rows_ref, even_ref, odd_ref)

    for n in range(GROUP):
        i, j = pair_of(f * GROUP + n)
        even = halo_parts(even_ref, i, j)
        odd = halo_parts(odd_ref, i, j)
        for k in range(4):
            e, o = ring_lift(even[k], odd[k])
            at = (8 * n + k) * half
            stack_ref[at : at + half, :] = e[8 : 8 + half]
            at += 4 * half
            stack_ref[at : at + half, :] = o[8 : 8 + half]
    stack_ref[...] = dot(stack_ref[...], table_ref[...])
    for n in range(GROUP):
        for x in range(nx // 2):
            out_ref[0, n, x] = high_ref[n, x]
        for band, (bz, by) in enumerate(((0, 1), (1, 0), (1, 1))):
            halo = []
            for k in range(4):
                at = (8 * n + 4 * by + k) * half
                halo.append(stack_ref[at : at + half, bz * lanes : (bz + 1) * lanes])
            e, o = lift_first([rest_ref[band, n, x] for x in range(nx)], halo)
            at = 4 * bz + 2 * by - 1
            for x in range(nx // 2):
                out_ref[at, n, x] = e[x] * band_scale(by, 0)
                out_ref[at + 1, n, x] = o[x] * band_scale(by, 1)


def detail_pass(rest, high, halo, table):
    _, _, nx, half, lanes = rest.shape
    nz, count, mx = 2 * lanes, half + 16, nx // 2
    return pl.pallas_call(
        detail_kernel,
        grid=(9 // GROUP,),
        in_specs=[
            pl.BlockSpec((3, GROUP, nx, half, lanes), lambda f: (0, f, 0, 0, 0)),
            per_field((mx, half, lanes)),
            whole((nz, nz)),
        ]
        + [whole(h.shape) for h in halo],
        out_specs=pl.BlockSpec((7, GROUP, mx, half, lanes), lambda f: (0, f, 0, 0, 0)),
        out_shape=jax.ShapeDtypeStruct((7, 9, mx, half, lanes), jnp.float32),
        scratch_shapes=[
            pltpu.VMEM((2, 2 * half + 32, lanes), jnp.float32),
            pltpu.VMEM((4, BEFORE + AFTER, count, nz), jnp.float32),
            pltpu.VMEM((4, BEFORE + AFTER, count, nz), jnp.float32),
            pltpu.VMEM((GROUP * 8 * half, nz), jnp.float32),
        ],
        compiler_params=pltpu.CompilerParams(vmem_limit_bytes=24 * MIB),
        cost_estimate=pl.CostEstimate(flops=9 * nx * half * nz * 200, bytes_accessed=9 * nx * half * nz * 16, transcendentals=0),
        name="detail_pass",
    )(rest, high, table, *halo)


def level_rows(refs, nz, lows, pad_ref, stack_ref):
    a_ref, before_ref, after_ref, down_ref, up_ref = refs
    nx, ny = a_ref.shape[1:3]
    half = ny // 2
    wide = stack_ref.shape[1]
    kept = half if lows else ny
    if nz < wide:
        pad_ref[...] = jnp.zeros_like(pad_ref)
    for f in range(9):
        for layer in range(nx + 4):
            if layer < nx:
                source = a_ref.at[f, layer]
            elif layer < nx + 2:
                source = before_ref.at[f, layer - nx]
            else:
                source = after_ref.at[f, layer - nx - 2]
            pad_ref[f, layer, :, :nz] = source[...]
    for f in range(9):
        for layer in range(nx + 4):
            e = pad_ref[f, layer, pl.ds(0, half, stride=2), :]
            o = pad_ref[f, layer, pl.ds(1, half, stride=2), :]
            rows = [down_ref[f, layer, 0:1, :], down_ref[f, layer, 1:2, :], up_ref[f, layer, 0:1, :], up_ref[f, layer, 1:2, :]]
            if nz < wide:
                rows = [jnp.concatenate([row, jnp.zeros((1, wide - nz), jnp.float32)], axis=1) for row in rows]
            e, o = sublane_lift(e, o, *rows)
            at = (f * (nx + 4) + layer) * kept
            stack_ref[at : at + half, :] = e
            if not lows:
                stack_ref[at + half : at + ny, :] = o


def level_approx_kernel(nz, *refs):
    table_ref, approx_ref, stress_ref = refs[5:8]
    sends, (pad_ref, stack_ref, out_ref, kept_ref) = refs[8:-4], refs[-4:]
    nx, ny = refs[0].shape[1:3]
    half, lanes = ny // 2, nz // 2
    level_rows(refs[:5], nz, True, pad_ref, stack_ref)
    out_ref[...] = dot(stack_ref[...], table_ref[...])
    for f in range(9):
        at = f * (nx + 4) * half
        layers = [out_ref[at + layer * half : at + (layer + 1) * half, :] for layer in range(nx + 4)]
        low, _ = lift_first(layers[:nx], layers[nx:])
        approx = [(t * band_scale(0, 0))[:, :lanes] for t in low]
        for x in range(nx // 2):
            if f < 3:
                kept_ref[f, x] = approx[x]
            else:
                i, j = product_pairs[f - 3]
                stress_ref[f - 3, x] = approx[x] - kept_ref[i, x] * kept_ref[j, x]
            approx_ref[f, x] = approx[x]
        for part, value in enumerate(parts_for_next(approx)):
            sends[0][f, part] = value
        for part, value in enumerate(parts_for_previous(approx)):
            sends[1][f, part] = value
        for at, layer in enumerate(approx):
            p, q, r, s = row_parts(layer)
            sends[2][f, at, 0:1, :] = p
            sends[2][f, at, 1:2, :] = q
            sends[3][f, at, 0:1, :] = r
            sends[3][f, at, 1:2, :] = s


def level_detail_kernel(nz, last, *refs):
    table_ref, detail_ref = refs[5:7]
    pad_ref, stack_ref, out_ref, kept_ref = refs[-4:]
    nx, ny = refs[0].shape[1:3]
    half, lanes = ny // 2, nz // 2
    wide = stack_ref.shape[1]
    level_rows(refs[:5], nz, False, pad_ref, stack_ref)
    out_ref[...] = dot(stack_ref[...], table_ref[...])
    for f in range(9):
        at = f * (nx + 4) * ny
        layers = [out_ref[at + layer * ny : at + (layer + 1) * ny, :] for layer in range(nx + 4)]
        low, high = lift_first(layers[:nx], layers[nx:])
        for x in range(nx // 2):
            for bx, value in enumerate((low[x], high[x])):
                for by in range(2):
                    t = value[by * half : (by + 1) * half] * band_scale(by, bx)
                    for bz in range(2):
                        band = 4 * bz + 2 * by + bx
                        piece = t[:, bz * (wide // 2) : bz * (wide // 2) + lanes]
                        if band:
                            detail_ref[band - 1, f, x] = piece
                        elif last:
                            stress_ref, approx_ref = refs[7:9]
                            if f < 3:
                                kept_ref[f, x] = piece
                                approx_ref[f, x] = piece
                            else:
                                i, j = product_pairs[f - 3]
                                stress_ref[f - 3, x] = piece - kept_ref[i, x] * kept_ref[j, x]


def level_call(kernel, approx, halo, out, kept):
    _, nx, ny, nz = approx.shape
    wide = max(nz, 128)
    vmem = pl.BlockSpec(memory_space=pltpu.VMEM)
    return pl.pallas_call(
        kernel,
        in_specs=[vmem] * 6,
        out_specs=[vmem] * len(out),
        out_shape=out,
        scratch_shapes=[
            pltpu.VMEM((9, nx + 4, ny, wide), jnp.float32),
            pltpu.VMEM((9 * (nx + 4) * kept, wide), jnp.float32),
            pltpu.VMEM((9 * (nx + 4) * kept, wide), jnp.float32),
            pltpu.VMEM((3, nx // 2, ny // 2, nz // 2), jnp.float32),
        ],
        compiler_params=pltpu.CompilerParams(vmem_limit_bytes=24 * MIB),
    )(approx, *halo, jnp.asarray(third_table(nz, wide)))


def level_approx(approx, halo):
    _, nx, ny, nz = approx.shape
    mx, half, lanes = nx // 2, ny // 2, nz // 2
    f32 = lambda *shape: jax.ShapeDtypeStruct(shape, jnp.float32)
    sends = ((2, half, lanes), (2, half, lanes), (mx, 2, lanes), (mx, 2, lanes))
    out = [f32(9, mx, half, lanes), f32(6, mx, half, lanes)] + [f32(9, *s) for s in sends]
    return level_call(lambda *refs: level_approx_kernel(nz, *refs), approx, halo, out, half)


def level_details(approx, halo, last):
    _, nx, ny, nz = approx.shape
    mx, half, lanes = nx // 2, ny // 2, nz // 2
    f32 = lambda *shape: jax.ShapeDtypeStruct(shape, jnp.float32)
    out = [f32(7, 9, mx, half, lanes)]
    if last:
        out += [f32(6, mx, half, lanes), f32(3, mx, half, lanes)]
    return level_call(lambda *refs: level_detail_kernel(nz, last, *refs), approx, halo, out, ny)


def exchange_small(to_next, to_prev, down, up):
    before = shifted(to_next, "gx", 1)
    after = shifted(to_prev, "gx", -1)
    rows = before.shape[2]
    cell = lambda at: jnp.concatenate([before[:, :, at : at + 1], after[:, :, at : at + 1]], axis=1)
    tail = jnp.concatenate(parts_for_next([cell(rows - 4 + i) for i in range(4)]), axis=2)
    head = jnp.concatenate(parts_for_previous([cell(i) for i in range(3)]), axis=2)
    down = jnp.concatenate([down, tail], axis=1)
    up = jnp.concatenate([up, head], axis=1)
    return before, after, shifted(down, "gy", 1), shifted(up, "gy", -1)


def exchange(to_next, to_prev, edge_next, edge_prev, down, up):
    from_prev_edge = shifted(edge_next, "gx", 1)
    from_next_edge = shifted(edge_prev, "gx", -1)
    before = shifted(to_next, "gx", 1)
    after = shifted(to_prev, "gx", -1)
    down = jnp.concatenate([down, from_prev_edge[:, :, 0:2], from_next_edge[:, :, 0:2]], axis=1)
    up = jnp.concatenate([up, from_prev_edge[:, :, 2:4], from_next_edge[:, :, 2:4]], axis=1)
    return before, after, shifted(down, "gy", 1), shifted(up, "gy", -1)


def body(velocity):
    _, nx, ny, nz = velocity.shape
    table = jnp.asarray(third_table(nz, nz))
    tail, head = velocity[:, nx - BEFORE :], velocity[:, :AFTER]
    edges = lambda t: jnp.concatenate([t[:, :, :8], t[:, :, ny - 8 :]], axis=2)
    edge_before = shifted(edges(tail), "gx", 1)
    edge_after = shifted(edges(head), "gx", -1)
    mid_before = shifted(tail[:, :, 8 : ny - 8], "gx", 1)
    mid_after = shifted(head[:, :, 8 : ny - 8], "gx", -1)
    own_before = shifted(velocity[:, :, ny - BEFORE :], "gy", 1)
    own_after = shifted(velocity[:, :, :AFTER], "gy", -1)
    low, rest = local_pass(velocity, own_before, own_after, table)
    edge_before, edge_after, low = lax.optimization_barrier((edge_before, edge_after, low))
    down = jnp.concatenate([edge_before[:, :, 12:], edge_after[:, :, 12:]], axis=1)
    up = jnp.concatenate([edge_before[:, :, :AFTER], edge_after[:, :, :AFTER]], axis=1)
    row_before = shifted(down, "gy", 1)
    row_after = shifted(up, "gy", -1)
    halo = (edge_before, mid_before, edge_after, mid_after, row_before, row_after)
    approx, high, stress_one, *sends = approx_pass(low, halo, table)
    second_halo = exchange(*sends)
    details_one = detail_pass(rest, high, halo, table)
    approx, details_one = lax.optimization_barrier((approx, details_one))
    second = approx
    approx, stress_two, *sends = level_approx(second, second_halo)
    third_halo = exchange_small(*sends)
    details_two, = level_details(second, second_halo, False)
    approx, details_two = lax.optimization_barrier((approx, details_two))
    details_three, stress_three, coarse = level_details(approx, third_halo, True)
    return details_one, stress_one, details_two, stress_two, details_three, stress_three, coarse


def solution(mesh):
    in_specs = (P(None, "gx", "gy", None),)
    out_specs = (
        P(None, None, "gx", "gy", None),
        P(None, "gx", "gy", None),
        P(None, None, "gx", "gy", None),
        P(None, "gx", "gy", None),
        P(None, None, "gx", "gy", None),
        P(None, "gx", "gy", None),
        P(None, "gx", "gy", None),
    )
    return jax.shard_map(body, mesh=mesh, in_specs=in_specs, out_specs=out_specs, check_vma=False)
```

```python
import jax
import jax.numpy as jnp
import numpy as np
from jax import lax
from jax.experimental import pallas as pl
from jax.experimental.pallas import tpu as pltpu
from jax.sharding import PartitionSpec as P

predict_one = -1.586134342
update_one = -0.05298011854
predict_two = 0.8829110762
update_two = 0.4435068522
scaling = 1.149604398
product_pairs = ((0, 0), (0, 1), (0, 2), (1, 1), (1, 2), (2, 2))
BEFORE = 4
AFTER = 3
GROUP = 3
MIB = 1 << 20


def shifted(block, axis, distance):
    size = lax.axis_size(axis)
    return lax.ppermute(block, axis, [(i, (i + distance) % size) for i in range(size)])


def third_table(length, lanes):
    eye = np.eye(length)
    e, o = eye[:, 0::2], eye[:, 1::2]
    following = lambda t: np.concatenate([t[:, 1:], t[:, -1:]], 1)
    preceding = lambda t: np.concatenate([t[:, :1], t[:, :-1]], 1)
    o = o + predict_one * (e + following(e))
    e = e + update_one * (o + preceding(o))
    o = o + predict_two * (e + following(e))
    e = e + update_two * (o + preceding(o))
    table = np.zeros((lanes, lanes))
    table[:length, : length // 2] = e * scaling
    table[:length, lanes // 2 : lanes // 2 + length // 2] = o / scaling
    return table.astype(np.float32)


def band_scale(by, bx):
    return float(scaling ** ((1 - 2 * by) + (1 - 2 * bx)))


def dot(a, b):
    return jnp.dot(a, b, precision=lax.Precision.HIGHEST, preferred_element_type=jnp.float32)


def ring_lift(e, o):
    n = e.shape[0]
    up = lambda t: pltpu.roll(t, n - 1, 0)
    down = lambda t: pltpu.roll(t, 1, 0)
    o = o + predict_one * (e + up(e))
    e = e + update_one * (o + down(o))
    o = o + predict_two * (e + up(e))
    e = e + update_two * (o + down(o))
    return e, o


def halo_lift(e, o, p, q, r, s, following, preceding, first, last):
    o1 = o + predict_one * (e + following(e, r))
    o1_before = p + predict_one * first(e)
    e1 = e + update_one * (preceding(o1, o1_before) + o1)
    e1_before = q + update_one * o1_before
    e1_after = r + update_one * (last(o1) + s)
    o2 = o1 + predict_two * (e1 + following(e1, e1_after))
    o2_before = o1_before + predict_two * (e1_before + first(e1))
    e2 = e1 + update_two * (preceding(o2, o2_before) + o2)
    return e2, o2


def halo_lift_list(e, o, p, q, r, s):
    m = len(e)
    e = list(e) + [r]
    o1 = [p + predict_one * e[0]]
    o1 += [o[i] + predict_one * (e[i] + e[i + 1]) for i in range(m)] + [s]
    e1 = [q + update_one * o1[0]]
    e1 += [e[i] + update_one * (o1[i] + o1[i + 1]) for i in range(m + 1)]
    o2 = [o1[i] + predict_two * (e1[i] + e1[i + 1]) for i in range(m + 1)]
    e2 = [e1[i + 1] + update_two * (o2[i] + o2[i + 1]) for i in range(m)]
    return e2, o2[1:]


def sublane_lift(e, o, p, q, r, s):
    n = e.shape[0]
    row = lax.broadcasted_iota(jnp.int32, e.shape, 0)
    following = lambda t, edge: jnp.where(row == n - 1, edge, pltpu.roll(t, n - 1, 0))
    preceding = lambda t, edge: jnp.where(row == 0, edge, pltpu.roll(t, 1, 0))
    return halo_lift(e, o, p, q, r, s, following, preceding, lambda t: t[0:1], lambda t: t[n - 1 : n])


def parts_for_next(c):
    p = c[-1] + predict_one * c[-2]
    q = c[-2] + update_one * (c[-3] + predict_one * (c[-4] + c[-2]))
    return p, q


def parts_for_previous(c):
    return c[0], c[1] + predict_one * (c[0] + c[2])


def row_parts(load, rows):
    tail, head = load(rows - 8), load(0)
    row = lax.broadcasted_iota(jnp.int32, tail.shape, 0)
    inner = tail + predict_one * (pltpu.roll(tail, 1, 0) + pltpu.roll(tail, 7, 0))
    p = tail + predict_one * pltpu.roll(tail, 1, 0)
    q = tail + update_one * pltpu.roll(inner, 1, 0)
    s = head + predict_one * (pltpu.roll(head, 1, 0) + pltpu.roll(head, 7, 0))
    return jnp.where(row == 7, p, q)[6:8], jnp.where(row == 0, head, s)[0:2]


def send_layers(layers, f, at, next_ref, prev_ref):
    for part, value in enumerate(parts_for_next(layers)):
        next_ref[f, part, at : at + 8, :] = value
    for part, value in enumerate(parts_for_previous(layers)):
        prev_ref[f, part, at : at + 8, :] = value


def send_rows(ref, f, down_ref, up_ref):
    for at in range(ref.shape[1]):
        tail, head = row_parts(lambda row: ref[f, at, row : row + 8, :], ref.shape[2])
        down_ref[f, at] = tail
        up_ref[f, at] = head


def local_kernel(v_ref, before_ref, after_ref, table_ref, low_ref, rest_ref, rows_ref, stack_ref):
    ny = v_ref.shape[2]
    half = ny // 2
    lanes = v_ref.shape[3] // 2
    even, odd = [], []
    for c in range(3):
        for h in range(2):
            cut = pl.ds(h * lanes, lanes)
            rows_ref[c, h, 12:16, :] = before_ref[c, 0, :, cut]
            rows_ref[c, h, 16 : 16 + ny, :] = v_ref[c, 0, :, cut]
            rows_ref[c, h, 16 + ny : 16 + ny + AFTER, :] = after_ref[c, 0, :, cut]
    count = half + 16
    for h in range(2):
        even = [rows_ref[c, h, pl.ds(0, count, stride=2), :] for c in range(3)]
        odd = [rows_ref[c, h, pl.ds(1, count, stride=2), :] for c in range(3)]
        for f in range(9):
            if f < 3:
                e, o = even[f], odd[f]
            else:
                i, j = product_pairs[f - 3]
                e, o = even[i] * even[j], odd[i] * odd[j]
            e, o = ring_lift(e, o)
            stack_ref[f * ny : f * ny + half, h * lanes : (h + 1) * lanes] = e[8 : 8 + half]
            stack_ref[f * ny + half : (f + 1) * ny, h * lanes : (h + 1) * lanes] = o[8 : 8 + half]
    out = dot(stack_ref[...], table_ref[...])
    for f in range(9):
        low_ref[f, 0] = out[f * ny : f * ny + half, :lanes]
        rest_ref[0, f, 0] = out[f * ny + half : (f + 1) * ny, :lanes]
        rest_ref[1, f, 0] = out[f * ny : f * ny + half, lanes:]
        rest_ref[2, f, 0] = out[f * ny + half : (f + 1) * ny, lanes:]


def local_pass(velocity, before, after, table, start):
    _, nx, ny, nz = velocity.shape
    nx = nx // 2
    half, lanes = ny // 2, nz // 2
    return pl.pallas_call(
        local_kernel,
        grid=(nx,),
        in_specs=[
            pl.BlockSpec((3, 1, ny, nz), lambda i: (0, i + start, 0, 0)),
            pl.BlockSpec((3, 1, BEFORE, nz), lambda i: (0, i + start, 0, 0)),
            pl.BlockSpec((3, 1, AFTER, nz), lambda i: (0, i + start, 0, 0)),
            pl.BlockSpec((nz, nz), lambda i: (0, 0)),
        ],
        out_specs=[
            pl.BlockSpec((9, 1, half, lanes), lambda i: (0, i, 0, 0)),
            pl.BlockSpec((3, 9, 1, half, lanes), lambda i: (0, 0, i, 0, 0)),
        ],
        out_shape=[
            jax.ShapeDtypeStruct((9, nx, half, lanes), jnp.float32),
            jax.ShapeDtypeStruct((3, 9, nx, half, lanes), jnp.float32),
        ],
        scratch_shapes=[pltpu.VMEM((3, 2, ny + 32, lanes), jnp.float32), pltpu.VMEM((9 * ny, nz), jnp.float32)],
        compiler_params=pltpu.CompilerParams(vmem_limit_bytes=24 * MIB),
        cost_estimate=pl.CostEstimate(flops=9 * nx * ny * nz * 512, bytes_accessed=9 * nx * ny * nz * 6, transcendentals=0),
        name="local_pass",
    )(velocity, before, after, table)


def pair_of(f):
    k = f - 3
    one = jnp.where(k < 3, 0, jnp.where(k < 5, 1, 2))
    two = jnp.where(k < 3, k, jnp.where(k < 5, k - 2, 2))
    return jnp.where(f < 3, f, one), jnp.where(f < 3, 3, two)


def gather_rows(refs, rows_ref, even_ref, odd_ref):
    edge_before, mid_before, edge_after, mid_after, row_before, row_after = refs
    mid = mid_before.shape[2]
    ny = mid + 16
    lanes = rows_ref.shape[2]
    count = ny // 2 + 16
    even_ref[3] = jnp.ones(even_ref.shape[1:], jnp.float32)
    odd_ref[3] = jnp.ones(odd_ref.shape[1:], jnp.float32)
    for c in range(3):
        for layer in range(BEFORE + AFTER):
            if layer < BEFORE:
                edge, middle, at = edge_before, mid_before, layer
            else:
                edge, middle, at = edge_after, mid_after, layer - BEFORE
            for h in range(2):
                cut = pl.ds(h * lanes, lanes)
                rows_ref[h, 12:16, :] = row_before[c, layer, :, cut]
                rows_ref[h, 16:24, :] = edge[c, at, 0:8, cut]
                rows_ref[h, 24 : 24 + mid, :] = middle[c, at, :, cut]
                rows_ref[h, 24 + mid : 32 + mid, :] = edge[c, at, 8:16, cut]
                rows_ref[h, 16 + ny : 16 + ny + AFTER, :] = row_after[c, layer, :, cut]
                even_ref[c, layer, :, cut] = rows_ref[h, pl.ds(0, count, stride=2), :]
                odd_ref[c, layer, :, cut] = rows_ref[h, pl.ds(1, count, stride=2), :]


def lift_first(layers, halo):
    return halo_lift_list(layers[0::2], layers[1::2], *halo)


def halo_stack(pairs, both, even_ref, odd_ref, part_ref, stack_ref):
    count, nz = even_ref.shape[2:]
    half, lanes = count - 16, nz // 2
    kinds = 8 if both else 4
    for n, (i, j) in enumerate(pairs):
        for h in range(2):
            cut = slice(h * lanes, (h + 1) * lanes)
            for parity, ref in enumerate((even_ref, odd_ref)):
                for r in range(0, count, 16):
                    rows = slice(r, r + 16)
                    g = [ref[i, layer, rows, cut] * ref[j, layer, rows, cut] for layer in range(BEFORE + AFTER)]
                    for k, value in enumerate(parts_for_next(g[:BEFORE]) + parts_for_previous(g[BEFORE:])):
                        part_ref[parity, k, rows, :] = value
            for k in range(4):
                e, o = ring_lift(part_ref[0, k], part_ref[1, k])
                at = (kinds * n + k) * half
                stack_ref[at : at + half, cut] = e[8 : 8 + half]
                if both:
                    at += 4 * half
                    stack_ref[at : at + half, cut] = o[8 : 8 + half]


def layer_list(refs, index, rows):
    return [ref[index + (x, rows)] for ref in refs for x in range(ref.shape[len(index)])]


def approx_kernel(*refs):
    low_refs, table_ref = refs[:2], refs[2]
    halo_refs = refs[3:9]
    approx_ref, high_ref, stress_ref = refs[9:12]
    next_ref, prev_ref, next_edge_ref, prev_edge_ref, down_ref, up_ref = refs[12:18]
    rows_ref, even_ref, odd_ref, kept_ref, part_ref, stack_ref, out_ref = refs[18:]
    f = pl.program_id(0)
    half, lanes = low_refs[0].shape[2:]
    mx = approx_ref.shape[1]

    @pl.when(f == 0)
    def _():
        gather_rows(halo_refs, rows_ref, even_ref, odd_ref)

    pairs = [pair_of(f * GROUP + n) for n in range(GROUP)]
    halo_stack(pairs, False, even_ref, odd_ref, part_ref, stack_ref)
    out_ref[...] = dot(stack_ref[...], table_ref[:, :lanes])
    for n in range(GROUP):
        for r in range(0, half, 8):
            rows = slice(r, r + 8)
            halo = [out_ref[(4 * n + k) * half + r : (4 * n + k) * half + r + 8, :] for k in range(4)]
            e, o = lift_first(layer_list(low_refs, (n,), rows), halo)
            e = [t * band_scale(0, 0) for t in e]
            for x in range(mx):
                approx_ref[n, x, rows, :] = e[x]
                high_ref[n, x, rows, :] = o[x] * band_scale(0, 1)
            send_layers(e, n, r, next_ref, prev_ref)
        send_rows(approx_ref, n, down_ref, up_ref)
        for ref, edge_ref in ((next_ref, next_edge_ref), (prev_ref, prev_edge_ref)):
            for part in range(2):
                tail, head = row_parts(lambda row: ref[n, part, row : row + 8, :], half)
                edge_ref[n, part, 0:2, :] = tail
                edge_ref[n, part, 2:4, :] = head

    @pl.when(f == 0)
    def _():
        kept_ref[...] = approx_ref[...]

    @pl.when(f > 0)
    def _():
        for n, (i, j) in enumerate(pairs):
            for x in range(mx):
                stress_ref[n, x] = approx_ref[n, x] - kept_ref[i, x] * kept_ref[j, x]


def whole(shape):
    return pl.BlockSpec(shape, lambda f: (0,) * len(shape))


def per_field(shape):
    return pl.BlockSpec((GROUP,) + shape, lambda f: (f,) + (0,) * len(shape))


def approx_pass(lows, halo, table):
    _, nx, half, lanes = lows[0].shape
    nz, count, mx = 2 * lanes, half + 16, nx
    f32 = lambda *shape: jax.ShapeDtypeStruct(shape, jnp.float32)
    sends = [(2, half, lanes), (2, half, lanes), (2, 4, lanes), (2, 4, lanes), (mx, 2, lanes), (mx, 2, lanes)]
    return pl.pallas_call(
        approx_kernel,
        grid=(9 // GROUP,),
        in_specs=[per_field((nx, half, lanes))] * 2 + [whole((nz, nz))] + [whole(h.shape) for h in halo],
        out_specs=[
            per_field((mx, half, lanes)),
            per_field((mx, half, lanes)),
            pl.BlockSpec((GROUP, mx, half, lanes), lambda f: (jnp.maximum(f - 1, 0), 0, 0, 0)),
        ]
        + [per_field(s) for s in sends],
        out_shape=[f32(9, mx, half, lanes), f32(9, mx, half, lanes), f32(6, mx, half, lanes)] + [f32(9, *s) for s in sends],
        scratch_shapes=halo_scratch(half, lanes)
        + [
            pltpu.VMEM((3, mx, half, lanes), jnp.float32),
            pltpu.VMEM((2, 4, count, lanes), jnp.float32),
            pltpu.VMEM((GROUP * 4 * half, nz), jnp.float32),
            pltpu.VMEM((GROUP * 4 * half, lanes), jnp.float32),
        ],
        compiler_params=pltpu.CompilerParams(vmem_limit_bytes=24 * MIB),
        name="approx_pass",
    )(*lows, table, *halo)


def halo_scratch(half, lanes):
    return [
        pltpu.VMEM((2, 2 * half + 32, lanes), jnp.float32),
        pltpu.VMEM((4, BEFORE + AFTER, half + 16, 2 * lanes), jnp.float32),
        pltpu.VMEM((4, BEFORE + AFTER, half + 16, 2 * lanes), jnp.float32),
    ]


def detail_kernel(*refs):
    rest_refs, high_ref, table_ref = refs[:2], refs[2], refs[3]
    halo_refs = refs[4:10]
    out_ref, rows_ref, even_ref, odd_ref, part_ref, stack_ref = refs[10:]
    f = pl.program_id(0)
    half, lanes = high_ref.shape[2:]
    mx = high_ref.shape[1]

    @pl.when(f == 0)
    def _():
        gather_rows(halo_refs, rows_ref, even_ref, odd_ref)

    pairs = [pair_of(f * GROUP + n) for n in range(GROUP)]
    halo_stack(pairs, True, even_ref, odd_ref, part_ref, stack_ref)
    stack_ref[...] = dot(stack_ref[...], table_ref[...])
    for n in range(GROUP):
        for x in range(mx):
            out_ref[0, n, x] = high_ref[n, x]
        for band, (bz, by) in enumerate(((0, 1), (1, 0), (1, 1))):
            plane = 4 * bz + 2 * by - 1
            for r in range(0, half, 8):
                rows = slice(r, r + 8)
                halo = []
                for k in range(4):
                    at = (8 * n + 4 * by + k) * half + r
                    halo.append(stack_ref[at : at + 8, bz * lanes : (bz + 1) * lanes])
                e, o = lift_first(layer_list(rest_refs, (band, n), rows), halo)
                for x in range(mx):
                    out_ref[plane, n, x, rows, :] = e[x] * band_scale(by, 0)
                    out_ref[plane + 1, n, x, rows, :] = o[x] * band_scale(by, 1)


def detail_pass(rests, high, halo, table):
    _, mx, half, lanes = high.shape
    nz, count = 2 * lanes, half + 16
    return pl.pallas_call(
        detail_kernel,
        grid=(9 // GROUP,),
        in_specs=[pl.BlockSpec((3, GROUP, mx, half, lanes), lambda f: (0, f, 0, 0, 0))] * 2
        + [per_field((mx, half, lanes)), whole((nz, nz))]
        + [whole(h.shape) for h in halo],
        out_specs=pl.BlockSpec((7, GROUP, mx, half, lanes), lambda f: (0, f, 0, 0, 0)),
        out_shape=jax.ShapeDtypeStruct((7, 9, mx, half, lanes), jnp.float32),
        scratch_shapes=halo_scratch(half, lanes)
        + [pltpu.VMEM((2, 4, count, lanes), jnp.float32), pltpu.VMEM((GROUP * 8 * half, nz), jnp.float32)],
        compiler_params=pltpu.CompilerParams(vmem_limit_bytes=24 * MIB),
        cost_estimate=pl.CostEstimate(flops=18 * mx * half * nz * 200, bytes_accessed=18 * mx * half * nz * 16, transcendentals=0),
        name="detail_pass",
    )(*rests, high, table, *halo)


def level_rows(refs, nz, lows, pad_ref, stack_ref):
    a_ref, before_ref, after_ref, down_ref, up_ref = refs
    nx, ny = a_ref.shape[1:3]
    half = ny // 2
    wide = stack_ref.shape[1]
    kept = half if lows else ny
    if nz < wide:
        pad_ref[...] = jnp.zeros_like(pad_ref)
    for f in range(9):
        for layer in range(nx + 4):
            if layer < nx:
                source, at = a_ref, layer
            elif layer < nx + 2:
                source, at = before_ref, layer - nx
            else:
                source, at = after_ref, layer - nx - 2
            if nz < wide:
                pad_ref[f, layer, :, :nz] = source[f, at]
                source, at = pad_ref, layer
            e = source[f, at, pl.ds(0, half, stride=2), :]
            o = source[f, at, pl.ds(1, half, stride=2), :]
            rows = [down_ref[f, layer, 1:2, :], down_ref[f, layer, 0:1, :], up_ref[f, layer, 0:1, :], up_ref[f, layer, 1:2, :]]
            if nz < wide:
                rows = [jnp.concatenate([row, jnp.zeros((1, wide - nz), jnp.float32)], axis=1) for row in rows]
            e, o = sublane_lift(e, o, *rows)
            at = (f * (nx + 4) + layer) * kept
            stack_ref[at : at + half, :] = e
            if not lows:
                stack_ref[at + half : at + ny, :] = o


def level_approx_kernel(nz, *refs):
    table_ref, approx_ref, stress_ref = refs[5:8]
    sends, (pad_ref, stack_ref, out_ref, kept_ref) = refs[8:-4], refs[-4:]
    nx, ny = refs[0].shape[1:3]
    half, lanes = ny // 2, nz // 2
    level_rows(refs[:5], nz, True, pad_ref, stack_ref)
    out_ref[...] = dot(stack_ref[...], table_ref[...])
    mx = nx // 2
    for f in range(9):
        for r in range(0, half, 8):
            rows = slice(r, r + 8)
            layers = []
            for layer in range(nx + 4):
                at = (f * (nx + 4) + layer) * half + r
                layers.append(out_ref[at : at + 8, :])
            low, _ = lift_first(layers[:nx], layers[nx:])
            approx = [(t * band_scale(0, 0))[:, :lanes] for t in low]
            for x in range(mx):
                if f < 3:
                    kept_ref[f, x, rows, :] = approx[x]
                else:
                    i, j = product_pairs[f - 3]
                    stress_ref[f - 3, x, rows, :] = approx[x] - kept_ref[i, x, rows, :] * kept_ref[j, x, rows, :]
                approx_ref[f, x, rows, :] = approx[x]
            send_layers(approx, f, r, sends[0], sends[1])
        send_rows(approx_ref, f, sends[2], sends[3])


def level_detail_kernel(nz, last, *refs):
    table_ref, detail_ref = refs[5:7]
    pad_ref, stack_ref, out_ref, kept_ref = refs[-4:]
    nx, ny = refs[0].shape[1:3]
    half, lanes = ny // 2, nz // 2
    wide = stack_ref.shape[1]
    level_rows(refs[:5], nz, False, pad_ref, stack_ref)
    out_ref[...] = dot(stack_ref[...], table_ref[...])
    for f in range(9):
        for by in range(2):
            for r in range(0, half, 8):
                rows = slice(r, r + 8)
                layers = []
                for layer in range(nx + 4):
                    at = (f * (nx + 4) + layer) * ny + by * half + r
                    layers.append(out_ref[at : at + 8, :])
                low, high = lift_first(layers[:nx], layers[nx:])
                for x in range(nx // 2):
                    for bx, value in enumerate((low[x], high[x])):
                        t = value * band_scale(by, bx)
                        for bz in range(2):
                            band = 4 * bz + 2 * by + bx
                            piece = t[:, bz * (wide // 2) : bz * (wide // 2) + lanes]
                            if band:
                                detail_ref[band - 1, f, x, rows, :] = piece
                            elif last:
                                stress_ref, approx_ref = refs[7:9]
                                if f < 3:
                                    kept_ref[f, x, rows, :] = piece
                                    approx_ref[f, x, rows, :] = piece
                                else:
                                    i, j = product_pairs[f - 3]
                                    stress_ref[f - 3, x, rows, :] = piece - kept_ref[i, x, rows, :] * kept_ref[j, x, rows, :]


def level_call(kernel, approx, halo, out, kept):
    _, nx, ny, nz = approx.shape
    wide = max(nz, 128)
    vmem = pl.BlockSpec(memory_space=pltpu.VMEM)
    return pl.pallas_call(
        kernel,
        in_specs=[vmem] * 6,
        out_specs=[vmem] * len(out),
        out_shape=out,
        scratch_shapes=[
            pltpu.VMEM((9, nx + 4, ny, wide), jnp.float32),
            pltpu.VMEM((9 * (nx + 4) * kept, wide), jnp.float32),
            pltpu.VMEM((9 * (nx + 4) * kept, wide), jnp.float32),
            pltpu.VMEM((3, nx // 2, ny // 2, nz // 2), jnp.float32),
        ],
        compiler_params=pltpu.CompilerParams(vmem_limit_bytes=24 * MIB),
    )(approx, *halo, jnp.asarray(third_table(nz, wide)))


def level_approx(approx, halo):
    _, nx, ny, nz = approx.shape
    mx, half, lanes = nx // 2, ny // 2, nz // 2
    f32 = lambda *shape: jax.ShapeDtypeStruct(shape, jnp.float32)
    sends = ((2, half, lanes), (2, half, lanes), (mx, 2, lanes), (mx, 2, lanes))
    out = [f32(9, mx, half, lanes), f32(6, mx, half, lanes)] + [f32(9, *s) for s in sends]
    return level_call(lambda *refs: level_approx_kernel(nz, *refs), approx, halo, out, half)


def level_details(approx, halo, last):
    _, nx, ny, nz = approx.shape
    mx, half, lanes = nx // 2, ny // 2, nz // 2
    f32 = lambda *shape: jax.ShapeDtypeStruct(shape, jnp.float32)
    out = [f32(7, 9, mx, half, lanes)]
    if last:
        out += [f32(6, mx, half, lanes), f32(3, mx, half, lanes)]
    return level_call(lambda *refs: level_detail_kernel(nz, last, *refs), approx, halo, out, ny)


def halo_rows(before, after, down, up):
    rows = before.shape[2]
    cell = lambda at: jnp.concatenate([before[:, :, at : at + 1], after[:, :, at : at + 1]], axis=1)
    p, q = parts_for_next([cell(rows - 4 + i) for i in range(4)])
    down = jnp.concatenate([down, jnp.concatenate([q, p], axis=2)], axis=1)
    head = jnp.concatenate(parts_for_previous([cell(i) for i in range(3)]), axis=2)
    up = jnp.concatenate([up, head], axis=1)
    return shifted(down, "gy", 1), shifted(up, "gy", -1)


def exchange(to_next, to_prev, edge_next, edge_prev, down, up):
    from_prev_edge = shifted(edge_next, "gx", 1)
    from_next_edge = shifted(edge_prev, "gx", -1)
    before = shifted(to_next, "gx", 1)
    after = shifted(to_prev, "gx", -1)
    down = jnp.concatenate([down, from_prev_edge[:, :, 0:2], from_next_edge[:, :, 0:2]], axis=1)
    up = jnp.concatenate([up, from_prev_edge[:, :, 2:4], from_next_edge[:, :, 2:4]], axis=1)
    return before, after, shifted(down, "gy", 1), shifted(up, "gy", -1)


def body(velocity):
    _, nx, ny, nz = velocity.shape
    table = jnp.asarray(third_table(nz, nz))
    tail, head = velocity[:, nx - BEFORE :], velocity[:, :AFTER]
    edges = lambda t: jnp.concatenate([t[:, :, :8], t[:, :, ny - 8 :]], axis=2)
    edge_before = shifted(edges(tail), "gx", 1)
    edge_after = shifted(edges(head), "gx", -1)
    mid_before = shifted(tail[:, :, 8 : ny - 8], "gx", 1)
    mid_after = shifted(head[:, :, 8 : ny - 8], "gx", -1)
    own_before = shifted(velocity[:, :, ny - BEFORE :], "gy", 1)
    own_after = shifted(velocity[:, :, :AFTER], "gy", -1)
    low_one, rest_one = local_pass(velocity, own_before, own_after, table, 0)
    edge_before, edge_after, low_one = lax.optimization_barrier((edge_before, edge_after, low_one))
    down = jnp.concatenate([edge_before[:, :, 12:], edge_after[:, :, 12:]], axis=1)
    up = jnp.concatenate([edge_before[:, :, :AFTER], edge_after[:, :, :AFTER]], axis=1)
    row_before = shifted(down, "gy", 1)
    row_after = shifted(up, "gy", -1)
    low_two, rest_two = local_pass(velocity, own_before, own_after, table, nx // 2)
    halo = (edge_before, mid_before, edge_after, mid_after, row_before, row_after)
    approx, high, stress_one, *sends = approx_pass((low_one, low_two), halo, table)
    second_halo = exchange(*sends)
    details_one = detail_pass((rest_one, rest_two), high, halo, table)
    approx, details_one = lax.optimization_barrier((approx, details_one))
    second = approx
    approx, stress_two, *sends = level_approx(second, second_halo)
    before = shifted(sends[0], "gx", 1)
    after = shifted(sends[1], "gx", -1)
    (details_two,) = level_details(second, second_halo, False)
    before, after, details_two = lax.optimization_barrier((before, after, details_two))
    third_halo = (before, after) + halo_rows(before, after, *sends[2:])
    details_three, stress_three, coarse = level_details(approx, third_halo, True)
    return details_one, stress_one, details_two, stress_two, details_three, stress_three, coarse


def solution(mesh):
    in_specs = (P(None, "gx", "gy", None),)
    out_specs = (
        P(None, None, "gx", "gy", None),
        P(None, "gx", "gy", None),
        P(None, None, "gx", "gy", None),
        P(None, "gx", "gy", None),
        P(None, None, "gx", "gy", None),
        P(None, "gx", "gy", None),
        P(None, "gx", "gy", None),
    )
    return jax.shard_map(body, mesh=mesh, in_specs=in_specs, out_specs=out_specs, check_vma=False)
```

```python
import jax
import jax.numpy as jnp
import numpy as np
from jax import lax
from jax.experimental import pallas as pl
from jax.experimental.pallas import tpu as pltpu
from jax.sharding import PartitionSpec as P

predict_one = -1.586134342
update_one = -0.05298011854
predict_two = 0.8829110762
update_two = 0.4435068522
scaling = 1.149604398
product_pairs = ((0, 0), (0, 1), (0, 2), (1, 1), (1, 2), (2, 2))
BEFORE = 4
AFTER = 3
GROUP = 3
MIB = 1 << 20


def shifted(block, axis, distance):
    size = lax.axis_size(axis)
    return lax.ppermute(block, axis, [(i, (i + distance) % size) for i in range(size)])


def third_table(length, lanes):
    eye = np.eye(length)
    e, o = eye[:, 0::2], eye[:, 1::2]
    following = lambda t: np.concatenate([t[:, 1:], t[:, -1:]], 1)
    preceding = lambda t: np.concatenate([t[:, :1], t[:, :-1]], 1)
    o = o + predict_one * (e + following(e))
    e = e + update_one * (o + preceding(o))
    o = o + predict_two * (e + following(e))
    e = e + update_two * (o + preceding(o))
    table = np.zeros((lanes, lanes))
    table[:length, : length // 2] = e * scaling
    table[:length, lanes // 2 : lanes // 2 + length // 2] = o / scaling
    return table.astype(np.float32)


def band_scale(by, bx):
    return float(scaling ** ((1 - 2 * by) + (1 - 2 * bx)))


def dot(a, b):
    a_high, b_high = a.astype(jnp.bfloat16), b.astype(jnp.bfloat16)
    a_low = (a - a_high.astype(jnp.float32)).astype(jnp.bfloat16)
    b_low = (b - b_high.astype(jnp.float32)).astype(jnp.bfloat16)
    part = lambda x, y: jnp.dot(x, y, preferred_element_type=jnp.float32)
    return part(a_high, b_high) + (part(a_high, b_low) + part(a_low, b_high))


def ring_lift(e, o):
    n = e.shape[0]
    up = lambda t: pltpu.roll(t, n - 1, 0)
    down = lambda t: pltpu.roll(t, 1, 0)
    o = o + predict_one * (e + up(e))
    e = e + update_one * (o + down(o))
    o = o + predict_two * (e + up(e))
    e = e + update_two * (o + down(o))
    return e, o


def halo_lift(e, o, p, q, r, s, following, preceding, first, last):
    o1 = o + predict_one * (e + following(e, r))
    o1_before = p + predict_one * first(e)
    e1 = e + update_one * (preceding(o1, o1_before) + o1)
    e1_before = q + update_one * o1_before
    e1_after = r + update_one * (last(o1) + s)
    o2 = o1 + predict_two * (e1 + following(e1, e1_after))
    o2_before = o1_before + predict_two * (e1_before + first(e1))
    e2 = e1 + update_two * (preceding(o2, o2_before) + o2)
    return e2, o2


def halo_lift_list(e, o, p, q, r, s):
    m = len(e)
    e = list(e) + [r]
    o1 = [p + predict_one * e[0]]
    o1 += [o[i] + predict_one * (e[i] + e[i + 1]) for i in range(m)] + [s]
    e1 = [q + update_one * o1[0]]
    e1 += [e[i] + update_one * (o1[i] + o1[i + 1]) for i in range(m + 1)]
    o2 = [o1[i] + predict_two * (e1[i] + e1[i + 1]) for i in range(m + 1)]
    e2 = [e1[i + 1] + update_two * (o2[i] + o2[i + 1]) for i in range(m)]
    return e2, o2[1:]


def sublane_lift(e, o, p, q, r, s):
    n = e.shape[0]
    row = lax.broadcasted_iota(jnp.int32, e.shape, 0)
    following = lambda t, edge: jnp.where(row == n - 1, edge, pltpu.roll(t, n - 1, 0))
    preceding = lambda t, edge: jnp.where(row == 0, edge, pltpu.roll(t, 1, 0))
    return halo_lift(e, o, p, q, r, s, following, preceding, lambda t: t[0:1], lambda t: t[n - 1 : n])


def parts_for_next(c):
    p = c[-1] + predict_one * c[-2]
    q = c[-2] + update_one * (c[-3] + predict_one * (c[-4] + c[-2]))
    return p, q


def parts_for_previous(c):
    return c[0], c[1] + predict_one * (c[0] + c[2])


def row_parts(load, rows):
    tail, head = load(rows - 8), load(0)
    row = lax.broadcasted_iota(jnp.int32, tail.shape, 0)
    inner = tail + predict_one * (pltpu.roll(tail, 1, 0) + pltpu.roll(tail, 7, 0))
    p = tail + predict_one * pltpu.roll(tail, 1, 0)
    q = tail + update_one * pltpu.roll(inner, 1, 0)
    s = head + predict_one * (pltpu.roll(head, 1, 0) + pltpu.roll(head, 7, 0))
    return jnp.where(row == 7, p, q)[6:8], jnp.where(row == 0, head, s)[0:2]


def send_layers(layers, f, at, next_ref, prev_ref):
    for part, value in enumerate(parts_for_next(layers)):
        next_ref[f, part, at : at + 8, :] = value
    for part, value in enumerate(parts_for_previous(layers)):
        prev_ref[f, part, at : at + 8, :] = value


def send_rows(ref, f, down_ref, up_ref):
    for at in range(ref.shape[1]):
        tail, head = row_parts(lambda row: ref[f, at, row : row + 8, :], ref.shape[2])
        down_ref[f, at] = tail
        up_ref[f, at] = head


def local_kernel(v_ref, before_ref, after_ref, table_ref, low_ref, rest_ref, rows_ref, stack_ref):
    ny = v_ref.shape[2]
    half = ny // 2
    lanes = v_ref.shape[3] // 2
    even, odd = [], []
    for c in range(3):
        for h in range(2):
            cut = pl.ds(h * lanes, lanes)
            rows_ref[c, h, 12:16, :] = before_ref[c, 0, :, cut]
            rows_ref[c, h, 16 : 16 + ny, :] = v_ref[c, 0, :, cut]
            rows_ref[c, h, 16 + ny : 16 + ny + AFTER, :] = after_ref[c, 0, :, cut]
    count = half + 16
    for h in range(2):
        even = [rows_ref[c, h, pl.ds(0, count, stride=2), :] for c in range(3)]
        odd = [rows_ref[c, h, pl.ds(1, count, stride=2), :] for c in range(3)]
        for f in range(9):
            if f < 3:
                e, o = even[f], odd[f]
            else:
                i, j = product_pairs[f - 3]
                e, o = even[i] * even[j], odd[i] * odd[j]
            e, o = ring_lift(e, o)
            stack_ref[f * ny : f * ny + half, h * lanes : (h + 1) * lanes] = e[8 : 8 + half]
            stack_ref[f * ny + half : (f + 1) * ny, h * lanes : (h + 1) * lanes] = o[8 : 8 + half]
    out = dot(stack_ref[...], table_ref[...])
    for f in range(9):
        low_ref[f, 0] = out[f * ny : f * ny + half, :lanes]
        rest_ref[0, f, 0] = out[f * ny + half : (f + 1) * ny, :lanes]
        rest_ref[1, f, 0] = out[f * ny : f * ny + half, lanes:]
        rest_ref[2, f, 0] = out[f * ny + half : (f + 1) * ny, lanes:]


def local_pass(velocity, before, after, table, start):
    _, nx, ny, nz = velocity.shape
    nx = nx // 2
    half, lanes = ny // 2, nz // 2
    return pl.pallas_call(
        local_kernel,
        grid=(nx,),
        in_specs=[
            pl.BlockSpec((3, 1, ny, nz), lambda i: (0, i + start, 0, 0)),
            pl.BlockSpec((3, 1, BEFORE, nz), lambda i: (0, i + start, 0, 0)),
            pl.BlockSpec((3, 1, AFTER, nz), lambda i: (0, i + start, 0, 0)),
            pl.BlockSpec((nz, nz), lambda i: (0, 0)),
        ],
        out_specs=[
            pl.BlockSpec((9, 1, half, lanes), lambda i: (0, i, 0, 0)),
            pl.BlockSpec((3, 9, 1, half, lanes), lambda i: (0, 0, i, 0, 0)),
        ],
        out_shape=[
            jax.ShapeDtypeStruct((9, nx, half, lanes), jnp.float32),
            jax.ShapeDtypeStruct((3, 9, nx, half, lanes), jnp.float32),
        ],
        scratch_shapes=[pltpu.VMEM((3, 2, ny + 32, lanes), jnp.float32), pltpu.VMEM((9 * ny, nz), jnp.float32)],
        compiler_params=pltpu.CompilerParams(vmem_limit_bytes=24 * MIB),
        cost_estimate=pl.CostEstimate(flops=9 * nx * ny * nz * 512, bytes_accessed=9 * nx * ny * nz * 6, transcendentals=0),
        name="local_pass",
    )(velocity, before, after, table)


def pair_of(f):
    k = f - 3
    one = jnp.where(k < 3, 0, jnp.where(k < 5, 1, 2))
    two = jnp.where(k < 3, k, jnp.where(k < 5, k - 2, 2))
    return jnp.where(f < 3, f, one), jnp.where(f < 3, 3, two)


def gather_rows(refs, rows_ref, even_ref, odd_ref):
    edge_before, mid_before, edge_after, mid_after, row_before, row_after = refs
    mid = mid_before.shape[2]
    ny = mid + 16
    lanes = rows_ref.shape[2]
    count = ny // 2 + 16
    even_ref[3] = jnp.ones(even_ref.shape[1:], jnp.float32)
    odd_ref[3] = jnp.ones(odd_ref.shape[1:], jnp.float32)
    for c in range(3):
        for layer in range(BEFORE + AFTER):
            if layer < BEFORE:
                edge, middle, at = edge_before, mid_before, layer
            else:
                edge, middle, at = edge_after, mid_after, layer - BEFORE
            for h in range(2):
                cut = pl.ds(h * lanes, lanes)
                rows_ref[h, 12:16, :] = row_before[c, layer, :, cut]
                rows_ref[h, 16:24, :] = edge[c, at, 0:8, cut]
                rows_ref[h, 24 : 24 + mid, :] = middle[c, at, :, cut]
                rows_ref[h, 24 + mid : 32 + mid, :] = edge[c, at, 8:16, cut]
                rows_ref[h, 16 + ny : 16 + ny + AFTER, :] = row_after[c, layer, :, cut]
                even_ref[c, layer, :, cut] = rows_ref[h, pl.ds(0, count, stride=2), :]
                odd_ref[c, layer, :, cut] = rows_ref[h, pl.ds(1, count, stride=2), :]


def lift_first(layers, halo):
    return halo_lift_list(layers[0::2], layers[1::2], *halo)


def halo_stack(pairs, both, even_ref, odd_ref, part_ref, stack_ref):
    count, nz = even_ref.shape[2:]
    half, lanes = count - 16, nz // 2
    kinds = 8 if both else 4
    for n, (i, j) in enumerate(pairs):
        for h in range(2):
            cut = slice(h * lanes, (h + 1) * lanes)
            for parity, ref in enumerate((even_ref, odd_ref)):
                for r in range(0, count, 16):
                    rows = slice(r, r + 16)
                    g = [ref[i, layer, rows, cut] * ref[j, layer, rows, cut] for layer in range(BEFORE + AFTER)]
                    for k, value in enumerate(parts_for_next(g[:BEFORE]) + parts_for_previous(g[BEFORE:])):
                        part_ref[parity, k, rows, :] = value
            for k in range(4):
                e, o = ring_lift(part_ref[0, k], part_ref[1, k])
                at = (kinds * n + k) * half
                stack_ref[at : at + half, cut] = e[8 : 8 + half]
                if both:
                    at += 4 * half
                    stack_ref[at : at + half, cut] = o[8 : 8 + half]


def layer_list(refs, index, rows):
    return [ref[index + (x, rows)] for ref in refs for x in range(ref.shape[len(index)])]


def approx_kernel(*refs):
    low_refs, table_ref = refs[:2], refs[2]
    halo_refs = refs[3:9]
    approx_ref, high_ref, stress_ref = refs[9:12]
    next_ref, prev_ref, next_edge_ref, prev_edge_ref, down_ref, up_ref = refs[12:18]
    rows_ref, even_ref, odd_ref, kept_ref, part_ref, stack_ref, out_ref = refs[18:]
    f = pl.program_id(0)
    half, lanes = low_refs[0].shape[2:]
    mx = approx_ref.shape[1]

    @pl.when(f == 0)
    def _():
        gather_rows(halo_refs, rows_ref, even_ref, odd_ref)

    pairs = [pair_of(f * GROUP + n) for n in range(GROUP)]
    halo_stack(pairs, False, even_ref, odd_ref, part_ref, stack_ref)
    out_ref[...] = dot(stack_ref[...], table_ref[:, :lanes])
    for n in range(GROUP):
        for r in range(0, half, 8):
            rows = slice(r, r + 8)
            halo = [out_ref[(4 * n + k) * half + r : (4 * n + k) * half + r + 8, :] for k in range(4)]
            e, o = lift_first(layer_list(low_refs, (n,), rows), halo)
            e = [t * band_scale(0, 0) for t in e]
            for x in range(mx):
                approx_ref[n, x, rows, :] = e[x]
                high_ref[n, x, rows, :] = o[x] * band_scale(0, 1)
            send_layers(e, n, r, next_ref, prev_ref)
        send_rows(approx_ref, n, down_ref, up_ref)
        for ref, edge_ref in ((next_ref, next_edge_ref), (prev_ref, prev_edge_ref)):
            for part in range(2):
                tail, head = row_parts(lambda row: ref[n, part, row : row + 8, :], half)
                edge_ref[n, part, 0:2, :] = tail
                edge_ref[n, part, 2:4, :] = head

    @pl.when(f == 0)
    def _():
        kept_ref[...] = approx_ref[...]

    @pl.when(f > 0)
    def _():
        for n, (i, j) in enumerate(pairs):
            for x in range(mx):
                stress_ref[n, x] = approx_ref[n, x] - kept_ref[i, x] * kept_ref[j, x]


def whole(shape):
    return pl.BlockSpec(shape, lambda f: (0,) * len(shape))


def per_field(shape):
    return pl.BlockSpec((GROUP,) + shape, lambda f: (f,) + (0,) * len(shape))


def approx_pass(lows, halo, table):
    _, nx, half, lanes = lows[0].shape
    nz, count, mx = 2 * lanes, half + 16, nx
    f32 = lambda *shape: jax.ShapeDtypeStruct(shape, jnp.float32)
    sends = [(2, half, lanes), (2, half, lanes), (2, 4, lanes), (2, 4, lanes), (mx, 2, lanes), (mx, 2, lanes)]
    return pl.pallas_call(
        approx_kernel,
        grid=(9 // GROUP,),
        in_specs=[per_field((nx, half, lanes))] * 2 + [whole((nz, nz))] + [whole(h.shape) for h in halo],
        out_specs=[
            per_field((mx, half, lanes)),
            per_field((mx, half, lanes)),
            pl.BlockSpec((GROUP, mx, half, lanes), lambda f: (jnp.maximum(f - 1, 0), 0, 0, 0)),
        ]
        + [per_field(s) for s in sends],
        out_shape=[f32(9, mx, half, lanes), f32(9, mx, half, lanes), f32(6, mx, half, lanes)] + [f32(9, *s) for s in sends],
        scratch_shapes=halo_scratch(half, lanes)
        + [
            pltpu.VMEM((3, mx, half, lanes), jnp.float32),
            pltpu.VMEM((2, 4, count, lanes), jnp.float32),
            pltpu.VMEM((GROUP * 4 * half, nz), jnp.float32),
            pltpu.VMEM((GROUP * 4 * half, lanes), jnp.float32),
        ],
        compiler_params=pltpu.CompilerParams(vmem_limit_bytes=24 * MIB),
        name="approx_pass",
    )(*lows, table, *halo)


def halo_scratch(half, lanes):
    return [
        pltpu.VMEM((2, 2 * half + 32, lanes), jnp.float32),
        pltpu.VMEM((4, BEFORE + AFTER, half + 16, 2 * lanes), jnp.float32),
        pltpu.VMEM((4, BEFORE + AFTER, half + 16, 2 * lanes), jnp.float32),
    ]


def detail_kernel(*refs):
    rest_refs, high_ref, table_ref = refs[:2], refs[2], refs[3]
    halo_refs = refs[4:10]
    out_ref, rows_ref, even_ref, odd_ref, part_ref, stack_ref = refs[10:]
    f = pl.program_id(0)
    half, lanes = high_ref.shape[2:]
    mx = high_ref.shape[1]

    @pl.when(f == 0)
    def _():
        gather_rows(halo_refs, rows_ref, even_ref, odd_ref)

    pairs = [pair_of(f * GROUP + n) for n in range(GROUP)]
    halo_stack(pairs, True, even_ref, odd_ref, part_ref, stack_ref)
    stack_ref[...] = dot(stack_ref[...], table_ref[...])
    for n in range(GROUP):
        for x in range(mx):
            out_ref[0, n, x] = high_ref[n, x]
        for band, (bz, by) in enumerate(((0, 1), (1, 0), (1, 1))):
            plane = 4 * bz + 2 * by - 1
            for r in range(0, half, 8):
                rows = slice(r, r + 8)
                halo = []
                for k in range(4):
                    at = (8 * n + 4 * by + k) * half + r
                    halo.append(stack_ref[at : at + 8, bz * lanes : (bz + 1) * lanes])
                e, o = lift_first(layer_list(rest_refs, (band, n), rows), halo)
                for x in range(mx):
                    out_ref[plane, n, x, rows, :] = e[x] * band_scale(by, 0)
                    out_ref[plane + 1, n, x, rows, :] = o[x] * band_scale(by, 1)


def detail_pass(rests, high, halo, table):
    _, mx, half, lanes = high.shape
    nz, count = 2 * lanes, half + 16
    return pl.pallas_call(
        detail_kernel,
        grid=(9 // GROUP,),
        in_specs=[pl.BlockSpec((3, GROUP, mx, half, lanes), lambda f: (0, f, 0, 0, 0))] * 2
        + [per_field((mx, half, lanes)), whole((nz, nz))]
        + [whole(h.shape) for h in halo],
        out_specs=pl.BlockSpec((7, GROUP, mx, half, lanes), lambda f: (0, f, 0, 0, 0)),
        out_shape=jax.ShapeDtypeStruct((7, 9, mx, half, lanes), jnp.float32),
        scratch_shapes=halo_scratch(half, lanes)
        + [pltpu.VMEM((2, 4, count, lanes), jnp.float32), pltpu.VMEM((GROUP * 8 * half, nz), jnp.float32)],
        compiler_params=pltpu.CompilerParams(vmem_limit_bytes=24 * MIB),
        cost_estimate=pl.CostEstimate(flops=18 * mx * half * nz * 200, bytes_accessed=18 * mx * half * nz * 16, transcendentals=0),
        name="detail_pass",
    )(*rests, high, table, *halo)


def level_rows(refs, nz, lows, pad_ref, stack_ref):
    a_ref, before_ref, after_ref, down_ref, up_ref = refs
    nx, ny = a_ref.shape[1:3]
    half = ny // 2
    wide = stack_ref.shape[1]
    kept = half if lows else ny
    if nz < wide:
        pad_ref[...] = jnp.zeros_like(pad_ref)
    for f in range(9):
        for layer in range(nx + 4):
            if layer < nx:
                source, at = a_ref, layer
            elif layer < nx + 2:
                source, at = before_ref, layer - nx
            else:
                source, at = after_ref, layer - nx - 2
            if nz < wide:
                pad_ref[f, layer, :, :nz] = source[f, at]
                source, at = pad_ref, layer
            e = source[f, at, pl.ds(0, half, stride=2), :]
            o = source[f, at, pl.ds(1, half, stride=2), :]
            rows = [down_ref[f, layer, 1:2, :], down_ref[f, layer, 0:1, :], up_ref[f, layer, 0:1, :], up_ref[f, layer, 1:2, :]]
            if nz < wide:
                rows = [jnp.concatenate([row, jnp.zeros((1, wide - nz), jnp.float32)], axis=1) for row in rows]
            e, o = sublane_lift(e, o, *rows)
            at = (f * (nx + 4) + layer) * kept
            stack_ref[at : at + half, :] = e
            if not lows:
                stack_ref[at + half : at + ny, :] = o


def level_approx_kernel(nz, *refs):
    table_ref, approx_ref, stress_ref = refs[5:8]
    sends, (pad_ref, stack_ref, out_ref, kept_ref) = refs[8:-4], refs[-4:]
    nx, ny = refs[0].shape[1:3]
    half, lanes = ny // 2, nz // 2
    level_rows(refs[:5], nz, True, pad_ref, stack_ref)
    out_ref[...] = dot(stack_ref[...], table_ref[...])
    mx = nx // 2
    for f in range(9):
        for r in range(0, half, 8):
            rows = slice(r, r + 8)
            layers = []
            for layer in range(nx + 4):
                at = (f * (nx + 4) + layer) * half + r
                layers.append(out_ref[at : at + 8, :])
            low, _ = lift_first(layers[:nx], layers[nx:])
            approx = [(t * band_scale(0, 0))[:, :lanes] for t in low]
            for x in range(mx):
                if f < 3:
                    kept_ref[f, x, rows, :] = approx[x]
                else:
                    i, j = product_pairs[f - 3]
                    stress_ref[f - 3, x, rows, :] = approx[x] - kept_ref[i, x, rows, :] * kept_ref[j, x, rows, :]
                approx_ref[f, x, rows, :] = approx[x]
            send_layers(approx, f, r, sends[0], sends[1])
        send_rows(approx_ref, f, sends[2], sends[3])


def level_detail_kernel(nz, last, *refs):
    table_ref, detail_ref = refs[5:7]
    pad_ref, stack_ref, out_ref, kept_ref = refs[-4:]
    nx, ny = refs[0].shape[1:3]
    half, lanes = ny // 2, nz // 2
    wide = stack_ref.shape[1]
    level_rows(refs[:5], nz, False, pad_ref, stack_ref)
    out_ref[...] = dot(stack_ref[...], table_ref[...])
    for f in range(9):
        for by in range(2):
            for r in range(0, half, 8):
                rows = slice(r, r + 8)
                layers = []
                for layer in range(nx + 4):
                    at = (f * (nx + 4) + layer) * ny + by * half + r
                    layers.append(out_ref[at : at + 8, :])
                low, high = lift_first(layers[:nx], layers[nx:])
                for x in range(nx // 2):
                    for bx, value in enumerate((low[x], high[x])):
                        t = value * band_scale(by, bx)
                        for bz in range(2):
                            band = 4 * bz + 2 * by + bx
                            piece = t[:, bz * (wide // 2) : bz * (wide // 2) + lanes]
                            if band:
                                detail_ref[band - 1, f, x, rows, :] = piece
                            elif last:
                                stress_ref, approx_ref = refs[7:9]
                                if f < 3:
                                    kept_ref[f, x, rows, :] = piece
                                    approx_ref[f, x, rows, :] = piece
                                else:
                                    i, j = product_pairs[f - 3]
                                    stress_ref[f - 3, x, rows, :] = piece - kept_ref[i, x, rows, :] * kept_ref[j, x, rows, :]


def level_call(kernel, approx, halo, out, kept):
    _, nx, ny, nz = approx.shape
    wide = max(nz, 128)
    vmem = pl.BlockSpec(memory_space=pltpu.VMEM)
    return pl.pallas_call(
        kernel,
        in_specs=[vmem] * 6,
        out_specs=[vmem] * len(out),
        out_shape=out,
        scratch_shapes=[
            pltpu.VMEM((9, nx + 4, ny, wide), jnp.float32),
            pltpu.VMEM((9 * (nx + 4) * kept, wide), jnp.float32),
            pltpu.VMEM((9 * (nx + 4) * kept, wide), jnp.float32),
            pltpu.VMEM((3, nx // 2, ny // 2, nz // 2), jnp.float32),
        ],
        compiler_params=pltpu.CompilerParams(vmem_limit_bytes=24 * MIB),
    )(approx, *halo, jnp.asarray(third_table(nz, wide)))


def level_approx(approx, halo):
    _, nx, ny, nz = approx.shape
    mx, half, lanes = nx // 2, ny // 2, nz // 2
    f32 = lambda *shape: jax.ShapeDtypeStruct(shape, jnp.float32)
    sends = ((2, half, lanes), (2, half, lanes), (mx, 2, lanes), (mx, 2, lanes))
    out = [f32(9, mx, half, lanes), f32(6, mx, half, lanes)] + [f32(9, *s) for s in sends]
    return level_call(lambda *refs: level_approx_kernel(nz, *refs), approx, halo, out, half)


def level_details(approx, halo, last):
    _, nx, ny, nz = approx.shape
    mx, half, lanes = nx // 2, ny // 2, nz // 2
    f32 = lambda *shape: jax.ShapeDtypeStruct(shape, jnp.float32)
    out = [f32(7, 9, mx, half, lanes)]
    if last:
        out += [f32(6, mx, half, lanes), f32(3, mx, half, lanes)]
    return level_call(lambda *refs: level_detail_kernel(nz, last, *refs), approx, halo, out, ny)


def halo_rows(before, after, down, up):
    rows = before.shape[2]
    cell = lambda at: jnp.concatenate([before[:, :, at : at + 1], after[:, :, at : at + 1]], axis=1)
    p, q = parts_for_next([cell(rows - 4 + i) for i in range(4)])
    down = jnp.concatenate([down, jnp.concatenate([q, p], axis=2)], axis=1)
    head = jnp.concatenate(parts_for_previous([cell(i) for i in range(3)]), axis=2)
    up = jnp.concatenate([up, head], axis=1)
    return shifted(down, "gy", 1), shifted(up, "gy", -1)


def exchange(to_next, to_prev, edge_next, edge_prev, down, up):
    from_prev_edge = shifted(edge_next, "gx", 1)
    from_next_edge = shifted(edge_prev, "gx", -1)
    before = shifted(to_next, "gx", 1)
    after = shifted(to_prev, "gx", -1)
    down = jnp.concatenate([down, from_prev_edge[:, :, 0:2], from_next_edge[:, :, 0:2]], axis=1)
    up = jnp.concatenate([up, from_prev_edge[:, :, 2:4], from_next_edge[:, :, 2:4]], axis=1)
    return before, after, shifted(down, "gy", 1), shifted(up, "gy", -1)


def body(velocity):
    _, nx, ny, nz = velocity.shape
    table = jnp.asarray(third_table(nz, nz))
    tail, head = velocity[:, nx - BEFORE :], velocity[:, :AFTER]
    edges = lambda t: jnp.concatenate([t[:, :, :8], t[:, :, ny - 8 :]], axis=2)
    edge_before = shifted(edges(tail), "gx", 1)
    edge_after = shifted(edges(head), "gx", -1)
    mid_before = shifted(tail[:, :, 8 : ny - 8], "gx", 1)
    mid_after = shifted(head[:, :, 8 : ny - 8], "gx", -1)
    own_before = shifted(velocity[:, :, ny - BEFORE :], "gy", 1)
    own_after = shifted(velocity[:, :, :AFTER], "gy", -1)
    low_one, rest_one = local_pass(velocity, own_before, own_after, table, 0)
    edge_before, edge_after, low_one = lax.optimization_barrier((edge_before, edge_after, low_one))
    down = jnp.concatenate([edge_before[:, :, 12:], edge_after[:, :, 12:]], axis=1)
    up = jnp.concatenate([edge_before[:, :, :AFTER], edge_after[:, :, :AFTER]], axis=1)
    row_before = shifted(down, "gy", 1)
    row_after = shifted(up, "gy", -1)
    low_two, rest_two = local_pass(velocity, own_before, own_after, table, nx // 2)
    halo = (edge_before, mid_before, edge_after, mid_after, row_before, row_after)
    approx, high, stress_one, *sends = approx_pass((low_one, low_two), halo, table)
    second_halo = exchange(*sends)
    details_one = detail_pass((rest_one, rest_two), high, halo, table)
    approx, details_one = lax.optimization_barrier((approx, details_one))
    second = approx
    approx, stress_two, *sends = level_approx(second, second_halo)
    before = shifted(sends[0], "gx", 1)
    after = shifted(sends[1], "gx", -1)
    (details_two,) = level_details(second, second_halo, False)
    before, after, details_two = lax.optimization_barrier((before, after, details_two))
    third_halo = (before, after) + halo_rows(before, after, *sends[2:])
    details_three, stress_three, coarse = level_details(approx, third_halo, True)
    return details_one, stress_one, details_two, stress_two, details_three, stress_three, coarse


def solution(mesh):
    in_specs = (P(None, "gx", "gy", None),)
    out_specs = (
        P(None, None, "gx", "gy", None),
        P(None, "gx", "gy", None),
        P(None, None, "gx", "gy", None),
        P(None, "gx", "gy", None),
        P(None, None, "gx", "gy", None),
        P(None, "gx", "gy", None),
        P(None, "gx", "gy", None),
    )
    return jax.shard_map(body, mesh=mesh, in_specs=in_specs, out_specs=out_specs, check_vma=False)
```

```python
import jax
import jax.numpy as jnp
import numpy as np
from jax import lax
from jax.experimental import pallas as pl
from jax.experimental.pallas import tpu as pltpu
from jax.sharding import PartitionSpec as P

predict_one = -1.586134342
update_one = -0.05298011854
predict_two = 0.8829110762
update_two = 0.4435068522
scaling = 1.149604398
product_pairs = ((0, 0), (0, 1), (0, 2), (1, 1), (1, 2), (2, 2))
BEFORE = 4
AFTER = 3
GROUP = 3
MIB = 1 << 20


def shifted(block, axis, distance):
    size = lax.axis_size(axis)
    return lax.ppermute(block, axis, [(i, (i + distance) % size) for i in range(size)])


def swapped(block, axis, odd):
    size = lax.axis_size(axis)
    route = []
    for i in range(size):
        route.append((i, (i + 1) % size if i % 2 == odd else (i - 1) % size))
    return lax.ppermute(block, axis, route)


def neighbours(to_next, to_prev, axis):
    even = lax.axis_index(axis) % 2 == 0
    near = swapped(jnp.where(even, to_next, to_prev), axis, 0)
    far = swapped(jnp.where(even, to_prev, to_next), axis, 1)
    return jnp.where(even, far, near), jnp.where(even, near, far)


def third_table(length, lanes):
    eye = np.eye(length)
    e, o = eye[:, 0::2], eye[:, 1::2]
    following = lambda t: np.concatenate([t[:, 1:], t[:, -1:]], 1)
    preceding = lambda t: np.concatenate([t[:, :1], t[:, :-1]], 1)
    o = o + predict_one * (e + following(e))
    e = e + update_one * (o + preceding(o))
    o = o + predict_two * (e + following(e))
    e = e + update_two * (o + preceding(o))
    table = np.zeros((lanes, lanes))
    table[:length, : length // 2] = e * scaling
    table[:length, lanes // 2 : lanes // 2 + length // 2] = o / scaling
    return table.astype(np.float32)


def band_scale(by, bx):
    return float(scaling ** ((1 - 2 * by) + (1 - 2 * bx)))


def dot(a, b):
    a_high, b_high = a.astype(jnp.bfloat16), b.astype(jnp.bfloat16)
    a_low = (a - a_high.astype(jnp.float32)).astype(jnp.bfloat16)
    b_low = (b - b_high.astype(jnp.float32)).astype(jnp.bfloat16)
    part = lambda x, y: jnp.dot(x, y, preferred_element_type=jnp.float32)
    return part(a_high, b_high) + (part(a_high, b_low) + part(a_low, b_high))


def ring_lift(e, o):
    n = e.shape[0]
    up = lambda t: pltpu.roll(t, n - 1, 0)
    down = lambda t: pltpu.roll(t, 1, 0)
    o = o + predict_one * (e + up(e))
    e = e + update_one * (o + down(o))
    o = o + predict_two * (e + up(e))
    e = e + update_two * (o + down(o))
    return e, o


def halo_lift(e, o, p, q, r, s, following, preceding, first, last):
    o1 = o + predict_one * (e + following(e, r))
    o1_before = p + predict_one * first(e)
    e1 = e + update_one * (preceding(o1, o1_before) + o1)
    e1_before = q + update_one * o1_before
    e1_after = r + update_one * (last(o1) + s)
    o2 = o1 + predict_two * (e1 + following(e1, e1_after))
    o2_before = o1_before + predict_two * (e1_before + first(e1))
    e2 = e1 + update_two * (preceding(o2, o2_before) + o2)
    return e2, o2


def halo_lift_list(e, o, p, q, r, s):
    m = len(e)
    e = list(e) + [r]
    o1 = [p + predict_one * e[0]]
    o1 += [o[i] + predict_one * (e[i] + e[i + 1]) for i in range(m)] + [s]
    e1 = [q + update_one * o1[0]]
    e1 += [e[i] + update_one * (o1[i] + o1[i + 1]) for i in range(m + 1)]
    o2 = [o1[i] + predict_two * (e1[i] + e1[i + 1]) for i in range(m + 1)]
    e2 = [e1[i + 1] + update_two * (o2[i] + o2[i + 1]) for i in range(m)]
    return e2, o2[1:]


def sublane_lift(e, o, p, q, r, s):
    n = e.shape[0]
    row = lax.broadcasted_iota(jnp.int32, e.shape, 0)
    following = lambda t, edge: jnp.where(row == n - 1, edge, pltpu.roll(t, n - 1, 0))
    preceding = lambda t, edge: jnp.where(row == 0, edge, pltpu.roll(t, 1, 0))
    return halo_lift(e, o, p, q, r, s, following, preceding, lambda t: t[0:1], lambda t: t[n - 1 : n])


def parts_for_next(c):
    p = c[-1] + predict_one * c[-2]
    q = c[-2] + update_one * (c[-3] + predict_one * (c[-4] + c[-2]))
    return p, q


def parts_for_previous(c):
    return c[0], c[1] + predict_one * (c[0] + c[2])


def row_parts(load, rows):
    tail, head = load(rows - 8), load(0)
    row = lax.broadcasted_iota(jnp.int32, tail.shape, 0)
    inner = tail + predict_one * (pltpu.roll(tail, 1, 0) + pltpu.roll(tail, 7, 0))
    p = tail + predict_one * pltpu.roll(tail, 1, 0)
    q = tail + update_one * pltpu.roll(inner, 1, 0)
    s = head + predict_one * (pltpu.roll(head, 1, 0) + pltpu.roll(head, 7, 0))
    return jnp.where(row == 7, p, q)[6:8], jnp.where(row == 0, head, s)[0:2]


def send_layers(layers, f, at, next_ref, prev_ref):
    for part, value in enumerate(parts_for_next(layers)):
        next_ref[f, part, at : at + 8, :] = value
    for part, value in enumerate(parts_for_previous(layers)):
        prev_ref[f, part, at : at + 8, :] = value


def send_rows(ref, f, down_ref, up_ref):
    for at in range(ref.shape[1]):
        tail, head = row_parts(lambda row: ref[f, at, row : row + 8, :], ref.shape[2])
        down_ref[f, at] = tail
        up_ref[f, at] = head


def local_kernel(v_ref, before_ref, after_ref, table_ref, low_ref, rest_ref, rows_ref, stack_ref):
    ny = v_ref.shape[2]
    half = ny // 2
    lanes = v_ref.shape[3] // 2
    even, odd = [], []
    for c in range(3):
        for h in range(2):
            cut = pl.ds(h * lanes, lanes)
            rows_ref[c, h, 12:16, :] = before_ref[c, 0, :, cut]
            rows_ref[c, h, 16 : 16 + ny, :] = v_ref[c, 0, :, cut]
            rows_ref[c, h, 16 + ny : 16 + ny + AFTER, :] = after_ref[c, 0, :, cut]
    count = half + 16
    for h in range(2):
        even = [rows_ref[c, h, pl.ds(0, count, stride=2), :] for c in range(3)]
        odd = [rows_ref[c, h, pl.ds(1, count, stride=2), :] for c in range(3)]
        for f in range(9):
            if f < 3:
                e, o = even[f], odd[f]
            else:
                i, j = product_pairs[f - 3]
                e, o = even[i] * even[j], odd[i] * odd[j]
            e, o = ring_lift(e, o)
            stack_ref[f * ny : f * ny + half, h * lanes : (h + 1) * lanes] = e[8 : 8 + half]
            stack_ref[f * ny + half : (f + 1) * ny, h * lanes : (h + 1) * lanes] = o[8 : 8 + half]
    out = dot(stack_ref[...], table_ref[...])
    for f in range(9):
        low_ref[f, 0] = out[f * ny : f * ny + half, :lanes]
        rest_ref[0, f, 0] = out[f * ny + half : (f + 1) * ny, :lanes]
        rest_ref[1, f, 0] = out[f * ny : f * ny + half, lanes:]
        rest_ref[2, f, 0] = out[f * ny + half : (f + 1) * ny, lanes:]


def local_pass(velocity, before, after, table, start):
    _, nx, ny, nz = velocity.shape
    nx = nx // 2
    half, lanes = ny // 2, nz // 2
    return pl.pallas_call(
        local_kernel,
        grid=(nx,),
        in_specs=[
            pl.BlockSpec((3, 1, ny, nz), lambda i: (0, i + start, 0, 0)),
            pl.BlockSpec((3, 1, BEFORE, nz), lambda i: (0, i + start, 0, 0)),
            pl.BlockSpec((3, 1, AFTER, nz), lambda i: (0, i + start, 0, 0)),
            pl.BlockSpec((nz, nz), lambda i: (0, 0)),
        ],
        out_specs=[
            pl.BlockSpec((9, 1, half, lanes), lambda i: (0, i, 0, 0)),
            pl.BlockSpec((3, 9, 1, half, lanes), lambda i: (0, 0, i, 0, 0)),
        ],
        out_shape=[
            jax.ShapeDtypeStruct((9, nx, half, lanes), jnp.float32),
            jax.ShapeDtypeStruct((3, 9, nx, half, lanes), jnp.float32),
        ],
        scratch_shapes=[pltpu.VMEM((3, 2, ny + 32, lanes), jnp.float32), pltpu.VMEM((9 * ny, nz), jnp.float32)],
        compiler_params=pltpu.CompilerParams(vmem_limit_bytes=24 * MIB),
        cost_estimate=pl.CostEstimate(flops=9 * nx * ny * nz * 512, bytes_accessed=9 * nx * ny * nz * 6, transcendentals=0),
        name="local_pass",
    )(velocity, before, after, table)


def pair_of(f):
    k = f - 3
    one = jnp.where(k < 3, 0, jnp.where(k < 5, 1, 2))
    two = jnp.where(k < 3, k, jnp.where(k < 5, k - 2, 2))
    return jnp.where(f < 3, f, one), jnp.where(f < 3, 3, two)


def gather_rows(refs, rows_ref, even_ref, odd_ref):
    edge_before, mid_before, edge_after, mid_after, row_before, row_after = refs
    mid = mid_before.shape[2]
    ny = mid + 16
    lanes = rows_ref.shape[2]
    count = ny // 2 + 16
    even_ref[3] = jnp.ones(even_ref.shape[1:], jnp.float32)
    odd_ref[3] = jnp.ones(odd_ref.shape[1:], jnp.float32)
    for c in range(3):
        for layer in range(BEFORE + AFTER):
            if layer < BEFORE:
                edge, middle, at = edge_before, mid_before, layer
            else:
                edge, middle, at = edge_after, mid_after, layer - BEFORE
            for h in range(2):
                cut = pl.ds(h * lanes, lanes)
                rows_ref[h, 12:16, :] = row_before[c, layer, :, cut]
                rows_ref[h, 16:24, :] = edge[c, at, 0:8, cut]
                rows_ref[h, 24 : 24 + mid, :] = middle[c, at, :, cut]
                rows_ref[h, 24 + mid : 32 + mid, :] = edge[c, at, 8:16, cut]
                rows_ref[h, 16 + ny : 16 + ny + AFTER, :] = row_after[c, layer, :, cut]
                even_ref[c, layer, :, cut] = rows_ref[h, pl.ds(0, count, stride=2), :]
                odd_ref[c, layer, :, cut] = rows_ref[h, pl.ds(1, count, stride=2), :]


def lift_first(layers, halo):
    return halo_lift_list(layers[0::2], layers[1::2], *halo)


def halo_stack(pairs, both, even_ref, odd_ref, part_ref, stack_ref):
    count, nz = even_ref.shape[2:]
    half, lanes = count - 16, nz // 2
    kinds = 8 if both else 4
    for n, (i, j) in enumerate(pairs):
        for h in range(2):
            cut = slice(h * lanes, (h + 1) * lanes)
            for parity, ref in enumerate((even_ref, odd_ref)):
                for r in range(0, count, 16):
                    rows = slice(r, r + 16)
                    g = [ref[i, layer, rows, cut] * ref[j, layer, rows, cut] for layer in range(BEFORE + AFTER)]
                    for k, value in enumerate(parts_for_next(g[:BEFORE]) + parts_for_previous(g[BEFORE:])):
                        part_ref[parity, k, rows, :] = value
            for k in range(4):
                e, o = ring_lift(part_ref[0, k], part_ref[1, k])
                at = (kinds * n + k) * half
                stack_ref[at : at + half, cut] = e[8 : 8 + half]
                if both:
                    at += 4 * half
                    stack_ref[at : at + half, cut] = o[8 : 8 + half]


def layer_list(refs, index, rows):
    return [ref[index + (x, rows)] for ref in refs for x in range(ref.shape[len(index)])]


def approx_kernel(*refs):
    low_refs, table_ref = refs[:2], refs[2]
    halo_refs = refs[3:9]
    approx_ref, high_ref, stress_ref = refs[9:12]
    next_ref, prev_ref, next_edge_ref, prev_edge_ref, down_ref, up_ref = refs[12:18]
    rows_ref, even_ref, odd_ref, kept_ref, part_ref, stack_ref, out_ref = refs[18:]
    f = pl.program_id(0)
    half, lanes = low_refs[0].shape[2:]
    mx = approx_ref.shape[1]

    @pl.when(f == 0)
    def _():
        gather_rows(halo_refs, rows_ref, even_ref, odd_ref)

    pairs = [pair_of(f * GROUP + n) for n in range(GROUP)]
    halo_stack(pairs, False, even_ref, odd_ref, part_ref, stack_ref)
    out_ref[...] = dot(stack_ref[...], table_ref[:, :lanes])
    for n in range(GROUP):
        for r in range(0, half, 8):
            rows = slice(r, r + 8)
            halo = [out_ref[(4 * n + k) * half + r : (4 * n + k) * half + r + 8, :] for k in range(4)]
            e, o = lift_first(layer_list(low_refs, (n,), rows), halo)
            e = [t * band_scale(0, 0) for t in e]
            for x in range(mx):
                approx_ref[n, x, rows, :] = e[x]
                high_ref[n, x, rows, :] = o[x] * band_scale(0, 1)
            send_layers(e, n, r, next_ref, prev_ref)
        send_rows(approx_ref, n, down_ref, up_ref)
        for ref, edge_ref in ((next_ref, next_edge_ref), (prev_ref, prev_edge_ref)):
            for part in range(2):
                tail, head = row_parts(lambda row: ref[n, part, row : row + 8, :], half)
                edge_ref[n, part, 0:2, :] = tail
                edge_ref[n, part, 2:4, :] = head

    @pl.when(f == 0)
    def _():
        kept_ref[...] = approx_ref[...]

    @pl.when(f > 0)
    def _():
        for n, (i, j) in enumerate(pairs):
            for x in range(mx):
                stress_ref[n, x] = approx_ref[n, x] - kept_ref[i, x] * kept_ref[j, x]


def whole(shape):
    return pl.BlockSpec(shape, lambda f: (0,) * len(shape))


def per_field(shape):
    return pl.BlockSpec((GROUP,) + shape, lambda f: (f,) + (0,) * len(shape))


def approx_pass(lows, halo, table):
    _, nx, half, lanes = lows[0].shape
    nz, count, mx = 2 * lanes, half + 16, nx
    f32 = lambda *shape: jax.ShapeDtypeStruct(shape, jnp.float32)
    sends = [(2, half, lanes), (2, half, lanes), (2, 4, lanes), (2, 4, lanes), (mx, 2, lanes), (mx, 2, lanes)]
    return pl.pallas_call(
        approx_kernel,
        grid=(9 // GROUP,),
        in_specs=[per_field((nx, half, lanes))] * 2 + [whole((nz, nz))] + [whole(h.shape) for h in halo],
        out_specs=[
            per_field((mx, half, lanes)),
            per_field((mx, half, lanes)),
            pl.BlockSpec((GROUP, mx, half, lanes), lambda f: (jnp.maximum(f - 1, 0), 0, 0, 0)),
        ]
        + [per_field(s) for s in sends],
        out_shape=[f32(9, mx, half, lanes), f32(9, mx, half, lanes), f32(6, mx, half, lanes)] + [f32(9, *s) for s in sends],
        scratch_shapes=halo_scratch(half, lanes)
        + [
            pltpu.VMEM((3, mx, half, lanes), jnp.float32),
            pltpu.VMEM((2, 4, count, lanes), jnp.float32),
            pltpu.VMEM((GROUP * 4 * half, nz), jnp.float32),
            pltpu.VMEM((GROUP * 4 * half, lanes), jnp.float32),
        ],
        compiler_params=pltpu.CompilerParams(vmem_limit_bytes=24 * MIB),
        name="approx_pass",
    )(*lows, table, *halo)


def halo_scratch(half, lanes):
    return [
        pltpu.VMEM((2, 2 * half + 32, lanes), jnp.float32),
        pltpu.VMEM((4, BEFORE + AFTER, half + 16, 2 * lanes), jnp.float32),
        pltpu.VMEM((4, BEFORE + AFTER, half + 16, 2 * lanes), jnp.float32),
    ]


def detail_kernel(*refs):
    rest_refs, high_ref, table_ref = refs[:2], refs[2], refs[3]
    halo_refs = refs[4:10]
    out_ref, rows_ref, even_ref, odd_ref, part_ref, stack_ref = refs[10:]
    f = pl.program_id(0)
    half, lanes = high_ref.shape[2:]
    mx = high_ref.shape[1]

    @pl.when(f == 0)
    def _():
        gather_rows(halo_refs, rows_ref, even_ref, odd_ref)

    pairs = [pair_of(f * GROUP + n) for n in range(GROUP)]
    halo_stack(pairs, True, even_ref, odd_ref, part_ref, stack_ref)
    stack_ref[...] = dot(stack_ref[...], table_ref[...])
    for n in range(GROUP):
        for x in range(mx):
            out_ref[0, n, x] = high_ref[n, x]
        for band, (bz, by) in enumerate(((0, 1), (1, 0), (1, 1))):
            plane = 4 * bz + 2 * by - 1
            for r in range(0, half, 8):
                rows = slice(r, r + 8)
                halo = []
                for k in range(4):
                    at = (8 * n + 4 * by + k) * half + r
                    halo.append(stack_ref[at : at + 8, bz * lanes : (bz + 1) * lanes])
                e, o = lift_first(layer_list(rest_refs, (band, n), rows), halo)
                for x in range(mx):
                    out_ref[plane, n, x, rows, :] = e[x] * band_scale(by, 0)
                    out_ref[plane + 1, n, x, rows, :] = o[x] * band_scale(by, 1)


def detail_pass(rests, high, halo, table):
    _, mx, half, lanes = high.shape
    nz, count = 2 * lanes, half + 16
    return pl.pallas_call(
        detail_kernel,
        grid=(9 // GROUP,),
        in_specs=[pl.BlockSpec((3, GROUP, mx, half, lanes), lambda f: (0, f, 0, 0, 0))] * 2
        + [per_field((mx, half, lanes)), whole((nz, nz))]
        + [whole(h.shape) for h in halo],
        out_specs=pl.BlockSpec((7, GROUP, mx, half, lanes), lambda f: (0, f, 0, 0, 0)),
        out_shape=jax.ShapeDtypeStruct((7, 9, mx, half, lanes), jnp.float32),
        scratch_shapes=halo_scratch(half, lanes)
        + [pltpu.VMEM((2, 4, count, lanes), jnp.float32), pltpu.VMEM((GROUP * 8 * half, nz), jnp.float32)],
        compiler_params=pltpu.CompilerParams(vmem_limit_bytes=24 * MIB),
        cost_estimate=pl.CostEstimate(flops=18 * mx * half * nz * 200, bytes_accessed=18 * mx * half * nz * 16, transcendentals=0),
        name="detail_pass",
    )(*rests, high, table, *halo)


def level_rows(refs, nz, lows, pad_ref, stack_ref):
    a_ref, before_ref, after_ref, down_ref, up_ref = refs
    nx, ny = a_ref.shape[1:3]
    half = ny // 2
    wide = stack_ref.shape[1]
    kept = half if lows else ny
    if nz < wide:
        pad_ref[...] = jnp.zeros_like(pad_ref)
    for f in range(9):
        for layer in range(nx + 4):
            if layer < nx:
                source, at = a_ref, layer
            elif layer < nx + 2:
                source, at = before_ref, layer - nx
            else:
                source, at = after_ref, layer - nx - 2
            if nz < wide:
                if layer < nx:
                    pad_ref[f, layer, :, :nz] = source[f, at]
                else:
                    pad_ref[f, layer, :, :nz] = source[f, :, at * nz : (at + 1) * nz]
                source, at = pad_ref, layer
            e = source[f, at, pl.ds(0, half, stride=2), :]
            o = source[f, at, pl.ds(1, half, stride=2), :]
            rows = [down_ref[f, layer, 1:2, :], down_ref[f, layer, 0:1, :], up_ref[f, layer, 0:1, :], up_ref[f, layer, 1:2, :]]
            if nz < wide:
                rows = [jnp.concatenate([row, jnp.zeros((1, wide - nz), jnp.float32)], axis=1) for row in rows]
            e, o = sublane_lift(e, o, *rows)
            at = (f * (nx + 4) + layer) * kept
            stack_ref[at : at + half, :] = e
            if not lows:
                stack_ref[at + half : at + ny, :] = o


def level_approx_kernel(nz, *refs):
    table_ref, approx_ref, stress_ref = refs[5:8]
    sends, (pad_ref, stack_ref, out_ref, kept_ref) = refs[8:-4], refs[-4:]
    nx, ny = refs[0].shape[1:3]
    half, lanes = ny // 2, nz // 2
    level_rows(refs[:5], nz, True, pad_ref, stack_ref)
    out_ref[...] = dot(stack_ref[...], table_ref[...])
    mx = nx // 2
    for f in range(9):
        for r in range(0, half, 8):
            rows = slice(r, r + 8)
            layers = []
            for layer in range(nx + 4):
                at = (f * (nx + 4) + layer) * half + r
                layers.append(out_ref[at : at + 8, :])
            low, _ = lift_first(layers[:nx], layers[nx:])
            approx = [(t * band_scale(0, 0))[:, :lanes] for t in low]
            for x in range(mx):
                if f < 3:
                    kept_ref[f, x, rows, :] = approx[x]
                else:
                    i, j = product_pairs[f - 3]
                    stress_ref[f - 3, x, rows, :] = approx[x] - kept_ref[i, x, rows, :] * kept_ref[j, x, rows, :]
                approx_ref[f, x, rows, :] = approx[x]
            for ref, parts in zip(sends, (parts_for_next(approx), parts_for_previous(approx))):
                for part, value in enumerate(parts):
                    ref[f, rows, part * lanes : (part + 1) * lanes] = value
        send_rows(approx_ref, f, sends[2], sends[3])


def level_detail_kernel(nz, last, *refs):
    table_ref, detail_ref = refs[5:7]
    pad_ref, stack_ref, out_ref, kept_ref = refs[-4:]
    nx, ny = refs[0].shape[1:3]
    half, lanes = ny // 2, nz // 2
    wide = stack_ref.shape[1]
    level_rows(refs[:5], nz, False, pad_ref, stack_ref)
    out_ref[...] = dot(stack_ref[...], table_ref[...])
    for f in range(9):
        for by in range(2):
            for r in range(0, half, 8):
                rows = slice(r, r + 8)
                layers = []
                for layer in range(nx + 4):
                    at = (f * (nx + 4) + layer) * ny + by * half + r
                    layers.append(out_ref[at : at + 8, :])
                low, high = lift_first(layers[:nx], layers[nx:])
                for x in range(nx // 2):
                    for bx, value in enumerate((low[x], high[x])):
                        t = value * band_scale(by, bx)
                        for bz in range(2):
                            band = 4 * bz + 2 * by + bx
                            piece = t[:, bz * (wide // 2) : bz * (wide // 2) + lanes]
                            if band:
                                detail_ref[band - 1, f, x, rows, :] = piece
                            elif last:
                                stress_ref, approx_ref = refs[7:9]
                                if f < 3:
                                    kept_ref[f, x, rows, :] = piece
                                    approx_ref[f, x, rows, :] = piece
                                else:
                                    i, j = product_pairs[f - 3]
                                    stress_ref[f - 3, x, rows, :] = piece - kept_ref[i, x, rows, :] * kept_ref[j, x, rows, :]


def level_call(kernel, approx, halo, out, kept):
    _, nx, ny, nz = approx.shape
    wide = max(nz, 128)
    vmem = pl.BlockSpec(memory_space=pltpu.VMEM)
    return pl.pallas_call(
        kernel,
        in_specs=[vmem] * 6,
        out_specs=[vmem] * len(out),
        out_shape=out,
        scratch_shapes=[
            pltpu.VMEM((9, nx + 4, ny, wide), jnp.float32),
            pltpu.VMEM((9 * (nx + 4) * kept, wide), jnp.float32),
            pltpu.VMEM((9 * (nx + 4) * kept, wide), jnp.float32),
            pltpu.VMEM((3, nx // 2, ny // 2, nz // 2), jnp.float32),
        ],
        compiler_params=pltpu.CompilerParams(vmem_limit_bytes=24 * MIB),
    )(approx, *halo, jnp.asarray(third_table(nz, wide)))


def level_approx(approx, halo):
    _, nx, ny, nz = approx.shape
    mx, half, lanes = nx // 2, ny // 2, nz // 2
    f32 = lambda *shape: jax.ShapeDtypeStruct(shape, jnp.float32)
    sends = ((half, 2 * lanes), (half, 2 * lanes), (mx, 2, lanes), (mx, 2, lanes))
    out = [f32(9, mx, half, lanes), f32(6, mx, half, lanes)] + [f32(9, *s) for s in sends]
    return level_call(lambda *refs: level_approx_kernel(nz, *refs), approx, halo, out, half)


def level_details(approx, halo, last):
    _, nx, ny, nz = approx.shape
    mx, half, lanes = nx // 2, ny // 2, nz // 2
    f32 = lambda *shape: jax.ShapeDtypeStruct(shape, jnp.float32)
    out = [f32(7, 9, mx, half, lanes)]
    if last:
        out += [f32(6, mx, half, lanes), f32(3, mx, half, lanes)]
    return level_call(lambda *refs: level_detail_kernel(nz, last, *refs), approx, halo, out, ny)


def halo_rows(before, after, down, up):
    rows, lanes = before.shape[1], down.shape[3]

    def cell(at):
        both = [t[:, at].reshape(9, 2, 1, lanes) for t in (before, after)]
        return jnp.concatenate(both, axis=1)

    p, q = parts_for_next([cell(rows - 4 + i) for i in range(4)])
    down = jnp.concatenate([down, jnp.concatenate([q, p], axis=2)], axis=1)
    head = jnp.concatenate(parts_for_previous([cell(i) for i in range(3)]), axis=2)
    up = jnp.concatenate([up, head], axis=1)
    return neighbours(down, up, "gy")


def exchange(to_next, to_prev, edge_next, edge_prev, down, up):
    before = shifted(to_next, "gx", 1)
    after = shifted(to_prev, "gx", -1)
    from_prev, from_next = neighbours(edge_next, edge_prev, "gx")
    down = jnp.concatenate([down, from_prev[:, :, 0:2], from_next[:, :, 0:2]], axis=1)
    up = jnp.concatenate([up, from_prev[:, :, 2:4], from_next[:, :, 2:4]], axis=1)
    return (before, after) + neighbours(down, up, "gy")


def body(velocity):
    _, nx, ny, nz = velocity.shape
    table = jnp.asarray(third_table(nz, nz))
    tail, head = velocity[:, nx - BEFORE :], velocity[:, :AFTER]
    edges = lambda t: jnp.concatenate([t[:, :, :8], t[:, :, ny - 8 :]], axis=2)
    edge_before = shifted(edges(tail), "gx", 1)
    edge_after = shifted(edges(head), "gx", -1)
    mid_before = shifted(tail[:, :, 8 : ny - 8], "gx", 1)
    mid_after = shifted(head[:, :, 8 : ny - 8], "gx", -1)
    own_before = shifted(velocity[:, :, ny - BEFORE :], "gy", 1)
    own_after = shifted(velocity[:, :, :AFTER], "gy", -1)
    low_one, rest_one = local_pass(velocity, own_before, own_after, table, 0)
    edge_before, edge_after, low_one = lax.optimization_barrier((edge_before, edge_after, low_one))
    down = jnp.concatenate([edge_before[:, :, 12:], edge_after[:, :, 12:]], axis=1)
    up = jnp.concatenate([edge_before[:, :, :AFTER], edge_after[:, :, :AFTER]], axis=1)
    row_before = shifted(down, "gy", 1)
    row_after = shifted(up, "gy", -1)
    low_two, rest_two = local_pass(velocity, own_before, own_after, table, nx // 2)
    halo = (edge_before, mid_before, edge_after, mid_after, row_before, row_after)
    approx, high, stress_one, *sends = approx_pass((low_one, low_two), halo, table)
    second_halo = exchange(*sends)
    details_one = detail_pass((rest_one, rest_two), high, halo, table)
    approx, details_one = lax.optimization_barrier((approx, details_one))
    second = approx
    approx, stress_two, *sends = level_approx(second, second_halo)
    before, after = neighbours(sends[0], sends[1], "gx")
    (details_two,) = level_details(second, second_halo, False)
    before, after, details_two = lax.optimization_barrier((before, after, details_two))
    third_halo = (before, after) + halo_rows(before, after, *sends[2:])
    details_three, stress_three, coarse = level_details(approx, third_halo, True)
    return details_one, stress_one, details_two, stress_two, details_three, stress_three, coarse


def solution(mesh):
    in_specs = (P(None, "gx", "gy", None),)
    out_specs = (
        P(None, None, "gx", "gy", None),
        P(None, "gx", "gy", None),
        P(None, None, "gx", "gy", None),
        P(None, "gx", "gy", None),
        P(None, None, "gx", "gy", None),
        P(None, "gx", "gy", None),
        P(None, "gx", "gy", None),
    )
    return jax.shard_map(body, mesh=mesh, in_specs=in_specs, out_specs=out_specs, check_vma=False)
```

```python
import jax
import jax.numpy as jnp
import numpy as np
from jax import lax
from jax.experimental import pallas as pl
from jax.experimental.pallas import tpu as pltpu
from jax.sharding import PartitionSpec as P

predict_one = -1.586134342
update_one = -0.05298011854
predict_two = 0.8829110762
update_two = 0.4435068522
scaling = 1.149604398
product_pairs = ((0, 0), (0, 1), (0, 2), (1, 1), (1, 2), (2, 2))
BEFORE = 4
AFTER = 3
GROUP = 3
MIB = 1 << 20


def shifted(block, axis, distance):
    size = lax.axis_size(axis)
    return lax.ppermute(block, axis, [(i, (i + distance) % size) for i in range(size)])


def third_table(length, lanes):
    eye = np.eye(length)
    e, o = eye[:, 0::2], eye[:, 1::2]
    following = lambda t: np.concatenate([t[:, 1:], t[:, -1:]], 1)
    preceding = lambda t: np.concatenate([t[:, :1], t[:, :-1]], 1)
    o = o + predict_one * (e + following(e))
    e = e + update_one * (o + preceding(o))
    o = o + predict_two * (e + following(e))
    e = e + update_two * (o + preceding(o))
    table = np.zeros((lanes, lanes))
    table[:length, : length // 2] = e * scaling
    table[:length, lanes // 2 : lanes // 2 + length // 2] = o / scaling
    return table.astype(np.float32)


def band_scale(by, bx):
    return float(scaling ** ((1 - 2 * by) + (1 - 2 * bx)))


def dot(a, b):
    a_high, b_high = a.astype(jnp.bfloat16), b.astype(jnp.bfloat16)
    a_low = (a - a_high.astype(jnp.float32)).astype(jnp.bfloat16)
    b_low = (b - b_high.astype(jnp.float32)).astype(jnp.bfloat16)
    part = lambda x, y: jnp.dot(x, y, preferred_element_type=jnp.float32)
    return part(a_high, b_high) + (part(a_high, b_low) + part(a_low, b_high))


def ring_lift(e, o):
    n = e.shape[0]
    up = lambda t: pltpu.roll(t, n - 1, 0)
    down = lambda t: pltpu.roll(t, 1, 0)
    o = o + predict_one * (e + up(e))
    e = e + update_one * (o + down(o))
    o = o + predict_two * (e + up(e))
    e = e + update_two * (o + down(o))
    return e, o


def halo_lift(e, o, p, q, r, s, following, preceding, first, last):
    o1 = o + predict_one * (e + following(e, r))
    o1_before = p + predict_one * first(e)
    e1 = e + update_one * (preceding(o1, o1_before) + o1)
    e1_before = q + update_one * o1_before
    e1_after = r + update_one * (last(o1) + s)
    o2 = o1 + predict_two * (e1 + following(e1, e1_after))
    o2_before = o1_before + predict_two * (e1_before + first(e1))
    e2 = e1 + update_two * (preceding(o2, o2_before) + o2)
    return e2, o2


def halo_lift_list(e, o, p, q, r, s):
    m = len(e)
    e = list(e) + [r]
    o1 = [p + predict_one * e[0]]
    o1 += [o[i] + predict_one * (e[i] + e[i + 1]) for i in range(m)] + [s]
    e1 = [q + update_one * o1[0]]
    e1 += [e[i] + update_one * (o1[i] + o1[i + 1]) for i in range(m + 1)]
    o2 = [o1[i] + predict_two * (e1[i] + e1[i + 1]) for i in range(m + 1)]
    e2 = [e1[i + 1] + update_two * (o2[i] + o2[i + 1]) for i in range(m)]
    return e2, o2[1:]


def sublane_lift(e, o, p, q, r, s):
    n = e.shape[0]
    row = lax.broadcasted_iota(jnp.int32, e.shape, 0)
    following = lambda t, edge: jnp.where(row == n - 1, edge, pltpu.roll(t, n - 1, 0))
    preceding = lambda t, edge: jnp.where(row == 0, edge, pltpu.roll(t, 1, 0))
    return halo_lift(e, o, p, q, r, s, following, preceding, lambda t: t[0:1], lambda t: t[n - 1 : n])


def parts_for_next(c):
    p = c[-1] + predict_one * c[-2]
    q = c[-2] + update_one * (c[-3] + predict_one * (c[-4] + c[-2]))
    return p, q


def parts_for_previous(c):
    return c[0], c[1] + predict_one * (c[0] + c[2])


def row_parts(load, rows):
    tail, head = load(rows - 8), load(0)
    row = lax.broadcasted_iota(jnp.int32, tail.shape, 0)
    inner = tail + predict_one * (pltpu.roll(tail, 1, 0) + pltpu.roll(tail, 7, 0))
    p = tail + predict_one * pltpu.roll(tail, 1, 0)
    q = tail + update_one * pltpu.roll(inner, 1, 0)
    s = head + predict_one * (pltpu.roll(head, 1, 0) + pltpu.roll(head, 7, 0))
    return jnp.where(row == 7, p, q)[6:8], jnp.where(row == 0, head, s)[0:2]


def send_layers(layers, f, at, next_ref, prev_ref):
    for part, value in enumerate(parts_for_next(layers)):
        next_ref[f, part, at : at + 8, :] = value
    for part, value in enumerate(parts_for_previous(layers)):
        prev_ref[f, part, at : at + 8, :] = value


def send_rows(ref, f, down_ref, up_ref):
    for at in range(ref.shape[1]):
        tail, head = row_parts(lambda row: ref[f, at, row : row + 8, :], ref.shape[2])
        down_ref[f, at] = tail
        up_ref[f, at] = head


def local_kernel(v_ref, before_ref, after_ref, table_ref, low_ref, rest_ref, rows_ref, stack_ref):
    ny = v_ref.shape[2]
    half = ny // 2
    lanes = v_ref.shape[3] // 2
    even, odd = [], []
    for c in range(3):
        for h in range(2):
            cut = pl.ds(h * lanes, lanes)
            rows_ref[c, h, 12:16, :] = before_ref[c, 0, :, cut]
            rows_ref[c, h, 16 : 16 + ny, :] = v_ref[c, 0, :, cut]
            rows_ref[c, h, 16 + ny : 16 + ny + AFTER, :] = after_ref[c, 0, :, cut]
    count = half + 16
    for h in range(2):
        even = [rows_ref[c, h, pl.ds(0, count, stride=2), :] for c in range(3)]
        odd = [rows_ref[c, h, pl.ds(1, count, stride=2), :] for c in range(3)]
        for f in range(9):
            if f < 3:
                e, o = even[f], odd[f]
            else:
                i, j = product_pairs[f - 3]
                e, o = even[i] * even[j], odd[i] * odd[j]
            e, o = ring_lift(e, o)
            stack_ref[f * ny : f * ny + half, h * lanes : (h + 1) * lanes] = e[8 : 8 + half]
            stack_ref[f * ny + half : (f + 1) * ny, h * lanes : (h + 1) * lanes] = o[8 : 8 + half]
    out = dot(stack_ref[...], table_ref[...])
    for f in range(9):
        low_ref[f, 0] = out[f * ny : f * ny + half, :lanes]
        rest_ref[0, f, 0] = out[f * ny + half : (f + 1) * ny, :lanes]
        rest_ref[1, f, 0] = out[f * ny : f * ny + half, lanes:]
        rest_ref[2, f, 0] = out[f * ny + half : (f + 1) * ny, lanes:]


def local_pass(velocity, before, after, table, start):
    _, nx, ny, nz = velocity.shape
    nx = nx // 2
    half, lanes = ny // 2, nz // 2
    return pl.pallas_call(
        local_kernel,
        grid=(nx,),
        in_specs=[
            pl.BlockSpec((3, 1, ny, nz), lambda i: (0, i + start, 0, 0)),
            pl.BlockSpec((3, 1, BEFORE, nz), lambda i: (0, i + start, 0, 0)),
            pl.BlockSpec((3, 1, AFTER, nz), lambda i: (0, i + start, 0, 0)),
            pl.BlockSpec((nz, nz), lambda i: (0, 0)),
        ],
        out_specs=[
            pl.BlockSpec((9, 1, half, lanes), lambda i: (0, i, 0, 0)),
            pl.BlockSpec((3, 9, 1, half, lanes), lambda i: (0, 0, i, 0, 0)),
        ],
        out_shape=[
            jax.ShapeDtypeStruct((9, nx, half, lanes), jnp.float32),
            jax.ShapeDtypeStruct((3, 9, nx, half, lanes), jnp.float32),
        ],
        scratch_shapes=[pltpu.VMEM((3, 2, ny + 32, lanes), jnp.float32), pltpu.VMEM((9 * ny, nz), jnp.float32)],
        compiler_params=pltpu.CompilerParams(vmem_limit_bytes=24 * MIB),
        cost_estimate=pl.CostEstimate(flops=9 * nx * ny * nz * 512, bytes_accessed=9 * nx * ny * nz * 6, transcendentals=0),
        name="local_pass",
    )(velocity, before, after, table)


def pair_of(f):
    k = f - 3
    one = jnp.where(k < 3, 0, jnp.where(k < 5, 1, 2))
    two = jnp.where(k < 3, k, jnp.where(k < 5, k - 2, 2))
    return jnp.where(f < 3, f, one), jnp.where(f < 3, 3, two)


def gather_rows(refs, rows_ref, even_ref, odd_ref):
    edge_before, mid_before, edge_after, mid_after, row_before, row_after = refs
    mid = mid_before.shape[2]
    ny = mid + 16
    lanes = rows_ref.shape[2]
    count = ny // 2 + 16
    even_ref[3] = jnp.ones(even_ref.shape[1:], jnp.float32)
    odd_ref[3] = jnp.ones(odd_ref.shape[1:], jnp.float32)
    for c in range(3):
        for layer in range(BEFORE + AFTER):
            if layer < BEFORE:
                edge, middle, at = edge_before, mid_before, layer
            else:
                edge, middle, at = edge_after, mid_after, layer - BEFORE
            for h in range(2):
                cut = pl.ds(h * lanes, lanes)
                rows_ref[h, 12:16, :] = row_before[c, layer, :, cut]
                rows_ref[h, 16:24, :] = edge[c, at, 0:8, cut]
                rows_ref[h, 24 : 24 + mid, :] = middle[c, at, :, cut]
                rows_ref[h, 24 + mid : 32 + mid, :] = edge[c, at, 8:16, cut]
                rows_ref[h, 16 + ny : 16 + ny + AFTER, :] = row_after[c, layer, :, cut]
                even_ref[c, layer, :, cut] = rows_ref[h, pl.ds(0, count, stride=2), :]
                odd_ref[c, layer, :, cut] = rows_ref[h, pl.ds(1, count, stride=2), :]


def lift_first(layers, halo):
    return halo_lift_list(layers[0::2], layers[1::2], *halo)


def halo_stack(pairs, both, even_ref, odd_ref, part_ref, stack_ref):
    count, nz = even_ref.shape[2:]
    half, lanes = count - 16, nz // 2
    kinds = 8 if both else 4
    for n, (i, j) in enumerate(pairs):
        for h in range(2):
            cut = slice(h * lanes, (h + 1) * lanes)
            for parity, ref in enumerate((even_ref, odd_ref)):
                for r in range(0, count, 16):
                    rows = slice(r, r + 16)
                    g = [ref[i, layer, rows, cut] * ref[j, layer, rows, cut] for layer in range(BEFORE + AFTER)]
                    for k, value in enumerate(parts_for_next(g[:BEFORE]) + parts_for_previous(g[BEFORE:])):
                        part_ref[parity, k, rows, :] = value
            for k in range(4):
                e, o = ring_lift(part_ref[0, k], part_ref[1, k])
                at = (kinds * n + k) * half
                stack_ref[at : at + half, cut] = e[8 : 8 + half]
                if both:
                    at += 4 * half
                    stack_ref[at : at + half, cut] = o[8 : 8 + half]


def layer_list(refs, index, rows):
    return [ref[index + (x, rows)] for ref in refs for x in range(ref.shape[len(index)])]


def approx_kernel(*refs):
    low_refs, table_ref = refs[:2], refs[2]
    halo_refs = refs[3:9]
    approx_ref, high_ref, stress_ref, next_ref, prev_ref, down_ref, up_ref = refs[9:16]
    rows_ref, even_ref, odd_ref, part_ref, stack_ref, out_ref = refs[16:]
    half, lanes = low_refs[0].shape[2:]
    mx = approx_ref.shape[1]
    gather_rows(halo_refs, rows_ref, even_ref, odd_ref)

    def group(g, carry):
        halo_stack([pair_of(g * GROUP + n) for n in range(GROUP)], False, even_ref, odd_ref, part_ref, stack_ref)
        out_ref[...] = dot(stack_ref[...], table_ref[:, :lanes])
        for n in range(GROUP):
            f = g * GROUP + n
            for r in range(0, half, 8):
                rows = slice(r, r + 8)
                halo = [out_ref[(4 * n + k) * half + r : (4 * n + k) * half + r + 8, :] for k in range(4)]
                e, o = lift_first(layer_list(low_refs, (f,), rows), halo)
                e = [t * band_scale(0, 0) for t in e]
                for x in range(mx):
                    approx_ref[f, x, rows, :] = e[x]
                    high_ref[f, x, rows, :] = o[x] * band_scale(0, 1)
                send_layers(e, f, r, next_ref, prev_ref)
            send_rows(approx_ref, f, down_ref, up_ref)
        return carry

    lax.fori_loop(0, 9 // GROUP, group, 0)
    for k, (i, j) in enumerate(product_pairs):
        stress_ref[k] = approx_ref[3 + k] - approx_ref[i] * approx_ref[j]


def whole(shape):
    return pl.BlockSpec(shape, lambda f: (0,) * len(shape))


def per_field(shape):
    return pl.BlockSpec((GROUP,) + shape, lambda f: (f,) + (0,) * len(shape))


def approx_pass(lows, halo, table):
    _, mx, half, lanes = lows[0].shape
    nz, count = 2 * lanes, half + 16
    f32 = lambda *shape: jax.ShapeDtypeStruct(shape, jnp.float32)
    sends = [(2, half, lanes), (2, half, lanes), (mx, 2, lanes), (mx, 2, lanes)]
    out = [f32(9, mx, half, lanes), f32(9, mx, half, lanes), f32(6, mx, half, lanes)] + [f32(9, *t) for t in sends]
    vmem = pl.BlockSpec(memory_space=pltpu.VMEM)
    return pl.pallas_call(
        approx_kernel,
        in_specs=[vmem] * (3 + len(halo)),
        out_specs=[vmem] * len(out),
        out_shape=out,
        scratch_shapes=halo_scratch(half, lanes)
        + [
            pltpu.VMEM((2, 4, count, lanes), jnp.float32),
            pltpu.VMEM((GROUP * 4 * half, nz), jnp.float32),
            pltpu.VMEM((GROUP * 4 * half, lanes), jnp.float32),
        ],
        compiler_params=pltpu.CompilerParams(vmem_limit_bytes=24 * MIB),
        name="approx_pass",
    )(*lows, table, *halo)


def halo_scratch(half, lanes):
    return [
        pltpu.VMEM((2, 2 * half + 32, lanes), jnp.float32),
        pltpu.VMEM((4, BEFORE + AFTER, half + 16, 2 * lanes), jnp.float32),
        pltpu.VMEM((4, BEFORE + AFTER, half + 16, 2 * lanes), jnp.float32),
    ]


def detail_kernel(*refs):
    rest_refs, high_ref, table_ref = refs[:2], refs[2], refs[3]
    halo_refs = refs[4:10]
    out_ref, rows_ref, even_ref, odd_ref, part_ref, stack_ref = refs[10:]
    f = pl.program_id(0)
    half, lanes = high_ref.shape[2:]
    mx = high_ref.shape[1]

    @pl.when(f == 0)
    def _():
        gather_rows(halo_refs, rows_ref, even_ref, odd_ref)

    pairs = [pair_of(f * GROUP + n) for n in range(GROUP)]
    halo_stack(pairs, True, even_ref, odd_ref, part_ref, stack_ref)
    stack_ref[...] = dot(stack_ref[...], table_ref[...])
    for n in range(GROUP):
        for x in range(mx):
            out_ref[0, n, x] = high_ref[n, x]
        for band, (bz, by) in enumerate(((0, 1), (1, 0), (1, 1))):
            plane = 4 * bz + 2 * by - 1
            for r in range(0, half, 8):
                rows = slice(r, r + 8)
                halo = []
                for k in range(4):
                    at = (8 * n + 4 * by + k) * half + r
                    halo.append(stack_ref[at : at + 8, bz * lanes : (bz + 1) * lanes])
                e, o = lift_first(layer_list(rest_refs, (band, n), rows), halo)
                for x in range(mx):
                    out_ref[plane, n, x, rows, :] = e[x] * band_scale(by, 0)
                    out_ref[plane + 1, n, x, rows, :] = o[x] * band_scale(by, 1)


def detail_pass(rests, high, halo, table):
    _, mx, half, lanes = high.shape
    nz, count = 2 * lanes, half + 16
    return pl.pallas_call(
        detail_kernel,
        grid=(9 // GROUP,),
        in_specs=[pl.BlockSpec((3, GROUP, mx, half, lanes), lambda f: (0, f, 0, 0, 0))] * 2
        + [per_field((mx, half, lanes)), whole((nz, nz))]
        + [whole(h.shape) for h in halo],
        out_specs=pl.BlockSpec((7, GROUP, mx, half, lanes), lambda f: (0, f, 0, 0, 0)),
        out_shape=jax.ShapeDtypeStruct((7, 9, mx, half, lanes), jnp.float32),
        scratch_shapes=halo_scratch(half, lanes)
        + [pltpu.VMEM((2, 4, count, lanes), jnp.float32), pltpu.VMEM((GROUP * 8 * half, nz), jnp.float32)],
        compiler_params=pltpu.CompilerParams(vmem_limit_bytes=24 * MIB),
        cost_estimate=pl.CostEstimate(flops=18 * mx * half * nz * 200, bytes_accessed=18 * mx * half * nz * 16, transcendentals=0),
        name="detail_pass",
    )(*rests, high, table, *halo)


def level_rows(refs, nz, lows, pad_ref, stack_ref):
    a_ref, before_ref, after_ref, down_ref, up_ref = refs
    nx, ny = a_ref.shape[1:3]
    half = ny // 2
    wide = stack_ref.shape[1]
    kept = half if lows else ny
    if nz < wide:
        pad_ref[...] = jnp.zeros_like(pad_ref)
    for f in range(9):
        for layer in range(nx + 4):
            if layer < nx:
                source, at = a_ref, layer
            elif layer < nx + 2:
                source, at = before_ref, layer - nx
            else:
                source, at = after_ref, layer - nx - 2
            if nz < wide:
                pad_ref[f, layer, :, :nz] = source[f, at]
                source, at = pad_ref, layer
            e = source[f, at, pl.ds(0, half, stride=2), :]
            o = source[f, at, pl.ds(1, half, stride=2), :]
            rows = [down_ref[f, layer, 1:2, :], down_ref[f, layer, 0:1, :], up_ref[f, layer, 0:1, :], up_ref[f, layer, 1:2, :]]
            if nz < wide:
                rows = [jnp.concatenate([row, jnp.zeros((1, wide - nz), jnp.float32)], axis=1) for row in rows]
            e, o = sublane_lift(e, o, *rows)
            at = (f * (nx + 4) + layer) * kept
            stack_ref[at : at + half, :] = e
            if not lows:
                stack_ref[at + half : at + ny, :] = o


def level_approx_kernel(nz, *refs):
    table_ref, approx_ref, stress_ref = refs[5:8]
    sends, (pad_ref, stack_ref, out_ref, kept_ref) = refs[8:-4], refs[-4:]
    nx, ny = refs[0].shape[1:3]
    half, lanes = ny // 2, nz // 2
    level_rows(refs[:5], nz, True, pad_ref, stack_ref)
    out_ref[...] = dot(stack_ref[...], table_ref[...])
    mx = nx // 2
    for f in range(9):
        for r in range(0, half, 8):
            rows = slice(r, r + 8)
            layers = []
            for layer in range(nx + 4):
                at = (f * (nx + 4) + layer) * half + r
                layers.append(out_ref[at : at + 8, :])
            low, _ = lift_first(layers[:nx], layers[nx:])
            approx = [(t * band_scale(0, 0))[:, :lanes] for t in low]
            for x in range(mx):
                if f < 3:
                    kept_ref[f, x, rows, :] = approx[x]
                else:
                    i, j = product_pairs[f - 3]
                    stress_ref[f - 3, x, rows, :] = approx[x] - kept_ref[i, x, rows, :] * kept_ref[j, x, rows, :]
                approx_ref[f, x, rows, :] = approx[x]
            send_layers(approx, f, r, sends[0], sends[1])
        send_rows(approx_ref, f, sends[2], sends[3])


def level_detail_kernel(nz, last, *refs):
    table_ref, detail_ref = refs[5:7]
    pad_ref, stack_ref, out_ref, kept_ref = refs[-4:]
    nx, ny = refs[0].shape[1:3]
    half, lanes = ny // 2, nz // 2
    wide = stack_ref.shape[1]
    level_rows(refs[:5], nz, False, pad_ref, stack_ref)
    out_ref[...] = dot(stack_ref[...], table_ref[...])
    for f in range(9):
        for by in range(2):
            for r in range(0, half, 8):
                rows = slice(r, r + 8)
                layers = []
                for layer in range(nx + 4):
                    at = (f * (nx + 4) + layer) * ny + by * half + r
                    layers.append(out_ref[at : at + 8, :])
                low, high = lift_first(layers[:nx], layers[nx:])
                for x in range(nx // 2):
                    for bx, value in enumerate((low[x], high[x])):
                        t = value * band_scale(by, bx)
                        for bz in range(2):
                            band = 4 * bz + 2 * by + bx
                            piece = t[:, bz * (wide // 2) : bz * (wide // 2) + lanes]
                            if band:
                                detail_ref[band - 1, f, x, rows, :] = piece
                            elif last:
                                stress_ref, approx_ref = refs[7:9]
                                if f < 3:
                                    kept_ref[f, x, rows, :] = piece
                                    approx_ref[f, x, rows, :] = piece
                                else:
                                    i, j = product_pairs[f - 3]
                                    stress_ref[f - 3, x, rows, :] = piece - kept_ref[i, x, rows, :] * kept_ref[j, x, rows, :]


def level_call(kernel, approx, halo, out, kept):
    _, nx, ny, nz = approx.shape
    wide = max(nz, 128)
    vmem = pl.BlockSpec(memory_space=pltpu.VMEM)
    return pl.pallas_call(
        kernel,
        in_specs=[vmem] * 6,
        out_specs=[vmem] * len(out),
        out_shape=out,
        scratch_shapes=[
            pltpu.VMEM((9, nx + 4, ny, wide), jnp.float32),
            pltpu.VMEM((9 * (nx + 4) * kept, wide), jnp.float32),
            pltpu.VMEM((9 * (nx + 4) * kept, wide), jnp.float32),
            pltpu.VMEM((3, nx // 2, ny // 2, nz // 2), jnp.float32),
        ],
        compiler_params=pltpu.CompilerParams(vmem_limit_bytes=24 * MIB),
    )(approx, *halo, jnp.asarray(third_table(nz, wide)))


def level_approx(approx, halo):
    _, nx, ny, nz = approx.shape
    mx, half, lanes = nx // 2, ny // 2, nz // 2
    f32 = lambda *shape: jax.ShapeDtypeStruct(shape, jnp.float32)
    sends = ((2, half, lanes), (2, half, lanes), (mx, 2, lanes), (mx, 2, lanes))
    out = [f32(9, mx, half, lanes), f32(6, mx, half, lanes)] + [f32(9, *s) for s in sends]
    return level_call(lambda *refs: level_approx_kernel(nz, *refs), approx, halo, out, half)


def level_details(approx, halo, last):
    _, nx, ny, nz = approx.shape
    mx, half, lanes = nx // 2, ny // 2, nz // 2
    f32 = lambda *shape: jax.ShapeDtypeStruct(shape, jnp.float32)
    out = [f32(7, 9, mx, half, lanes)]
    if last:
        out += [f32(6, mx, half, lanes), f32(3, mx, half, lanes)]
    return level_call(lambda *refs: level_detail_kernel(nz, last, *refs), approx, halo, out, ny)


def halo_rows(before, after, down, up):
    rows = before.shape[2]
    cell = lambda at: jnp.concatenate([before[:, :, at : at + 1], after[:, :, at : at + 1]], axis=1)
    p, q = parts_for_next([cell(rows - 4 + i) for i in range(4)])
    down = jnp.concatenate([down, jnp.concatenate([q, p], axis=2)], axis=1)
    head = jnp.concatenate(parts_for_previous([cell(i) for i in range(3)]), axis=2)
    up = jnp.concatenate([up, head], axis=1)
    return shifted(down, "gy", 1), shifted(up, "gy", -1)


def body(velocity):
    _, nx, ny, nz = velocity.shape
    table = jnp.asarray(third_table(nz, nz))
    tail, head = velocity[:, nx - BEFORE :], velocity[:, :AFTER]
    edges = lambda t: jnp.concatenate([t[:, :, :8], t[:, :, ny - 8 :]], axis=2)
    edge_before = shifted(edges(tail), "gx", 1)
    edge_after = shifted(edges(head), "gx", -1)
    mid_before = shifted(tail[:, :, 8 : ny - 8], "gx", 1)
    mid_after = shifted(head[:, :, 8 : ny - 8], "gx", -1)
    own_before = shifted(velocity[:, :, ny - BEFORE :], "gy", 1)
    own_after = shifted(velocity[:, :, :AFTER], "gy", -1)
    low_one, rest_one = local_pass(velocity, own_before, own_after, table, 0)
    edge_before, edge_after, low_one = lax.optimization_barrier((edge_before, edge_after, low_one))
    down = jnp.concatenate([edge_before[:, :, 12:], edge_after[:, :, 12:]], axis=1)
    up = jnp.concatenate([edge_before[:, :, :AFTER], edge_after[:, :, :AFTER]], axis=1)
    row_before = shifted(down, "gy", 1)
    row_after = shifted(up, "gy", -1)
    low_two, rest_two = local_pass(velocity, own_before, own_after, table, nx // 2)
    halo = (edge_before, mid_before, edge_after, mid_after, row_before, row_after)
    approx, high, stress_one, *sends = approx_pass((low_one, low_two), halo, table)
    before = shifted(sends[0], "gx", 1)
    after = shifted(sends[1], "gx", -1)
    details_one = detail_pass((rest_one, rest_two), high, halo, table)
    before, after, details_one = lax.optimization_barrier((before, after, details_one))
    second_halo = (before, after) + halo_rows(before, after, *sends[2:])
    second = approx
    approx, stress_two, *sends = level_approx(second, second_halo)
    before = shifted(sends[0], "gx", 1)
    after = shifted(sends[1], "gx", -1)
    (details_two,) = level_details(second, second_halo, False)
    before, after, details_two = lax.optimization_barrier((before, after, details_two))
    third_halo = (before, after) + halo_rows(before, after, *sends[2:])
    details_three, stress_three, coarse = level_details(approx, third_halo, True)
    return details_one, stress_one, details_two, stress_two, details_three, stress_three, coarse


def solution(mesh):
    in_specs = (P(None, "gx", "gy", None),)
    out_specs = (
        P(None, None, "gx", "gy", None),
        P(None, "gx", "gy", None),
        P(None, None, "gx", "gy", None),
        P(None, "gx", "gy", None),
        P(None, None, "gx", "gy", None),
        P(None, "gx", "gy", None),
        P(None, "gx", "gy", None),
    )
    return jax.shard_map(body, mesh=mesh, in_specs=in_specs, out_specs=out_specs, check_vma=False)
```

```python
import jax
import jax.numpy as jnp
import numpy as np
from jax import lax
from jax.experimental import pallas as pl
from jax.experimental.pallas import tpu as pltpu
from jax.sharding import PartitionSpec as P

predict_one = -1.586134342
update_one = -0.05298011854
predict_two = 0.8829110762
update_two = 0.4435068522
scaling = 1.149604398
product_pairs = ((0, 0), (0, 1), (0, 2), (1, 1), (1, 2), (2, 2))
BEFORE = 4
AFTER = 3
GROUP = 3
MIB = 1 << 20


def shifted(block, axis, distance):
    size = lax.axis_size(axis)
    return lax.ppermute(block, axis, [(i, (i + distance) % size) for i in range(size)])


def third_table(length, lanes):
    eye = np.eye(length)
    e, o = eye[:, 0::2], eye[:, 1::2]
    following = lambda t: np.concatenate([t[:, 1:], t[:, -1:]], 1)
    preceding = lambda t: np.concatenate([t[:, :1], t[:, :-1]], 1)
    o = o + predict_one * (e + following(e))
    e = e + update_one * (o + preceding(o))
    o = o + predict_two * (e + following(e))
    e = e + update_two * (o + preceding(o))
    table = np.zeros((lanes, lanes))
    table[:length, : length // 2] = e * scaling
    table[:length, lanes // 2 : lanes // 2 + length // 2] = o / scaling
    return table.astype(np.float32)


def band_scale(by, bx):
    return float(scaling ** ((1 - 2 * by) + (1 - 2 * bx)))


def dot(a, b):
    a_high, b_high = a.astype(jnp.bfloat16), b.astype(jnp.bfloat16)
    a_low = (a - a_high.astype(jnp.float32)).astype(jnp.bfloat16)
    b_low = (b - b_high.astype(jnp.float32)).astype(jnp.bfloat16)
    part = lambda x, y: jnp.dot(x, y, preferred_element_type=jnp.float32)
    return part(a_high, b_high) + (part(a_high, b_low) + part(a_low, b_high))


def ring_lift(e, o):
    n = e.shape[0]
    up = lambda t: pltpu.roll(t, n - 1, 0)
    down = lambda t: pltpu.roll(t, 1, 0)
    o = o + predict_one * (e + up(e))
    e = e + update_one * (o + down(o))
    o = o + predict_two * (e + up(e))
    e = e + update_two * (o + down(o))
    return e, o


def halo_lift(e, o, p, q, r, s, following, preceding, first, last):
    o1 = o + predict_one * (e + following(e, r))
    o1_before = p + predict_one * first(e)
    e1 = e + update_one * (preceding(o1, o1_before) + o1)
    e1_before = q + update_one * o1_before
    e1_after = r + update_one * (last(o1) + s)
    o2 = o1 + predict_two * (e1 + following(e1, e1_after))
    o2_before = o1_before + predict_two * (e1_before + first(e1))
    e2 = e1 + update_two * (preceding(o2, o2_before) + o2)
    return e2, o2


def halo_lift_list(e, o, p, q, r, s):
    m = len(e)
    e = list(e) + [r]
    o1 = [p + predict_one * e[0]]
    o1 += [o[i] + predict_one * (e[i] + e[i + 1]) for i in range(m)] + [s]
    e1 = [q + update_one * o1[0]]
    e1 += [e[i] + update_one * (o1[i] + o1[i + 1]) for i in range(m + 1)]
    o2 = [o1[i] + predict_two * (e1[i] + e1[i + 1]) for i in range(m + 1)]
    e2 = [e1[i + 1] + update_two * (o2[i] + o2[i + 1]) for i in range(m)]
    return e2, o2[1:]


def sublane_lift(e, o, p, q, r, s):
    n = e.shape[0]
    row = lax.broadcasted_iota(jnp.int32, e.shape, 0)
    following = lambda t, edge: jnp.where(row == n - 1, edge, pltpu.roll(t, n - 1, 0))
    preceding = lambda t, edge: jnp.where(row == 0, edge, pltpu.roll(t, 1, 0))
    return halo_lift(e, o, p, q, r, s, following, preceding, lambda t: t[0:1], lambda t: t[n - 1 : n])


def parts_for_next(c):
    p = c[-1] + predict_one * c[-2]
    q = c[-2] + update_one * (c[-3] + predict_one * (c[-4] + c[-2]))
    return p, q


def parts_for_previous(c):
    return c[0], c[1] + predict_one * (c[0] + c[2])


def row_parts(load, rows):
    tail, head = load(rows - 8), load(0)
    row = lax.broadcasted_iota(jnp.int32, tail.shape, 0)
    inner = tail + predict_one * (pltpu.roll(tail, 1, 0) + pltpu.roll(tail, 7, 0))
    p = tail + predict_one * pltpu.roll(tail, 1, 0)
    q = tail + update_one * pltpu.roll(inner, 1, 0)
    s = head + predict_one * (pltpu.roll(head, 1, 0) + pltpu.roll(head, 7, 0))
    return jnp.where(row == 7, p, q)[6:8], jnp.where(row == 0, head, s)[0:2]


def send_layers(layers, f, at, next_ref, prev_ref):
    for part, value in enumerate(parts_for_next(layers)):
        next_ref[f, part, at : at + 8, :] = value
    for part, value in enumerate(parts_for_previous(layers)):
        prev_ref[f, part, at : at + 8, :] = value


def send_rows(ref, f, down_ref, up_ref):
    for at in range(ref.shape[1]):
        tail, head = row_parts(lambda row: ref[f, at, row : row + 8, :], ref.shape[2])
        down_ref[f, at] = tail
        up_ref[f, at] = head


def local_kernel(v_ref, before_ref, after_ref, table_ref, low_ref, rest_ref, rows_ref, stack_ref):
    ny = v_ref.shape[2]
    half = ny // 2
    lanes = v_ref.shape[3] // 2
    even, odd = [], []
    for c in range(3):
        for h in range(2):
            cut = pl.ds(h * lanes, lanes)
            rows_ref[c, h, 12:16, :] = before_ref[c, 0, :, cut]
            rows_ref[c, h, 16 : 16 + ny, :] = v_ref[c, 0, :, cut]
            rows_ref[c, h, 16 + ny : 16 + ny + AFTER, :] = after_ref[c, 0, :, cut]
    count = half + 16
    for h in range(2):
        even = [rows_ref[c, h, pl.ds(0, count, stride=2), :] for c in range(3)]
        odd = [rows_ref[c, h, pl.ds(1, count, stride=2), :] for c in range(3)]
        for f in range(9):
            if f < 3:
                e, o = even[f], odd[f]
            else:
                i, j = product_pairs[f - 3]
                e, o = even[i] * even[j], odd[i] * odd[j]
            e, o = ring_lift(e, o)
            stack_ref[f * ny : f * ny + half, h * lanes : (h + 1) * lanes] = e[8 : 8 + half]
            stack_ref[f * ny + half : (f + 1) * ny, h * lanes : (h + 1) * lanes] = o[8 : 8 + half]
    out = dot(stack_ref[...], table_ref[...])
    for f in range(9):
        low_ref[f, 0] = out[f * ny : f * ny + half, :lanes]
        rest_ref[0, f, 0] = out[f * ny + half : (f + 1) * ny, :lanes]
        rest_ref[1, f, 0] = out[f * ny : f * ny + half, lanes:]
        rest_ref[2, f, 0] = out[f * ny + half : (f + 1) * ny, lanes:]


def local_pass(velocity, before, after, table, start):
    _, nx, ny, nz = velocity.shape
    nx = nx // 2
    half, lanes = ny // 2, nz // 2
    return pl.pallas_call(
        local_kernel,
        grid=(nx,),
        in_specs=[
            pl.BlockSpec((3, 1, ny, nz), lambda i: (0, i + start, 0, 0)),
            pl.BlockSpec((3, 1, BEFORE, nz), lambda i: (0, i + start, 0, 0)),
            pl.BlockSpec((3, 1, AFTER, nz), lambda i: (0, i + start, 0, 0)),
            pl.BlockSpec((nz, nz), lambda i: (0, 0)),
        ],
        out_specs=[
            pl.BlockSpec((9, 1, half, lanes), lambda i: (0, i, 0, 0)),
            pl.BlockSpec((3, 9, 1, half, lanes), lambda i: (0, 0, i, 0, 0)),
        ],
        out_shape=[
            jax.ShapeDtypeStruct((9, nx, half, lanes), jnp.float32),
            jax.ShapeDtypeStruct((3, 9, nx, half, lanes), jnp.float32),
        ],
        scratch_shapes=[pltpu.VMEM((3, 2, ny + 32, lanes), jnp.float32), pltpu.VMEM((9 * ny, nz), jnp.float32)],
        compiler_params=pltpu.CompilerParams(vmem_limit_bytes=24 * MIB),
        cost_estimate=pl.CostEstimate(flops=9 * nx * ny * nz * 512, bytes_accessed=9 * nx * ny * nz * 6, transcendentals=0),
        name="local_pass",
    )(velocity, before, after, table)


def pair_of(f):
    k = f - 3
    one = jnp.where(k < 3, 0, jnp.where(k < 5, 1, 2))
    two = jnp.where(k < 3, k, jnp.where(k < 5, k - 2, 2))
    return jnp.where(f < 3, f, one), jnp.where(f < 3, 3, two)


def gather_rows(refs, first, rows_ref, even_ref, odd_ref):
    edge, middle, row_before, row_after = refs
    layers, mid = middle.shape[1:3]
    ny = mid + 16
    lanes = rows_ref.shape[2]
    count = ny // 2 + 16
    even_ref[3] = jnp.ones(even_ref.shape[1:], jnp.float32)
    odd_ref[3] = jnp.ones(odd_ref.shape[1:], jnp.float32)
    for c in range(3):
        for layer in range(layers):
            for h in range(2):
                cut = pl.ds(h * lanes, lanes)
                rows_ref[h, 12:16, :] = row_before[c, first + layer, :, cut]
                rows_ref[h, 16:24, :] = edge[c, layer, 0:8, cut]
                rows_ref[h, 24 : 24 + mid, :] = middle[c, layer, :, cut]
                rows_ref[h, 24 + mid : 32 + mid, :] = edge[c, layer, 8:16, cut]
                rows_ref[h, 16 + ny : 16 + ny + AFTER, :] = row_after[c, first + layer, :, cut]
                even_ref[c, layer, :, cut] = rows_ref[h, pl.ds(0, count, stride=2), :]
                odd_ref[c, layer, :, cut] = rows_ref[h, pl.ds(1, count, stride=2), :]


def lift_first(layers, halo):
    return halo_lift_list(layers[0::2], layers[1::2], *halo)


def halo_stack(pairs, both, combine, even_ref, odd_ref, part_ref, stack_ref):
    count, nz = even_ref.shape[2:]
    half, lanes = count - 16, nz // 2
    kinds = 4 if both else 2
    for n, (i, j) in enumerate(pairs):
        for h in range(2):
            cut = slice(h * lanes, (h + 1) * lanes)
            for parity, ref in enumerate((even_ref, odd_ref)):
                for r in range(0, count, 16):
                    rows = slice(r, r + 16)
                    g = [ref[i, layer, rows, cut] * ref[j, layer, rows, cut] for layer in range(ref.shape[1])]
                    for k, value in enumerate(combine(g)):
                        part_ref[parity, k, rows, :] = value
            for k in range(2):
                e, o = ring_lift(part_ref[0, k], part_ref[1, k])
                at = (kinds * n + k) * half
                stack_ref[at : at + half, cut] = e[8 : 8 + half]
                if both:
                    at += 2 * half
                    stack_ref[at : at + half, cut] = o[8 : 8 + half]


def halo_kernel(*refs):
    table_ref, low_ref, rest_ref = refs[4:7]
    rows_ref, even_ref, odd_ref, part_ref, stack_ref = refs[7:]
    half, lanes = low_ref.shape[2:]
    gather_rows(refs[:4], 0, rows_ref, even_ref, odd_ref)

    def group(g, carry):
        pairs = [pair_of(g * GROUP + n) for n in range(GROUP)]
        halo_stack(pairs, True, parts_for_next, even_ref, odd_ref, part_ref, stack_ref)
        stack_ref[...] = dot(stack_ref[...], table_ref[...])
        for n in range(GROUP):
            for k in range(2):
                low, high = (slice((4 * n + k + m) * half, (4 * n + k + m + 1) * half) for m in (0, 2))
                low_ref[g * GROUP + n, k] = stack_ref[low, :lanes]
                rest_ref[0, g * GROUP + n, k] = stack_ref[high, :lanes]
                rest_ref[1, g * GROUP + n, k] = stack_ref[low, lanes:]
                rest_ref[2, g * GROUP + n, k] = stack_ref[high, lanes:]
        return carry

    lax.fori_loop(0, 9 // GROUP, group, 0)


def halo_pass(halo, table):
    half, lanes = (halo[1].shape[2] + 16) // 2, halo[1].shape[3] // 2
    vmem = pl.BlockSpec(memory_space=pltpu.VMEM)
    return pl.pallas_call(
        halo_kernel,
        in_specs=[vmem] * 5,
        out_specs=[vmem] * 2,
        out_shape=[
            jax.ShapeDtypeStruct((9, 2, half, lanes), jnp.float32),
            jax.ShapeDtypeStruct((3, 9, 2, half, lanes), jnp.float32),
        ],
        scratch_shapes=halo_scratch(half, lanes, BEFORE, True),
        compiler_params=pltpu.CompilerParams(vmem_limit_bytes=24 * MIB),
        name="halo_pass",
    )(*halo, table)


def layer_list(refs, index, rows):
    return [ref[index + (x, rows)] for ref in refs for x in range(ref.shape[len(index)])]


def approx_kernel(*refs):
    low_refs, before_ref, table_ref = refs[:2], refs[2], refs[3]
    halo_refs = refs[4:8]
    approx_ref, high_ref, stress_ref = refs[8:11]
    next_ref, prev_ref, next_edge_ref, prev_edge_ref, down_ref, up_ref = refs[11:17]
    rows_ref, even_ref, odd_ref, part_ref, stack_ref, kept_ref, out_ref = refs[17:]
    f = pl.program_id(0)
    half, lanes = low_refs[0].shape[2:]
    mx = approx_ref.shape[1]

    @pl.when(f == 0)
    def _():
        gather_rows(halo_refs, BEFORE, rows_ref, even_ref, odd_ref)

    pairs = [pair_of(f * GROUP + n) for n in range(GROUP)]
    halo_stack(pairs, False, parts_for_previous, even_ref, odd_ref, part_ref, stack_ref)
    out_ref[...] = dot(stack_ref[...], table_ref[:, :lanes])
    for n in range(GROUP):
        for r in range(0, half, 8):
            rows = slice(r, r + 8)
            halo = [before_ref[n, k, rows, :] for k in range(2)]
            halo += [out_ref[(2 * n + k) * half + r : (2 * n + k) * half + r + 8, :] for k in range(2)]
            e, o = lift_first(layer_list(low_refs, (n,), rows), halo)
            e = [t * band_scale(0, 0) for t in e]
            for x in range(mx):
                approx_ref[n, x, rows, :] = e[x]
                high_ref[n, x, rows, :] = o[x] * band_scale(0, 1)
            send_layers(e, n, r, next_ref, prev_ref)
        send_rows(approx_ref, n, down_ref, up_ref)
        for ref, edge_ref in ((next_ref, next_edge_ref), (prev_ref, prev_edge_ref)):
            for part in range(2):
                tail, head = row_parts(lambda row: ref[n, part, row : row + 8, :], half)
                edge_ref[n, part, 0:2, :] = tail
                edge_ref[n, part, 2:4, :] = head

    @pl.when(f == 0)
    def _():
        kept_ref[...] = approx_ref[...]

    @pl.when(f > 0)
    def _():
        for n, (i, j) in enumerate(pairs):
            for x in range(mx):
                stress_ref[n, x] = approx_ref[n, x] - kept_ref[i, x] * kept_ref[j, x]


def whole(shape):
    return pl.BlockSpec(shape, lambda f: (0,) * len(shape))


def per_field(shape):
    return pl.BlockSpec((GROUP,) + shape, lambda f: (f,) + (0,) * len(shape))


def approx_pass(lows, before, halo, table):
    _, nx, half, lanes = lows[0].shape
    nz, mx = 2 * lanes, nx
    f32 = lambda *shape: jax.ShapeDtypeStruct(shape, jnp.float32)
    sends = [(2, half, lanes), (2, half, lanes), (2, 4, lanes), (2, 4, lanes), (mx, 2, lanes), (mx, 2, lanes)]
    return pl.pallas_call(
        approx_kernel,
        grid=(9 // GROUP,),
        in_specs=[per_field((nx, half, lanes))] * 2
        + [per_field((2, half, lanes)), whole((nz, nz))]
        + [whole(h.shape) for h in halo],
        out_specs=[
            per_field((mx, half, lanes)),
            per_field((mx, half, lanes)),
            pl.BlockSpec((GROUP, mx, half, lanes), lambda f: (jnp.maximum(f - 1, 0), 0, 0, 0)),
        ]
        + [per_field(s) for s in sends],
        out_shape=[f32(9, mx, half, lanes), f32(9, mx, half, lanes), f32(6, mx, half, lanes)] + [f32(9, *s) for s in sends],
        scratch_shapes=halo_scratch(half, lanes, AFTER, False)
        + [
            pltpu.VMEM((3, mx, half, lanes), jnp.float32),
            pltpu.VMEM((GROUP * 2 * half, lanes), jnp.float32),
        ],
        compiler_params=pltpu.CompilerParams(vmem_limit_bytes=24 * MIB),
        name="approx_pass",
    )(*lows, before, table, *halo)


def halo_scratch(half, lanes, layers, both):
    return [
        pltpu.VMEM((2, 2 * half + 32, lanes), jnp.float32),
        pltpu.VMEM((4, layers, half + 16, 2 * lanes), jnp.float32),
        pltpu.VMEM((4, layers, half + 16, 2 * lanes), jnp.float32),
        pltpu.VMEM((2, 2, half + 16, lanes), jnp.float32),
        pltpu.VMEM((GROUP * (4 if both else 2) * half, 2 * lanes), jnp.float32),
    ]


def detail_kernel(*refs):
    rest_refs, before_ref, high_ref, table_ref = refs[:2], refs[2], refs[3], refs[4]
    halo_refs = refs[5:9]
    out_ref, rows_ref, even_ref, odd_ref, part_ref, stack_ref = refs[9:]
    f = pl.program_id(0)
    half, lanes = high_ref.shape[2:]
    mx = high_ref.shape[1]

    @pl.when(f == 0)
    def _():
        gather_rows(halo_refs, BEFORE, rows_ref, even_ref, odd_ref)

    pairs = [pair_of(f * GROUP + n) for n in range(GROUP)]
    halo_stack(pairs, True, parts_for_previous, even_ref, odd_ref, part_ref, stack_ref)
    stack_ref[...] = dot(stack_ref[...], table_ref[...])
    for n in range(GROUP):
        for x in range(mx):
            out_ref[0, n, x] = high_ref[n, x]
        for band, (bz, by) in enumerate(((0, 1), (1, 0), (1, 1))):
            plane = 4 * bz + 2 * by - 1
            for r in range(0, half, 8):
                rows = slice(r, r + 8)
                halo = [before_ref[band, n, k, rows, :] for k in range(2)]
                for k in range(2):
                    at = (4 * n + 2 * by + k) * half + r
                    halo.append(stack_ref[at : at + 8, bz * lanes : (bz + 1) * lanes])
                e, o = lift_first(layer_list(rest_refs, (band, n), rows), halo)
                for x in range(mx):
                    out_ref[plane, n, x, rows, :] = e[x] * band_scale(by, 0)
                    out_ref[plane + 1, n, x, rows, :] = o[x] * band_scale(by, 1)


def detail_pass(rests, before, high, halo, table):
    _, mx, half, lanes = high.shape
    nz = 2 * lanes
    return pl.pallas_call(
        detail_kernel,
        grid=(9 // GROUP,),
        in_specs=[pl.BlockSpec((3, GROUP, mx, half, lanes), lambda f: (0, f, 0, 0, 0))] * 2
        + [pl.BlockSpec((3, GROUP, 2, half, lanes), lambda f: (0, f, 0, 0, 0)), per_field((mx, half, lanes)), whole((nz, nz))]
        + [whole(h.shape) for h in halo],
        out_specs=pl.BlockSpec((7, GROUP, mx, half, lanes), lambda f: (0, f, 0, 0, 0)),
        out_shape=jax.ShapeDtypeStruct((7, 9, mx, half, lanes), jnp.float32),
        scratch_shapes=halo_scratch(half, lanes, AFTER, True),
        compiler_params=pltpu.CompilerParams(vmem_limit_bytes=24 * MIB),
        cost_estimate=pl.CostEstimate(flops=18 * mx * half * nz * 200, bytes_accessed=18 * mx * half * nz * 16, transcendentals=0),
        name="detail_pass",
    )(*rests, before, high, table, *halo)


def level_rows(refs, nz, nx, span, lows, pad_ref, stack_ref):
    a_ref, before_ref, after_ref, down_ref, up_ref = refs
    ny = (before_ref if a_ref is None else a_ref).shape[2]
    half = ny // 2
    wide = stack_ref.shape[1]
    kept = half if lows else ny
    if nz < wide:
        pad_ref[...] = jnp.zeros_like(pad_ref)
    for f in range(9):
        for step, layer in enumerate(span):
            if layer < nx:
                source, at = a_ref, layer
            elif layer < nx + 2:
                source, at = before_ref, layer - nx
            else:
                source, at = after_ref, layer - nx - 2
            if nz < wide:
                pad_ref[f, layer, :, :nz] = source[f, at]
                source, at = pad_ref, layer
            e = source[f, at, pl.ds(0, half, stride=2), :]
            o = source[f, at, pl.ds(1, half, stride=2), :]
            rows = [down_ref[f, layer, 1:2, :], down_ref[f, layer, 0:1, :], up_ref[f, layer, 0:1, :], up_ref[f, layer, 1:2, :]]
            if nz < wide:
                rows = [jnp.concatenate([row, jnp.zeros((1, wide - nz), jnp.float32)], axis=1) for row in rows]
            e, o = sublane_lift(e, o, *rows)
            at = (f * len(span) + step) * kept
            stack_ref[at : at + half, :] = e
            if not lows:
                stack_ref[at + half : at + ny, :] = o


def level_own_kernel(nz, a_ref, down_ref, up_ref, table_ref, own_ref, stack_ref):
    nx, _ = a_ref.shape[1:3]
    level_rows((a_ref, None, None, down_ref, up_ref), nz, nx, range(nx), True, None, stack_ref)
    own_ref[...] = dot(stack_ref[...], table_ref[...]).reshape(own_ref.shape)


def level_approx_kernel(nz, *refs):
    own_ref, table_ref, approx_ref, stress_ref = refs[0], refs[5], refs[6], refs[7]
    sends, (stack_ref, out_ref, kept_ref) = refs[8:-3], refs[-3:]
    nx, half = own_ref.shape[1:3]
    lanes = nz // 2
    level_rows((None,) + refs[1:5], nz, nx, range(nx, nx + 4), True, None, stack_ref)
    out_ref[...] = dot(stack_ref[...], table_ref[...])
    mx = nx // 2
    for f in range(9):
        for r in range(0, half, 8):
            rows = slice(r, r + 8)
            halo = []
            for k in range(4):
                at = (f * 4 + k) * half + r
                halo.append(out_ref[at : at + 8, :])
            low, _ = lift_first([own_ref[f, x, rows, :] for x in range(nx)], halo)
            approx = [(t * band_scale(0, 0))[:, :lanes] for t in low]
            for x in range(mx):
                if f < 3:
                    kept_ref[f, x, rows, :] = approx[x]
                else:
                    i, j = product_pairs[f - 3]
                    stress_ref[f - 3, x, rows, :] = approx[x] - kept_ref[i, x, rows, :] * kept_ref[j, x, rows, :]
                approx_ref[f, x, rows, :] = approx[x]
            send_layers(approx, f, r, sends[0], sends[1])
        send_rows(approx_ref, f, sends[2], sends[3])


def level_detail_kernel(nz, last, *refs):
    table_ref, detail_ref = refs[5:7]
    pad_ref, stack_ref, out_ref, kept_ref = refs[-4:]
    nx, ny = refs[0].shape[1:3]
    half, lanes = ny // 2, nz // 2
    wide = stack_ref.shape[1]
    level_rows(refs[:5], nz, nx, range(nx + 4), False, pad_ref, stack_ref)
    out_ref[...] = dot(stack_ref[...], table_ref[...])
    for f in range(9):
        for by in range(2):
            for r in range(0, half, 8):
                rows = slice(r, r + 8)
                layers = []
                for layer in range(nx + 4):
                    at = (f * (nx + 4) + layer) * ny + by * half + r
                    layers.append(out_ref[at : at + 8, :])
                low, high = lift_first(layers[:nx], layers[nx:])
                for x in range(nx // 2):
                    for bx, value in enumerate((low[x], high[x])):
                        t = value * band_scale(by, bx)
                        for bz in range(2):
                            band = 4 * bz + 2 * by + bx
                            piece = t[:, bz * (wide // 2) : bz * (wide // 2) + lanes]
                            if band:
                                detail_ref[band - 1, f, x, rows, :] = piece
                            elif last:
                                stress_ref, approx_ref = refs[7:9]
                                if f < 3:
                                    kept_ref[f, x, rows, :] = piece
                                    approx_ref[f, x, rows, :] = piece
                                else:
                                    i, j = product_pairs[f - 3]
                                    stress_ref[f - 3, x, rows, :] = piece - kept_ref[i, x, rows, :] * kept_ref[j, x, rows, :]


def level_call(kernel, approx, halo, out, kept):
    _, nx, ny, nz = approx.shape
    wide = max(nz, 128)
    vmem = pl.BlockSpec(memory_space=pltpu.VMEM)
    return pl.pallas_call(
        kernel,
        in_specs=[vmem] * 6,
        out_specs=[vmem] * len(out),
        out_shape=out,
        scratch_shapes=[
            pltpu.VMEM((9, nx + 4, ny, wide), jnp.float32),
            pltpu.VMEM((9 * (nx + 4) * kept, wide), jnp.float32),
            pltpu.VMEM((9 * (nx + 4) * kept, wide), jnp.float32),
            pltpu.VMEM((3, nx // 2, ny // 2, nz // 2), jnp.float32),
        ],
        compiler_params=pltpu.CompilerParams(vmem_limit_bytes=24 * MIB),
    )(approx, *halo, jnp.asarray(third_table(nz, wide)))


def level_approx(approx, halo):
    _, nx, ny, nz = approx.shape
    mx, half, lanes = nx // 2, ny // 2, nz // 2
    f32 = lambda *shape: jax.ShapeDtypeStruct(shape, jnp.float32)
    vmem = pl.BlockSpec(memory_space=pltpu.VMEM)
    params = pltpu.CompilerParams(vmem_limit_bytes=24 * MIB)
    table = jnp.asarray(third_table(nz, nz))
    own = pl.pallas_call(
        lambda *refs: level_own_kernel(nz, *refs),
        in_specs=[vmem] * 4,
        out_specs=vmem,
        out_shape=f32(9, nx, half, nz),
        scratch_shapes=[pltpu.VMEM((9 * nx * half, nz), jnp.float32)],
        compiler_params=params,
        name="level_own",
    )(approx, *halo[2:], table)
    sends = ((2, half, lanes), (2, half, lanes), (mx, 2, lanes), (mx, 2, lanes))
    out = [f32(9, mx, half, lanes), f32(6, mx, half, lanes)] + [f32(9, *s) for s in sends]
    return pl.pallas_call(
        lambda *refs: level_approx_kernel(nz, *refs),
        in_specs=[vmem] * 6,
        out_specs=[vmem] * len(out),
        out_shape=out,
        scratch_shapes=[
            pltpu.VMEM((9 * 4 * half, nz), jnp.float32),
            pltpu.VMEM((9 * 4 * half, nz), jnp.float32),
            pltpu.VMEM((3, mx, half, lanes), jnp.float32),
        ],
        compiler_params=params,
        name="level_approx",
    )(own, *halo, table)


def level_details(approx, halo, last):
    _, nx, ny, nz = approx.shape
    mx, half, lanes = nx // 2, ny // 2, nz // 2
    f32 = lambda *shape: jax.ShapeDtypeStruct(shape, jnp.float32)
    out = [f32(7, 9, mx, half, lanes)]
    if last:
        out += [f32(6, mx, half, lanes), f32(3, mx, half, lanes)]
    return level_call(lambda *refs: level_detail_kernel(nz, last, *refs), approx, halo, out, ny)


def halo_rows(before, after, down, up):
    rows = before.shape[2]
    cell = lambda at: jnp.concatenate([before[:, :, at : at + 1], after[:, :, at : at + 1]], axis=1)
    p, q = parts_for_next([cell(rows - 4 + i) for i in range(4)])
    down = jnp.concatenate([down, jnp.concatenate([q, p], axis=2)], axis=1)
    head = jnp.concatenate(parts_for_previous([cell(i) for i in range(3)]), axis=2)
    up = jnp.concatenate([up, head], axis=1)
    return shifted(down, "gy", 1), shifted(up, "gy", -1)


def exchange(to_next, to_prev, edge_next, edge_prev, down, up):
    from_prev_edge = shifted(edge_next, "gx", 1)
    from_next_edge = shifted(edge_prev, "gx", -1)
    before = shifted(to_next, "gx", 1)
    after = shifted(to_prev, "gx", -1)
    down = jnp.concatenate([down, from_prev_edge[:, :, 0:2], from_next_edge[:, :, 0:2]], axis=1)
    up = jnp.concatenate([up, from_prev_edge[:, :, 2:4], from_next_edge[:, :, 2:4]], axis=1)
    return before, after, shifted(down, "gy", 1), shifted(up, "gy", -1)


def body(velocity):
    _, nx, ny, nz = velocity.shape
    table = jnp.asarray(third_table(nz, nz))
    tail, head = velocity[:, nx - BEFORE :], velocity[:, :AFTER]
    edges = lambda t: jnp.concatenate([t[:, :, :8], t[:, :, ny - 8 :]], axis=2)
    edge_before = shifted(edges(tail), "gx", 1)
    edge_after = shifted(edges(head), "gx", -1)
    mid_before = shifted(tail[:, :, 8 : ny - 8], "gx", 1)
    mid_after = shifted(head[:, :, 8 : ny - 8], "gx", -1)
    own_before = shifted(velocity[:, :, ny - BEFORE :], "gy", 1)
    own_after = shifted(velocity[:, :, :AFTER], "gy", -1)
    low_one, rest_one = local_pass(velocity, own_before, own_after, table, 0)
    edge_before, edge_after, low_one = lax.optimization_barrier((edge_before, edge_after, low_one))
    down = jnp.concatenate([edge_before[:, :, 12:], edge_after[:, :, 12:]], axis=1)
    up = jnp.concatenate([edge_before[:, :, :AFTER], edge_after[:, :, :AFTER]], axis=1)
    row_before = shifted(down, "gy", 1)
    row_after = shifted(up, "gy", -1)
    low_two, rest_two = local_pass(velocity, own_before, own_after, table, nx // 2)
    low_before, rest_before = halo_pass((edge_before, mid_before, row_before, row_after), table)
    halo = (edge_after, mid_after, row_before, row_after)
    approx, high, stress_one, *sends = approx_pass((low_one, low_two), low_before, halo, table)
    second_halo = exchange(*sends)
    details_one = detail_pass((rest_one, rest_two), rest_before, high, halo, table)
    approx, details_one = lax.optimization_barrier((approx, details_one))
    second = approx
    approx, stress_two, *sends = level_approx(second, second_halo)
    before = shifted(sends[0], "gx", 1)
    after = shifted(sends[1], "gx", -1)
    (details_two,) = level_details(second, second_halo, False)
    before, after, details_two = lax.optimization_barrier((before, after, details_two))
    third_halo = (before, after) + halo_rows(before, after, *sends[2:])
    details_three, stress_three, coarse = level_details(approx, third_halo, True)
    return details_one, stress_one, details_two, stress_two, details_three, stress_three, coarse


def solution(mesh):
    in_specs = (P(None, "gx", "gy", None),)
    out_specs = (
        P(None, None, "gx", "gy", None),
        P(None, "gx", "gy", None),
        P(None, None, "gx", "gy", None),
        P(None, "gx", "gy", None),
        P(None, None, "gx", "gy", None),
        P(None, "gx", "gy", None),
        P(None, "gx", "gy", None),
    )
    return jax.shard_map(body, mesh=mesh, in_specs=in_specs, out_specs=out_specs, check_vma=False)
```

```python
import jax
import jax.numpy as jnp
import numpy as np
from jax import lax
from jax.experimental import pallas as pl
from jax.experimental.pallas import tpu as pltpu
from jax.sharding import PartitionSpec as P

predict_one = -1.586134342
update_one = -0.05298011854
predict_two = 0.8829110762
update_two = 0.4435068522
scaling = 1.149604398
product_pairs = ((0, 0), (0, 1), (0, 2), (1, 1), (1, 2), (2, 2))
BEFORE = 4
AFTER = 3
GROUP = 3
MIB = 1 << 20


def shifted(block, axis, distance):
    size = lax.axis_size(axis)
    return lax.ppermute(block, axis, [(i, (i + distance) % size) for i in range(size)])


def third_table(length, lanes):
    eye = np.eye(length)
    e, o = eye[:, 0::2], eye[:, 1::2]
    following = lambda t: np.concatenate([t[:, 1:], t[:, -1:]], 1)
    preceding = lambda t: np.concatenate([t[:, :1], t[:, :-1]], 1)
    o = o + predict_one * (e + following(e))
    e = e + update_one * (o + preceding(o))
    o = o + predict_two * (e + following(e))
    e = e + update_two * (o + preceding(o))
    table = np.zeros((lanes, lanes))
    table[:length, : length // 2] = e * scaling
    table[:length, lanes // 2 : lanes // 2 + length // 2] = o / scaling
    return table.astype(np.float32)


def band_scale(by, bx):
    return float(scaling ** ((1 - 2 * by) + (1 - 2 * bx)))


def dot(a, b):
    a_high, b_high = a.astype(jnp.bfloat16), b.astype(jnp.bfloat16)
    a_low = (a - a_high.astype(jnp.float32)).astype(jnp.bfloat16)
    b_low = (b - b_high.astype(jnp.float32)).astype(jnp.bfloat16)
    part = lambda x, y: jnp.dot(x, y, preferred_element_type=jnp.float32)
    return part(a_high, b_high) + (part(a_high, b_low) + part(a_low, b_high))


def ring_lift(e, o):
    n = e.shape[0]
    up = lambda t: pltpu.roll(t, n - 1, 0)
    down = lambda t: pltpu.roll(t, 1, 0)
    o = o + predict_one * (e + up(e))
    e = e + update_one * (o + down(o))
    o = o + predict_two * (e + up(e))
    e = e + update_two * (o + down(o))
    return e, o


def halo_lift(e, o, p, q, r, s, following, preceding, first, last):
    o1 = o + predict_one * (e + following(e, r))
    o1_before = p + predict_one * first(e)
    e1 = e + update_one * (preceding(o1, o1_before) + o1)
    e1_before = q + update_one * o1_before
    e1_after = r + update_one * (last(o1) + s)
    o2 = o1 + predict_two * (e1 + following(e1, e1_after))
    o2_before = o1_before + predict_two * (e1_before + first(e1))
    e2 = e1 + update_two * (preceding(o2, o2_before) + o2)
    return e2, o2


def halo_lift_list(e, o, p, q, r, s):
    m = len(e)
    e = list(e) + [r]
    o1 = [p + predict_one * e[0]]
    o1 += [o[i] + predict_one * (e[i] + e[i + 1]) for i in range(m)] + [s]
    e1 = [q + update_one * o1[0]]
    e1 += [e[i] + update_one * (o1[i] + o1[i + 1]) for i in range(m + 1)]
    o2 = [o1[i] + predict_two * (e1[i] + e1[i + 1]) for i in range(m + 1)]
    e2 = [e1[i + 1] + update_two * (o2[i] + o2[i + 1]) for i in range(m)]
    return e2, o2[1:]


def sublane_lift(e, o, p, q, r, s):
    n = e.shape[0]
    row = lax.broadcasted_iota(jnp.int32, e.shape, 0)
    following = lambda t, edge: jnp.where(row == n - 1, edge, pltpu.roll(t, n - 1, 0))
    preceding = lambda t, edge: jnp.where(row == 0, edge, pltpu.roll(t, 1, 0))
    return halo_lift(e, o, p, q, r, s, following, preceding, lambda t: t[0:1], lambda t: t[n - 1 : n])


def parts_for_next(c):
    p = c[-1] + predict_one * c[-2]
    q = c[-2] + update_one * (c[-3] + predict_one * (c[-4] + c[-2]))
    return p, q


def parts_for_previous(c):
    return c[0], c[1] + predict_one * (c[0] + c[2])


def row_parts(load, rows):
    tail, head = load(rows - 8), load(0)
    row = lax.broadcasted_iota(jnp.int32, tail.shape, 0)
    inner = tail + predict_one * (pltpu.roll(tail, 1, 0) + pltpu.roll(tail, 7, 0))
    p = tail + predict_one * pltpu.roll(tail, 1, 0)
    q = tail + update_one * pltpu.roll(inner, 1, 0)
    s = head + predict_one * (pltpu.roll(head, 1, 0) + pltpu.roll(head, 7, 0))
    return jnp.where(row == 7, p, q)[6:8], jnp.where(row == 0, head, s)[0:2]


def send_layers(layers, f, at, next_ref, prev_ref):
    for part, value in enumerate(parts_for_next(layers)):
        next_ref[f, part, at : at + 8, :] = value
    for part, value in enumerate(parts_for_previous(layers)):
        prev_ref[f, part, at : at + 8, :] = value


def send_rows(ref, f, down_ref, up_ref):
    for at in range(ref.shape[1]):
        tail, head = row_parts(lambda row: ref[f, at, row : row + 8, :], ref.shape[2])
        down_ref[f, at] = tail
        up_ref[f, at] = head


def local_kernel(v_ref, before_ref, after_ref, table_ref, low_ref, rest_ref, rows_ref, stack_ref):
    ny = v_ref.shape[2]
    half = ny // 2
    lanes = v_ref.shape[3] // 2
    even, odd = [], []
    for c in range(3):
        for h in range(2):
            cut = pl.ds(h * lanes, lanes)
            rows_ref[c, h, 12:16, :] = before_ref[c, 0, :, cut]
            rows_ref[c, h, 16 : 16 + ny, :] = v_ref[c, 0, :, cut]
            rows_ref[c, h, 16 + ny : 16 + ny + AFTER, :] = after_ref[c, 0, :, cut]
    count = half + 16
    for h in range(2):
        even = [rows_ref[c, h, pl.ds(0, count, stride=2), :] for c in range(3)]
        odd = [rows_ref[c, h, pl.ds(1, count, stride=2), :] for c in range(3)]
        for f in range(9):
            if f < 3:
                e, o = even[f], odd[f]
            else:
                i, j = product_pairs[f - 3]
                e, o = even[i] * even[j], odd[i] * odd[j]
            e, o = ring_lift(e, o)
            stack_ref[f * ny : f * ny + half, h * lanes : (h + 1) * lanes] = e[8 : 8 + half]
            stack_ref[f * ny + half : (f + 1) * ny, h * lanes : (h + 1) * lanes] = o[8 : 8 + half]
    out = dot(stack_ref[...], table_ref[...])
    for f in range(9):
        low_ref[f, 0] = out[f * ny : f * ny + half, :lanes]
        rest_ref[0, f, 0] = out[f * ny + half : (f + 1) * ny, :lanes]
        rest_ref[1, f, 0] = out[f * ny : f * ny + half, lanes:]
        rest_ref[2, f, 0] = out[f * ny + half : (f + 1) * ny, lanes:]


def local_pass(velocity, before, after, table, start):
    _, nx, ny, nz = velocity.shape
    nx = nx // 2
    half, lanes = ny // 2, nz // 2
    return pl.pallas_call(
        local_kernel,
        grid=(nx,),
        in_specs=[
            pl.BlockSpec((3, 1, ny, nz), lambda i: (0, i + start, 0, 0)),
            pl.BlockSpec((3, 1, BEFORE, nz), lambda i: (0, i + start, 0, 0)),
            pl.BlockSpec((3, 1, AFTER, nz), lambda i: (0, i + start, 0, 0)),
            pl.BlockSpec((nz, nz), lambda i: (0, 0)),
        ],
        out_specs=[
            pl.BlockSpec((9, 1, half, lanes), lambda i: (0, i, 0, 0)),
            pl.BlockSpec((3, 9, 1, half, lanes), lambda i: (0, 0, i, 0, 0)),
        ],
        out_shape=[
            jax.ShapeDtypeStruct((9, nx, half, lanes), jnp.float32),
            jax.ShapeDtypeStruct((3, 9, nx, half, lanes), jnp.float32),
        ],
        scratch_shapes=[pltpu.VMEM((3, 2, ny + 32, lanes), jnp.float32), pltpu.VMEM((9 * ny, nz), jnp.float32)],
        compiler_params=pltpu.CompilerParams(vmem_limit_bytes=24 * MIB),
        cost_estimate=pl.CostEstimate(flops=9 * nx * ny * nz * 512, bytes_accessed=9 * nx * ny * nz * 6, transcendentals=0),
        name="local_pass",
    )(velocity, before, after, table)


def pair_of(f):
    k = f - 3
    one = jnp.where(k < 3, 0, jnp.where(k < 5, 1, 2))
    two = jnp.where(k < 3, k, jnp.where(k < 5, k - 2, 2))
    return jnp.where(f < 3, f, one), jnp.where(f < 3, 3, two)


def gather_rows(refs, first, rows_ref, even_ref, odd_ref):
    edge, middle, row_before, row_after = refs
    layers, mid = middle.shape[1:3]
    ny = mid + 16
    lanes = rows_ref.shape[2]
    count = ny // 2 + 16
    even_ref[3] = jnp.ones(even_ref.shape[1:], jnp.float32)
    odd_ref[3] = jnp.ones(odd_ref.shape[1:], jnp.float32)
    for c in range(3):
        for layer in range(layers):
            for h in range(2):
                cut = pl.ds(h * lanes, lanes)
                rows_ref[h, 12:16, :] = row_before[c, first + layer, :, cut]
                rows_ref[h, 16:24, :] = edge[c, layer, 0:8, cut]
                rows_ref[h, 24 : 24 + mid, :] = middle[c, layer, :, cut]
                rows_ref[h, 24 + mid : 32 + mid, :] = edge[c, layer, 8:16, cut]
                rows_ref[h, 16 + ny : 16 + ny + AFTER, :] = row_after[c, first + layer, :, cut]
                even_ref[c, layer, :, cut] = rows_ref[h, pl.ds(0, count, stride=2), :]
                odd_ref[c, layer, :, cut] = rows_ref[h, pl.ds(1, count, stride=2), :]


def lift_first(layers, halo):
    return halo_lift_list(layers[0::2], layers[1::2], *halo)


def halo_stack(pairs, both, combine, even_ref, odd_ref, part_ref, stack_ref):
    count, nz = even_ref.shape[2:]
    half, lanes = count - 16, nz // 2
    kinds = 4 if both else 2
    for n, (i, j) in enumerate(pairs):
        for h in range(2):
            cut = slice(h * lanes, (h + 1) * lanes)
            for parity, ref in enumerate((even_ref, odd_ref)):
                for r in range(0, count, 16):
                    rows = slice(r, r + 16)
                    g = [ref[i, layer, rows, cut] * ref[j, layer, rows, cut] for layer in range(ref.shape[1])]
                    for k, value in enumerate(combine(g)):
                        part_ref[parity, k, rows, :] = value
            for k in range(2):
                e, o = ring_lift(part_ref[0, k], part_ref[1, k])
                at = (kinds * n + k) * half
                stack_ref[at : at + half, cut] = e[8 : 8 + half]
                if both:
                    at += 2 * half
                    stack_ref[at : at + half, cut] = o[8 : 8 + half]


def halo_kernel(*refs):
    table_ref, low_ref, rest_ref = refs[4:7]
    rows_ref, even_ref, odd_ref, part_ref, stack_ref = refs[7:]
    half, lanes = low_ref.shape[2:]
    gather_rows(refs[:4], 0, rows_ref, even_ref, odd_ref)

    def group(g, carry):
        pairs = [pair_of(g * GROUP + n) for n in range(GROUP)]
        halo_stack(pairs, True, parts_for_next, even_ref, odd_ref, part_ref, stack_ref)
        stack_ref[...] = dot(stack_ref[...], table_ref[...])
        for n in range(GROUP):
            for k in range(2):
                low, high = (slice((4 * n + k + m) * half, (4 * n + k + m + 1) * half) for m in (0, 2))
                low_ref[g * GROUP + n, k] = stack_ref[low, :lanes]
                rest_ref[0, g * GROUP + n, k] = stack_ref[high, :lanes]
                rest_ref[1, g * GROUP + n, k] = stack_ref[low, lanes:]
                rest_ref[2, g * GROUP + n, k] = stack_ref[high, lanes:]
        return carry

    lax.fori_loop(0, 9 // GROUP, group, 0)


def halo_pass(halo, table):
    half, lanes = (halo[1].shape[2] + 16) // 2, halo[1].shape[3] // 2
    vmem = pl.BlockSpec(memory_space=pltpu.VMEM)
    return pl.pallas_call(
        halo_kernel,
        in_specs=[vmem] * 5,
        out_specs=[vmem] * 2,
        out_shape=[
            jax.ShapeDtypeStruct((9, 2, half, lanes), jnp.float32),
            jax.ShapeDtypeStruct((3, 9, 2, half, lanes), jnp.float32),
        ],
        scratch_shapes=halo_scratch(half, lanes, BEFORE, True),
        compiler_params=pltpu.CompilerParams(vmem_limit_bytes=24 * MIB),
        name="halo_pass",
    )(*halo, table)


def layer_list(refs, index, rows):
    return [ref[index + (x, rows)] for ref in refs for x in range(ref.shape[len(index)])]


def approx_kernel(*refs):
    low_refs, before_ref, table_ref = refs[:2], refs[2], refs[3]
    halo_refs = refs[4:8]
    approx_ref, high_ref, stress_ref = refs[8:11]
    next_ref, prev_ref, next_edge_ref, prev_edge_ref, down_ref, up_ref = refs[11:17]
    rows_ref, even_ref, odd_ref, part_ref, stack_ref, kept_ref, out_ref = refs[17:]
    f = pl.program_id(0)
    half, lanes = low_refs[0].shape[2:]
    mx = approx_ref.shape[1]

    @pl.when(f == 0)
    def _():
        gather_rows(halo_refs, BEFORE, rows_ref, even_ref, odd_ref)

    pairs = [pair_of(f * GROUP + n) for n in range(GROUP)]
    halo_stack(pairs, False, parts_for_previous, even_ref, odd_ref, part_ref, stack_ref)
    out_ref[...] = dot(stack_ref[...], table_ref[:, :lanes])
    for n in range(GROUP):
        for r in range(0, half, 8):
            rows = slice(r, r + 8)
            halo = [before_ref[n, k, rows, :] for k in range(2)]
            halo += [out_ref[(2 * n + k) * half + r : (2 * n + k) * half + r + 8, :] for k in range(2)]
            e, o = lift_first(layer_list(low_refs, (n,), rows), halo)
            e = [t * band_scale(0, 0) for t in e]
            for x in range(mx):
                approx_ref[n, x, rows, :] = e[x]
                high_ref[n, x, rows, :] = o[x] * band_scale(0, 1)
            send_layers(e, n, r, next_ref, prev_ref)
        send_rows(approx_ref, n, down_ref, up_ref)
        for ref, edge_ref in ((next_ref, next_edge_ref), (prev_ref, prev_edge_ref)):
            for part in range(2):
                tail, head = row_parts(lambda row: ref[n, part, row : row + 8, :], half)
                edge_ref[n, part, 0:2, :] = tail
                edge_ref[n, part, 2:4, :] = head

    @pl.when(f == 0)
    def _():
        kept_ref[...] = approx_ref[...]

    @pl.when(f > 0)
    def _():
        for n, (i, j) in enumerate(pairs):
            for x in range(mx):
                stress_ref[n, x] = approx_ref[n, x] - kept_ref[i, x] * kept_ref[j, x]


def whole(shape):
    return pl.BlockSpec(shape, lambda f: (0,) * len(shape))


def per_field(shape):
    return pl.BlockSpec((GROUP,) + shape, lambda f: (f,) + (0,) * len(shape))


def approx_pass(lows, before, halo, table):
    _, nx, half, lanes = lows[0].shape
    nz, mx = 2 * lanes, nx
    f32 = lambda *shape: jax.ShapeDtypeStruct(shape, jnp.float32)
    sends = [(2, half, lanes), (2, half, lanes), (2, 4, lanes), (2, 4, lanes), (mx, 2, lanes), (mx, 2, lanes)]
    return pl.pallas_call(
        approx_kernel,
        grid=(9 // GROUP,),
        in_specs=[per_field((nx, half, lanes))] * 2
        + [per_field((2, half, lanes)), whole((nz, nz))]
        + [whole(h.shape) for h in halo],
        out_specs=[
            per_field((mx, half, lanes)),
            per_field((mx, half, lanes)),
            pl.BlockSpec((GROUP, mx, half, lanes), lambda f: (jnp.maximum(f - 1, 0), 0, 0, 0)),
        ]
        + [per_field(s) for s in sends],
        out_shape=[f32(9, mx, half, lanes), f32(9, mx, half, lanes), f32(6, mx, half, lanes)] + [f32(9, *s) for s in sends],
        scratch_shapes=halo_scratch(half, lanes, AFTER, False)
        + [
            pltpu.VMEM((3, mx, half, lanes), jnp.float32),
            pltpu.VMEM((GROUP * 2 * half, lanes), jnp.float32),
        ],
        compiler_params=pltpu.CompilerParams(vmem_limit_bytes=24 * MIB),
        name="approx_pass",
    )(*lows, before, table, *halo)


def halo_scratch(half, lanes, layers, both):
    return [
        pltpu.VMEM((2, 2 * half + 32, lanes), jnp.float32),
        pltpu.VMEM((4, layers, half + 16, 2 * lanes), jnp.float32),
        pltpu.VMEM((4, layers, half + 16, 2 * lanes), jnp.float32),
        pltpu.VMEM((2, 2, half + 16, lanes), jnp.float32),
        pltpu.VMEM((GROUP * (4 if both else 2) * half, 2 * lanes), jnp.float32),
    ]


def detail_kernel(*refs):
    rest_refs, before_ref, high_ref, table_ref = refs[:2], refs[2], refs[3], refs[4]
    halo_refs = refs[5:9]
    out_ref, rows_ref, even_ref, odd_ref, part_ref, stack_ref = refs[9:]
    f = pl.program_id(0)
    half, lanes = high_ref.shape[2:]
    mx = high_ref.shape[1]

    @pl.when(f == 0)
    def _():
        gather_rows(halo_refs, BEFORE, rows_ref, even_ref, odd_ref)

    pairs = [pair_of(f * GROUP + n) for n in range(GROUP)]
    halo_stack(pairs, True, parts_for_previous, even_ref, odd_ref, part_ref, stack_ref)
    stack_ref[...] = dot(stack_ref[...], table_ref[...])
    for n in range(GROUP):
        for x in range(mx):
            out_ref[0, n, x] = high_ref[n, x]
        for band, (bz, by) in enumerate(((0, 1), (1, 0), (1, 1))):
            plane = 4 * bz + 2 * by - 1
            for r in range(0, half, 8):
                rows = slice(r, r + 8)
                halo = [before_ref[band, n, k, rows, :] for k in range(2)]
                for k in range(2):
                    at = (4 * n + 2 * by + k) * half + r
                    halo.append(stack_ref[at : at + 8, bz * lanes : (bz + 1) * lanes])
                e, o = lift_first(layer_list(rest_refs, (band, n), rows), halo)
                for x in range(mx):
                    out_ref[plane, n, x, rows, :] = e[x] * band_scale(by, 0)
                    out_ref[plane + 1, n, x, rows, :] = o[x] * band_scale(by, 1)


def detail_pass(rests, before, high, halo, table):
    _, mx, half, lanes = high.shape
    nz = 2 * lanes
    return pl.pallas_call(
        detail_kernel,
        grid=(9 // GROUP,),
        in_specs=[pl.BlockSpec((3, GROUP, mx, half, lanes), lambda f: (0, f, 0, 0, 0))] * 2
        + [pl.BlockSpec((3, GROUP, 2, half, lanes), lambda f: (0, f, 0, 0, 0)), per_field((mx, half, lanes)), whole((nz, nz))]
        + [whole(h.shape) for h in halo],
        out_specs=pl.BlockSpec((7, GROUP, mx, half, lanes), lambda f: (0, f, 0, 0, 0)),
        out_shape=jax.ShapeDtypeStruct((7, 9, mx, half, lanes), jnp.float32),
        scratch_shapes=halo_scratch(half, lanes, AFTER, True),
        compiler_params=pltpu.CompilerParams(vmem_limit_bytes=24 * MIB),
        cost_estimate=pl.CostEstimate(flops=18 * mx * half * nz * 200, bytes_accessed=18 * mx * half * nz * 16, transcendentals=0),
        name="detail_pass",
    )(*rests, before, high, table, *halo)


def level_rows(refs, nz, nx, span, lows, pad_ref, stack_ref):
    a_ref, before_ref, after_ref, down_ref, up_ref = refs
    ny = (before_ref if a_ref is None else a_ref).shape[2]
    half = ny // 2
    wide = stack_ref.shape[1]
    kept = half if lows else ny
    if nz < wide:
        pad_ref[...] = jnp.zeros_like(pad_ref)
    for f in range(9):
        for step, layer in enumerate(span):
            if layer < nx:
                source, at = a_ref, layer
            elif layer < nx + 2:
                source, at = before_ref, layer - nx
            else:
                source, at = after_ref, layer - nx - 2
            if nz < wide:
                pad_ref[f, layer, :, :nz] = source[f, at]
                source, at = pad_ref, layer
            e = source[f, at, pl.ds(0, half, stride=2), :]
            o = source[f, at, pl.ds(1, half, stride=2), :]
            rows = [down_ref[f, layer, 1:2, :], down_ref[f, layer, 0:1, :], up_ref[f, layer, 0:1, :], up_ref[f, layer, 1:2, :]]
            if nz < wide:
                rows = [jnp.concatenate([row, jnp.zeros((1, wide - nz), jnp.float32)], axis=1) for row in rows]
            e, o = sublane_lift(e, o, *rows)
            at = (f * len(span) + step) * kept
            stack_ref[at : at + half, :] = e
            if not lows:
                stack_ref[at + half : at + ny, :] = o


def level_own_kernel(nz, a_ref, down_ref, up_ref, table_ref, own_ref, stack_ref):
    nx, _ = a_ref.shape[1:3]
    level_rows((a_ref, None, None, down_ref, up_ref), nz, nx, range(nx), True, None, stack_ref)
    own_ref[...] = dot(stack_ref[...], table_ref[...]).reshape(own_ref.shape)


def level_approx_kernel(nz, *refs):
    own_ref, table_ref, approx_ref, stress_ref = refs[0], refs[5], refs[6], refs[7]
    sends, (stack_ref, out_ref, kept_ref) = refs[8:-3], refs[-3:]
    nx, half = own_ref.shape[1:3]
    lanes = nz // 2
    level_rows((None,) + refs[1:5], nz, nx, range(nx, nx + 4), True, None, stack_ref)
    out_ref[...] = dot(stack_ref[...], table_ref[...])
    mx = nx // 2
    for f in range(9):
        for r in range(0, half, 8):
            rows = slice(r, r + 8)
            halo = []
            for k in range(4):
                at = (f * 4 + k) * half + r
                halo.append(out_ref[at : at + 8, :])
            low, _ = lift_first([own_ref[f, x, rows, :] for x in range(nx)], halo)
            approx = [(t * band_scale(0, 0))[:, :lanes] for t in low]
            for x in range(mx):
                if f < 3:
                    kept_ref[f, x, rows, :] = approx[x]
                else:
                    i, j = product_pairs[f - 3]
                    stress_ref[f - 3, x, rows, :] = approx[x] - kept_ref[i, x, rows, :] * kept_ref[j, x, rows, :]
                approx_ref[f, x, rows, :] = approx[x]
            send_layers(approx, f, r, sends[0], sends[1])
        send_rows(approx_ref, f, sends[2], sends[3])


def level_detail_kernel(nz, last, *refs):
    table_ref, detail_ref = refs[5:7]
    pad_ref, stack_ref, out_ref, kept_ref = refs[-4:]
    nx, ny = refs[0].shape[1:3]
    half, lanes = ny // 2, nz // 2
    wide = stack_ref.shape[1]
    level_rows(refs[:5], nz, nx, range(nx + 4), False, pad_ref, stack_ref)
    out_ref[...] = dot(stack_ref[...], table_ref[...])
    for f in range(9):
        for by in range(2):
            for r in range(0, half, 8):
                rows = slice(r, r + 8)
                layers = []
                for layer in range(nx + 4):
                    at = (f * (nx + 4) + layer) * ny + by * half + r
                    layers.append(out_ref[at : at + 8, :])
                low, high = lift_first(layers[:nx], layers[nx:])
                for x in range(nx // 2):
                    for bx, value in enumerate((low[x], high[x])):
                        t = value * band_scale(by, bx)
                        for bz in range(2):
                            band = 4 * bz + 2 * by + bx
                            piece = t[:, bz * (wide // 2) : bz * (wide // 2) + lanes]
                            if band:
                                detail_ref[band - 1, f, x, rows, :] = piece
                            elif last:
                                stress_ref, approx_ref = refs[7:9]
                                if f < 3:
                                    kept_ref[f, x, rows, :] = piece
                                    approx_ref[f, x, rows, :] = piece
                                else:
                                    i, j = product_pairs[f - 3]
                                    stress_ref[f - 3, x, rows, :] = piece - kept_ref[i, x, rows, :] * kept_ref[j, x, rows, :]


def level_call(kernel, approx, halo, out, kept):
    _, nx, ny, nz = approx.shape
    wide = max(nz, 128)
    vmem = pl.BlockSpec(memory_space=pltpu.VMEM)
    return pl.pallas_call(
        kernel,
        in_specs=[vmem] * 6,
        out_specs=[vmem] * len(out),
        out_shape=out,
        scratch_shapes=[
            pltpu.VMEM((9, nx + 4, ny, wide), jnp.float32),
            pltpu.VMEM((9 * (nx + 4) * kept, wide), jnp.float32),
            pltpu.VMEM((9 * (nx + 4) * kept, wide), jnp.float32),
            pltpu.VMEM((3, nx // 2, ny // 2, nz // 2), jnp.float32),
        ],
        compiler_params=pltpu.CompilerParams(vmem_limit_bytes=24 * MIB),
    )(approx, *halo, jnp.asarray(third_table(nz, wide)))


def level_approx(approx, halo):
    _, nx, ny, nz = approx.shape
    mx, half, lanes = nx // 2, ny // 2, nz // 2
    f32 = lambda *shape: jax.ShapeDtypeStruct(shape, jnp.float32)
    vmem = pl.BlockSpec(memory_space=pltpu.VMEM)
    params = pltpu.CompilerParams(vmem_limit_bytes=24 * MIB)
    table = jnp.asarray(third_table(nz, nz))
    own = pl.pallas_call(
        lambda *refs: level_own_kernel(nz, *refs),
        in_specs=[vmem] * 4,
        out_specs=vmem,
        out_shape=f32(9, nx, half, nz),
        scratch_shapes=[pltpu.VMEM((9 * nx * half, nz), jnp.float32)],
        compiler_params=params,
        name="level_own",
    )(approx, *halo[2:], table)
    sends = ((2, half, lanes), (2, half, lanes), (mx, 2, lanes), (mx, 2, lanes))
    out = [f32(9, mx, half, lanes), f32(6, mx, half, lanes)] + [f32(9, *s) for s in sends]
    return pl.pallas_call(
        lambda *refs: level_approx_kernel(nz, *refs),
        in_specs=[vmem] * 6,
        out_specs=[vmem] * len(out),
        out_shape=out,
        scratch_shapes=[
            pltpu.VMEM((9 * 4 * half, nz), jnp.float32),
            pltpu.VMEM((9 * 4 * half, nz), jnp.float32),
            pltpu.VMEM((3, mx, half, lanes), jnp.float32),
        ],
        compiler_params=params,
        name="level_approx",
    )(own, *halo, table)


def level_details(approx, halo, last):
    _, nx, ny, nz = approx.shape
    mx, half, lanes = nx // 2, ny // 2, nz // 2
    f32 = lambda *shape: jax.ShapeDtypeStruct(shape, jnp.float32)
    out = [f32(7, 9, mx, half, lanes)]
    if last:
        out += [f32(6, mx, half, lanes), f32(3, mx, half, lanes)]
    return level_call(lambda *refs: level_detail_kernel(nz, last, *refs), approx, halo, out, ny)


def halo_rows(before, after, down, up):
    rows = before.shape[2]
    cell = lambda at: jnp.concatenate([before[:, :, at : at + 1], after[:, :, at : at + 1]], axis=1)
    p, q = parts_for_next([cell(rows - 4 + i) for i in range(4)])
    down = jnp.concatenate([down, jnp.concatenate([q, p], axis=2)], axis=1)
    head = jnp.concatenate(parts_for_previous([cell(i) for i in range(3)]), axis=2)
    up = jnp.concatenate([up, head], axis=1)
    return shifted(down, "gy", 1), shifted(up, "gy", -1)


def exchange(to_next, to_prev, edge_next, edge_prev, down, up, meanwhile):
    from_prev = shifted(edge_next, "gx", 1)
    from_next = shifted(edge_prev, "gx", -1)
    before = shifted(to_next, "gx", 1)
    after = shifted(to_prev, "gx", -1)
    from_prev, from_next, result = lax.optimization_barrier((from_prev, from_next, meanwhile()))
    down = jnp.concatenate([down, from_prev[:, :, 0:2], from_next[:, :, 0:2]], axis=1)
    up = jnp.concatenate([up, from_prev[:, :, 2:4], from_next[:, :, 2:4]], axis=1)
    return (before, after, shifted(down, "gy", 1), shifted(up, "gy", -1)), result


def body(velocity):
    _, nx, ny, nz = velocity.shape
    table = jnp.asarray(third_table(nz, nz))
    tail, head = velocity[:, nx - BEFORE :], velocity[:, :AFTER]
    edges = lambda t: jnp.concatenate([t[:, :, :8], t[:, :, ny - 8 :]], axis=2)
    edge_before = shifted(edges(tail), "gx", 1)
    edge_after = shifted(edges(head), "gx", -1)
    mid_before = shifted(tail[:, :, 8 : ny - 8], "gx", 1)
    mid_after = shifted(head[:, :, 8 : ny - 8], "gx", -1)
    own_before = shifted(velocity[:, :, ny - BEFORE :], "gy", 1)
    own_after = shifted(velocity[:, :, :AFTER], "gy", -1)
    low_one, rest_one = local_pass(velocity, own_before, own_after, table, 0)
    low_two, rest_two = local_pass(velocity, own_before, own_after, table, nx // 2)
    edge_before, edge_after, low_one, low_two = lax.optimization_barrier((edge_before, edge_after, low_one, low_two))
    down = jnp.concatenate([edge_before[:, :, 12:], edge_after[:, :, 12:]], axis=1)
    up = jnp.concatenate([edge_before[:, :, :AFTER], edge_after[:, :, :AFTER]], axis=1)
    row_before = shifted(down, "gy", 1)
    row_after = shifted(up, "gy", -1)
    low_before, rest_before = halo_pass((edge_before, mid_before, row_before, row_after), table)
    halo = (edge_after, mid_after, row_before, row_after)
    approx, high, stress_one, *sends = approx_pass((low_one, low_two), low_before, halo, table)
    second_halo, details_one = exchange(
        *sends, lambda: detail_pass((rest_one, rest_two), rest_before, high, halo, table)
    )
    second = approx
    approx, stress_two, *sends = level_approx(second, second_halo)
    before = shifted(sends[0], "gx", 1)
    after = shifted(sends[1], "gx", -1)
    (details_two,) = level_details(second, second_halo, False)
    before, after, details_two = lax.optimization_barrier((before, after, details_two))
    third_halo = (before, after) + halo_rows(before, after, *sends[2:])
    details_three, stress_three, coarse = level_details(approx, third_halo, True)
    return details_one, stress_one, details_two, stress_two, details_three, stress_three, coarse


def solution(mesh):
    in_specs = (P(None, "gx", "gy", None),)
    out_specs = (
        P(None, None, "gx", "gy", None),
        P(None, "gx", "gy", None),
        P(None, None, "gx", "gy", None),
        P(None, "gx", "gy", None),
        P(None, None, "gx", "gy", None),
        P(None, "gx", "gy", None),
        P(None, "gx", "gy", None),
    )
    return jax.shard_map(body, mesh=mesh, in_specs=in_specs, out_specs=out_specs, check_vma=False)
```

```python
import jax
import jax.numpy as jnp
import numpy as np
from jax import lax
from jax.experimental import pallas as pl
from jax.experimental.pallas import tpu as pltpu
from jax.sharding import PartitionSpec as P

predict_one = -1.586134342
update_one = -0.05298011854
predict_two = 0.8829110762
update_two = 0.4435068522
scaling = 1.149604398
product_pairs = ((0, 0), (0, 1), (0, 2), (1, 1), (1, 2), (2, 2))
BEFORE = 4
AFTER = 3
GROUP = 3
MIB = 1 << 20


def shifted(block, axis, distance):
    size = lax.axis_size(axis)
    return lax.ppermute(block, axis, [(i, (i + distance) % size) for i in range(size)])


def third_table(length, lanes):
    eye = np.eye(length)
    e, o = eye[:, 0::2], eye[:, 1::2]
    following = lambda t: np.concatenate([t[:, 1:], t[:, -1:]], 1)
    preceding = lambda t: np.concatenate([t[:, :1], t[:, :-1]], 1)
    o = o + predict_one * (e + following(e))
    e = e + update_one * (o + preceding(o))
    o = o + predict_two * (e + following(e))
    e = e + update_two * (o + preceding(o))
    table = np.zeros((lanes, lanes))
    table[:length, : length // 2] = e * scaling
    table[:length, lanes // 2 : lanes // 2 + length // 2] = o / scaling
    return table.astype(np.float32)


def band_scale(by, bx):
    return float(scaling ** ((1 - 2 * by) + (1 - 2 * bx)))


def dot(a, b):
    a_high, b_high = a.astype(jnp.bfloat16), b.astype(jnp.bfloat16)
    a_low = (a - a_high.astype(jnp.float32)).astype(jnp.bfloat16)
    b_low = (b - b_high.astype(jnp.float32)).astype(jnp.bfloat16)
    part = lambda x, y: jnp.dot(x, y, preferred_element_type=jnp.float32)
    return part(a_high, b_high) + (part(a_high, b_low) + part(a_low, b_high))


def ring_lift(e, o):
    n = e.shape[0]
    up = lambda t: pltpu.roll(t, n - 1, 0)
    down = lambda t: pltpu.roll(t, 1, 0)
    o = o + predict_one * (e + up(e))
    e = e + update_one * (o + down(o))
    o = o + predict_two * (e + up(e))
    e = e + update_two * (o + down(o))
    return e, o


def halo_lift(e, o, p, q, r, s, following, preceding, first, last):
    o1 = o + predict_one * (e + following(e, r))
    o1_before = p + predict_one * first(e)
    e1 = e + update_one * (preceding(o1, o1_before) + o1)
    e1_before = q + update_one * o1_before
    e1_after = r + update_one * (last(o1) + s)
    o2 = o1 + predict_two * (e1 + following(e1, e1_after))
    o2_before = o1_before + predict_two * (e1_before + first(e1))
    e2 = e1 + update_two * (preceding(o2, o2_before) + o2)
    return e2, o2


def halo_lift_list(e, o, p, q, r, s):
    m = len(e)
    e = list(e) + [r]
    o1 = [p + predict_one * e[0]]
    o1 += [o[i] + predict_one * (e[i] + e[i + 1]) for i in range(m)] + [s]
    e1 = [q + update_one * o1[0]]
    e1 += [e[i] + update_one * (o1[i] + o1[i + 1]) for i in range(m + 1)]
    o2 = [o1[i] + predict_two * (e1[i] + e1[i + 1]) for i in range(m + 1)]
    e2 = [e1[i + 1] + update_two * (o2[i] + o2[i + 1]) for i in range(m)]
    return e2, o2[1:]


def sublane_lift(e, o, p, q, r, s):
    n = e.shape[0]
    row = lax.broadcasted_iota(jnp.int32, e.shape, 0)
    following = lambda t, edge: jnp.where(row == n - 1, edge, pltpu.roll(t, n - 1, 0))
    preceding = lambda t, edge: jnp.where(row == 0, edge, pltpu.roll(t, 1, 0))
    return halo_lift(e, o, p, q, r, s, following, preceding, lambda t: t[0:1], lambda t: t[n - 1 : n])


def parts_for_next(c):
    p = c[-1] + predict_one * c[-2]
    q = c[-2] + update_one * (c[-3] + predict_one * (c[-4] + c[-2]))
    return p, q


def parts_for_previous(c):
    return c[0], c[1] + predict_one * (c[0] + c[2])


def row_parts(load, rows):
    tail, head = load(rows - 8), load(0)
    row = lax.broadcasted_iota(jnp.int32, tail.shape, 0)
    inner = tail + predict_one * (pltpu.roll(tail, 1, 0) + pltpu.roll(tail, 7, 0))
    p = tail + predict_one * pltpu.roll(tail, 1, 0)
    q = tail + update_one * pltpu.roll(inner, 1, 0)
    s = head + predict_one * (pltpu.roll(head, 1, 0) + pltpu.roll(head, 7, 0))
    return jnp.where(row == 7, p, q)[6:8], jnp.where(row == 0, head, s)[0:2]


def send_layers(layers, f, at, next_ref, prev_ref):
    for part, value in enumerate(parts_for_next(layers)):
        next_ref[f, part, at : at + 8, :] = value
    for part, value in enumerate(parts_for_previous(layers)):
        prev_ref[f, part, at : at + 8, :] = value


def send_rows(ref, f, down_ref, up_ref):
    for at in range(ref.shape[1]):
        tail, head = row_parts(lambda row: ref[f, at, row : row + 8, :], ref.shape[2])
        down_ref[f, at] = tail
        up_ref[f, at] = head


def local_kernel(v_ref, before_ref, after_ref, table_ref, low_ref, rest_ref, rows_ref, stack_ref):
    ny = v_ref.shape[2]
    half = ny // 2
    lanes = v_ref.shape[3] // 2
    even, odd = [], []
    for c in range(3):
        for h in range(2):
            cut = pl.ds(h * lanes, lanes)
            rows_ref[c, h, 12:16, :] = before_ref[c, 0, :, cut]
            rows_ref[c, h, 16 : 16 + ny, :] = v_ref[c, 0, :, cut]
            rows_ref[c, h, 16 + ny : 16 + ny + AFTER, :] = after_ref[c, 0, :, cut]
    count = half + 16
    for h in range(2):
        even = [rows_ref[c, h, pl.ds(0, count, stride=2), :] for c in range(3)]
        odd = [rows_ref[c, h, pl.ds(1, count, stride=2), :] for c in range(3)]
        for f in range(9):
            if f < 3:
                e, o = even[f], odd[f]
            else:
                i, j = product_pairs[f - 3]
                e, o = even[i] * even[j], odd[i] * odd[j]
            e, o = ring_lift(e, o)
            stack_ref[f * ny : f * ny + half, h * lanes : (h + 1) * lanes] = e[8 : 8 + half]
            stack_ref[f * ny + half : (f + 1) * ny, h * lanes : (h + 1) * lanes] = o[8 : 8 + half]
    out = dot(stack_ref[...], table_ref[...])
    for f in range(9):
        low_ref[f, 0] = out[f * ny : f * ny + half, :lanes]
        rest_ref[0, f, 0] = out[f * ny + half : (f + 1) * ny, :lanes]
        rest_ref[1, f, 0] = out[f * ny : f * ny + half, lanes:]
        rest_ref[2, f, 0] = out[f * ny + half : (f + 1) * ny, lanes:]


def local_pass(velocity, before, after, table, start):
    _, nx, ny, nz = velocity.shape
    nx = nx // 2
    half, lanes = ny // 2, nz // 2
    return pl.pallas_call(
        local_kernel,
        grid=(nx,),
        in_specs=[
            pl.BlockSpec((3, 1, ny, nz), lambda i: (0, i + start, 0, 0)),
            pl.BlockSpec((3, 1, BEFORE, nz), lambda i: (0, i + start, 0, 0)),
            pl.BlockSpec((3, 1, AFTER, nz), lambda i: (0, i + start, 0, 0)),
            pl.BlockSpec((nz, nz), lambda i: (0, 0)),
        ],
        out_specs=[
            pl.BlockSpec((9, 1, half, lanes), lambda i: (0, i, 0, 0)),
            pl.BlockSpec((3, 9, 1, half, lanes), lambda i: (0, 0, i, 0, 0)),
        ],
        out_shape=[
            jax.ShapeDtypeStruct((9, nx, half, lanes), jnp.float32),
            jax.ShapeDtypeStruct((3, 9, nx, half, lanes), jnp.float32),
        ],
        scratch_shapes=[pltpu.VMEM((3, 2, ny + 32, lanes), jnp.float32), pltpu.VMEM((9 * ny, nz), jnp.float32)],
        compiler_params=pltpu.CompilerParams(vmem_limit_bytes=24 * MIB),
        cost_estimate=pl.CostEstimate(flops=9 * nx * ny * nz * 512, bytes_accessed=9 * nx * ny * nz * 6, transcendentals=0),
        name="local_pass",
    )(velocity, before, after, table)


def pair_of(f):
    k = f - 3
    one = jnp.where(k < 3, 0, jnp.where(k < 5, 1, 2))
    two = jnp.where(k < 3, k, jnp.where(k < 5, k - 2, 2))
    return jnp.where(f < 3, f, one), jnp.where(f < 3, 3, two)


def gather_rows(refs, first, rows_ref, even_ref, odd_ref):
    edge, middle, row_before, row_after = refs
    layers, mid = middle.shape[1:3]
    ny = mid + 16
    lanes = rows_ref.shape[2]
    count = ny // 2 + 16
    even_ref[3] = jnp.ones(even_ref.shape[1:], jnp.float32)
    odd_ref[3] = jnp.ones(odd_ref.shape[1:], jnp.float32)
    for c in range(3):
        for layer in range(layers):
            for h in range(2):
                cut = pl.ds(h * lanes, lanes)
                rows_ref[h, 12:16, :] = row_before[c, first + layer, :, cut]
                rows_ref[h, 16:24, :] = edge[c, layer, 0:8, cut]
                rows_ref[h, 24 : 24 + mid, :] = middle[c, layer, :, cut]
                rows_ref[h, 24 + mid : 32 + mid, :] = edge[c, layer, 8:16, cut]
                rows_ref[h, 16 + ny : 16 + ny + AFTER, :] = row_after[c, first + layer, :, cut]
                even_ref[c, layer, :, cut] = rows_ref[h, pl.ds(0, count, stride=2), :]
                odd_ref[c, layer, :, cut] = rows_ref[h, pl.ds(1, count, stride=2), :]


def lift_first(layers, halo):
    return halo_lift_list(layers[0::2], layers[1::2], *halo)


def halo_stack(pairs, both, combine, even_ref, odd_ref, part_ref, stack_ref):
    count, nz = even_ref.shape[2:]
    half, lanes = count - 16, nz // 2
    kinds = 4 if both else 2
    for n, (i, j) in enumerate(pairs):
        for h in range(2):
            cut = slice(h * lanes, (h + 1) * lanes)
            for parity, ref in enumerate((even_ref, odd_ref)):
                for r in range(0, count, 16):
                    rows = slice(r, r + 16)
                    g = [ref[i, layer, rows, cut] * ref[j, layer, rows, cut] for layer in range(ref.shape[1])]
                    for k, value in enumerate(combine(g)):
                        part_ref[parity, k, rows, :] = value
            for k in range(2):
                e, o = ring_lift(part_ref[0, k], part_ref[1, k])
                at = (kinds * n + k) * half
                stack_ref[at : at + half, cut] = e[8 : 8 + half]
                if both:
                    at += 2 * half
                    stack_ref[at : at + half, cut] = o[8 : 8 + half]


def halo_kernel(*refs):
    table_ref, low_ref, rest_ref = refs[4:7]
    rows_ref, even_ref, odd_ref, part_ref, stack_ref = refs[7:]
    half, lanes = low_ref.shape[2:]
    gather_rows(refs[:4], 0, rows_ref, even_ref, odd_ref)

    def group(g, carry):
        pairs = [pair_of(g * GROUP + n) for n in range(GROUP)]
        halo_stack(pairs, True, parts_for_next, even_ref, odd_ref, part_ref, stack_ref)
        stack_ref[...] = dot(stack_ref[...], table_ref[...])
        for n in range(GROUP):
            for k in range(2):
                low, high = (slice((4 * n + k + m) * half, (4 * n + k + m + 1) * half) for m in (0, 2))
                low_ref[g * GROUP + n, k] = stack_ref[low, :lanes]
                rest_ref[0, g * GROUP + n, k] = stack_ref[high, :lanes]
                rest_ref[1, g * GROUP + n, k] = stack_ref[low, lanes:]
                rest_ref[2, g * GROUP + n, k] = stack_ref[high, lanes:]
        return carry

    lax.fori_loop(0, 9 // GROUP, group, 0)


def halo_pass(halo, table):
    half, lanes = (halo[1].shape[2] + 16) // 2, halo[1].shape[3] // 2
    vmem = pl.BlockSpec(memory_space=pltpu.VMEM)
    return pl.pallas_call(
        halo_kernel,
        in_specs=[vmem] * 5,
        out_specs=[vmem] * 2,
        out_shape=[
            jax.ShapeDtypeStruct((9, 2, half, lanes), jnp.float32),
            jax.ShapeDtypeStruct((3, 9, 2, half, lanes), jnp.float32),
        ],
        scratch_shapes=halo_scratch(half, lanes, BEFORE, True),
        compiler_params=pltpu.CompilerParams(vmem_limit_bytes=24 * MIB),
        name="halo_pass",
    )(*halo, table)


def layer_list(refs, index, rows):
    return [ref[index + (x, rows)] for ref in refs for x in range(ref.shape[len(index)])]


def approx_kernel(*refs):
    low_refs, before_ref, table_ref = refs[:2], refs[2], refs[3]
    halo_refs = refs[4:8]
    approx_ref, high_ref, stress_ref = refs[8:11]
    next_ref, prev_ref, next_edge_ref, prev_edge_ref, down_ref, up_ref = refs[11:17]
    rows_ref, even_ref, odd_ref, part_ref, stack_ref, kept_ref, out_ref = refs[17:]
    f = pl.program_id(0)
    half, lanes = low_refs[0].shape[2:]
    mx = approx_ref.shape[1]

    @pl.when(f == 0)
    def _():
        gather_rows(halo_refs, BEFORE, rows_ref, even_ref, odd_ref)

    pairs = [pair_of(f * GROUP + n) for n in range(GROUP)]
    halo_stack(pairs, False, parts_for_previous, even_ref, odd_ref, part_ref, stack_ref)
    out_ref[...] = dot(stack_ref[...], table_ref[:, :lanes])
    for n in range(GROUP):
        for r in range(0, half, 8):
            rows = slice(r, r + 8)
            halo = [before_ref[n, k, rows, :] for k in range(2)]
            halo += [out_ref[(2 * n + k) * half + r : (2 * n + k) * half + r + 8, :] for k in range(2)]
            e, o = lift_first(layer_list(low_refs, (n,), rows), halo)
            e = [t * band_scale(0, 0) for t in e]
            for x in range(mx):
                approx_ref[n, x, rows, :] = e[x]
                high_ref[n, x, rows, :] = o[x] * band_scale(0, 1)
            send_layers(e, n, r, next_ref, prev_ref)
        send_rows(approx_ref, n, down_ref, up_ref)
        for ref, edge_ref in ((next_ref, next_edge_ref), (prev_ref, prev_edge_ref)):
            for part in range(2):
                tail, head = row_parts(lambda row: ref[n, part, row : row + 8, :], half)
                edge_ref[n, part, 0:2, :] = tail
                edge_ref[n, part, 2:4, :] = head

    @pl.when(f == 0)
    def _():
        kept_ref[...] = approx_ref[...]

    @pl.when(f > 0)
    def _():
        for n, (i, j) in enumerate(pairs):
            for x in range(mx):
                stress_ref[n, x] = approx_ref[n, x] - kept_ref[i, x] * kept_ref[j, x]


def whole(shape):
    return pl.BlockSpec(shape, lambda f: (0,) * len(shape))


def per_field(shape):
    return pl.BlockSpec((GROUP,) + shape, lambda f: (f,) + (0,) * len(shape))


def approx_pass(lows, before, halo, table):
    _, nx, half, lanes = lows[0].shape
    nz, mx = 2 * lanes, nx
    f32 = lambda *shape: jax.ShapeDtypeStruct(shape, jnp.float32)
    sends = [(2, half, lanes), (2, half, lanes), (2, 4, lanes), (2, 4, lanes), (mx, 2, lanes), (mx, 2, lanes)]
    return pl.pallas_call(
        approx_kernel,
        grid=(9 // GROUP,),
        in_specs=[per_field((nx, half, lanes))] * 2
        + [per_field((2, half, lanes)), whole((nz, nz))]
        + [whole(h.shape) for h in halo],
        out_specs=[
            per_field((mx, half, lanes)),
            per_field((mx, half, lanes)),
            pl.BlockSpec((GROUP, mx, half, lanes), lambda f: (jnp.maximum(f - 1, 0), 0, 0, 0)),
        ]
        + [per_field(s) for s in sends],
        out_shape=[f32(9, mx, half, lanes), f32(9, mx, half, lanes), f32(6, mx, half, lanes)] + [f32(9, *s) for s in sends],
        scratch_shapes=halo_scratch(half, lanes, AFTER, False)
        + [
            pltpu.VMEM((3, mx, half, lanes), jnp.float32),
            pltpu.VMEM((GROUP * 2 * half, lanes), jnp.float32),
        ],
        compiler_params=pltpu.CompilerParams(vmem_limit_bytes=24 * MIB),
        name="approx_pass",
    )(*lows, before, table, *halo)


def halo_scratch(half, lanes, layers, both):
    return [
        pltpu.VMEM((2, 2 * half + 32, lanes), jnp.float32),
        pltpu.VMEM((4, layers, half + 16, 2 * lanes), jnp.float32),
        pltpu.VMEM((4, layers, half + 16, 2 * lanes), jnp.float32),
        pltpu.VMEM((2, 2, half + 16, lanes), jnp.float32),
        pltpu.VMEM((GROUP * (4 if both else 2) * half, 2 * lanes), jnp.float32),
    ]


def detail_kernel(start, *refs):
    if start:
        refs = refs[:9] + refs[10:]
    rest_refs, before_ref, high_ref, table_ref = refs[:2], refs[2], refs[3], refs[4]
    halo_refs = refs[5:9]
    out_ref, rows_ref, even_ref, odd_ref, part_ref, stack_ref = refs[9:]
    f = pl.program_id(0)
    half, lanes = high_ref.shape[2:]
    mx = high_ref.shape[1]

    @pl.when(f == 0)
    def _():
        gather_rows(halo_refs, BEFORE, rows_ref, even_ref, odd_ref)

    pairs = [pair_of((f + start) * GROUP + n) for n in range(GROUP)]
    halo_stack(pairs, True, parts_for_previous, even_ref, odd_ref, part_ref, stack_ref)
    stack_ref[...] = dot(stack_ref[...], table_ref[...])
    for n in range(GROUP):
        for x in range(mx):
            out_ref[0, n, x] = high_ref[n, x]
        for band, (bz, by) in enumerate(((0, 1), (1, 0), (1, 1))):
            plane = 4 * bz + 2 * by - 1
            for r in range(0, half, 8):
                rows = slice(r, r + 8)
                halo = [before_ref[band, n, k, rows, :] for k in range(2)]
                for k in range(2):
                    at = (4 * n + 2 * by + k) * half + r
                    halo.append(stack_ref[at : at + 8, bz * lanes : (bz + 1) * lanes])
                e, o = lift_first(layer_list(rest_refs, (band, n), rows), halo)
                for x in range(mx):
                    out_ref[plane, n, x, rows, :] = e[x] * band_scale(by, 0)
                    out_ref[plane + 1, n, x, rows, :] = o[x] * band_scale(by, 1)


def detail_pass(rests, before, high, halo, table, start, stop, details=None):
    _, mx, half, lanes = high.shape
    nz = 2 * lanes
    aliased = [] if details is None else [details]
    band = lambda count, *shape: pl.BlockSpec((count, GROUP) + shape, lambda f: (0, f + start) + (0,) * len(shape))
    return pl.pallas_call(
        lambda *refs: detail_kernel(start, *refs),
        grid=(stop - start,),
        in_specs=[band(3, mx, half, lanes)] * 2
        + [
            band(3, 2, half, lanes),
            pl.BlockSpec((GROUP, mx, half, lanes), lambda f: (f + start, 0, 0, 0)),
            whole((nz, nz)),
        ]
        + [whole(h.shape) for h in halo]
        + [pl.BlockSpec(memory_space=pl.ANY)] * len(aliased),
        out_specs=band(7, mx, half, lanes),
        out_shape=jax.ShapeDtypeStruct((7, 9, mx, half, lanes), jnp.float32),
        input_output_aliases={9: 0} if aliased else {},
        scratch_shapes=halo_scratch(half, lanes, AFTER, True),
        compiler_params=pltpu.CompilerParams(vmem_limit_bytes=24 * MIB),
        cost_estimate=pl.CostEstimate(
            flops=2 * (stop - start) * GROUP * mx * half * nz * 200,
            bytes_accessed=2 * (stop - start) * GROUP * mx * half * nz * 16,
            transcendentals=0,
        ),
        name="detail_pass",
    )(*rests, before, high, table, *halo, *aliased)


def level_rows(refs, nz, nx, span, lows, pad_ref, stack_ref):
    a_ref, before_ref, after_ref, down_ref, up_ref = refs
    ny = (before_ref if a_ref is None else a_ref).shape[2]
    half = ny // 2
    wide = stack_ref.shape[1]
    kept = half if lows else ny
    if nz < wide:
        pad_ref[...] = jnp.zeros_like(pad_ref)
    for f in range(9):
        for step, layer in enumerate(span):
            if layer < nx:
                source, at = a_ref, layer
            elif layer < nx + 2:
                source, at = before_ref, layer - nx
            else:
                source, at = after_ref, layer - nx - 2
            if nz < wide:
                pad_ref[f, layer, :, :nz] = source[f, at]
                source, at = pad_ref, layer
            e = source[f, at, pl.ds(0, half, stride=2), :]
            o = source[f, at, pl.ds(1, half, stride=2), :]
            rows = [down_ref[f, layer, 1:2, :], down_ref[f, layer, 0:1, :], up_ref[f, layer, 0:1, :], up_ref[f, layer, 1:2, :]]
            if nz < wide:
                rows = [jnp.concatenate([row, jnp.zeros((1, wide - nz), jnp.float32)], axis=1) for row in rows]
            e, o = sublane_lift(e, o, *rows)
            at = (f * len(span) + step) * kept
            stack_ref[at : at + half, :] = e
            if not lows:
                stack_ref[at + half : at + ny, :] = o


def level_own_kernel(nz, a_ref, down_ref, up_ref, table_ref, own_ref, stack_ref):
    nx, _ = a_ref.shape[1:3]
    level_rows((a_ref, None, None, down_ref, up_ref), nz, nx, range(nx), True, None, stack_ref)
    own_ref[...] = dot(stack_ref[...], table_ref[...]).reshape(own_ref.shape)


def level_approx_kernel(nz, *refs):
    own_ref, table_ref, approx_ref, stress_ref = refs[0], refs[5], refs[6], refs[7]
    sends, (stack_ref, out_ref, kept_ref) = refs[8:-3], refs[-3:]
    nx, half = own_ref.shape[1:3]
    lanes = nz // 2
    level_rows((None,) + refs[1:5], nz, nx, range(nx, nx + 4), True, None, stack_ref)
    out_ref[...] = dot(stack_ref[...], table_ref[...])
    mx = nx // 2
    for f in range(9):
        for r in range(0, half, 8):
            rows = slice(r, r + 8)
            halo = []
            for k in range(4):
                at = (f * 4 + k) * half + r
                halo.append(out_ref[at : at + 8, :])
            low, _ = lift_first([own_ref[f, x, rows, :] for x in range(nx)], halo)
            approx = [(t * band_scale(0, 0))[:, :lanes] for t in low]
            for x in range(mx):
                if f < 3:
                    kept_ref[f, x, rows, :] = approx[x]
                else:
                    i, j = product_pairs[f - 3]
                    stress_ref[f - 3, x, rows, :] = approx[x] - kept_ref[i, x, rows, :] * kept_ref[j, x, rows, :]
                approx_ref[f, x, rows, :] = approx[x]
            send_layers(approx, f, r, sends[0], sends[1])
        send_rows(approx_ref, f, sends[2], sends[3])


def level_detail_kernel(nz, last, *refs):
    table_ref, detail_ref = refs[5:7]
    pad_ref, stack_ref, out_ref, kept_ref = refs[-4:]
    nx, ny = refs[0].shape[1:3]
    half, lanes = ny // 2, nz // 2
    wide = stack_ref.shape[1]
    level_rows(refs[:5], nz, nx, range(nx + 4), False, pad_ref, stack_ref)
    out_ref[...] = dot(stack_ref[...], table_ref[...])
    for f in range(9):
        for by in range(2):
            for r in range(0, half, 8):
                rows = slice(r, r + 8)
                layers = []
                for layer in range(nx + 4):
                    at = (f * (nx + 4) + layer) * ny + by * half + r
                    layers.append(out_ref[at : at + 8, :])
                low, high = lift_first(layers[:nx], layers[nx:])
                for x in range(nx // 2):
                    for bx, value in enumerate((low[x], high[x])):
                        t = value * band_scale(by, bx)
                        for bz in range(2):
                            band = 4 * bz + 2 * by + bx
                            piece = t[:, bz * (wide // 2) : bz * (wide // 2) + lanes]
                            if band:
                                detail_ref[band - 1, f, x, rows, :] = piece
                            elif last:
                                stress_ref, approx_ref = refs[7:9]
                                if f < 3:
                                    kept_ref[f, x, rows, :] = piece
                                    approx_ref[f, x, rows, :] = piece
                                else:
                                    i, j = product_pairs[f - 3]
                                    stress_ref[f - 3, x, rows, :] = piece - kept_ref[i, x, rows, :] * kept_ref[j, x, rows, :]


def level_call(kernel, approx, halo, out, kept):
    _, nx, ny, nz = approx.shape
    wide = max(nz, 128)
    vmem = pl.BlockSpec(memory_space=pltpu.VMEM)
    return pl.pallas_call(
        kernel,
        in_specs=[vmem] * 6,
        out_specs=[vmem] * len(out),
        out_shape=out,
        scratch_shapes=[
            pltpu.VMEM((9, nx + 4, ny, wide), jnp.float32),
            pltpu.VMEM((9 * (nx + 4) * kept, wide), jnp.float32),
            pltpu.VMEM((9 * (nx + 4) * kept, wide), jnp.float32),
            pltpu.VMEM((3, nx // 2, ny // 2, nz // 2), jnp.float32),
        ],
        compiler_params=pltpu.CompilerParams(vmem_limit_bytes=24 * MIB),
    )(approx, *halo, jnp.asarray(third_table(nz, wide)))


def level_approx(approx, halo):
    _, nx, ny, nz = approx.shape
    mx, half, lanes = nx // 2, ny // 2, nz // 2
    f32 = lambda *shape: jax.ShapeDtypeStruct(shape, jnp.float32)
    vmem = pl.BlockSpec(memory_space=pltpu.VMEM)
    params = pltpu.CompilerParams(vmem_limit_bytes=24 * MIB)
    table = jnp.asarray(third_table(nz, nz))
    own = pl.pallas_call(
        lambda *refs: level_own_kernel(nz, *refs),
        in_specs=[vmem] * 4,
        out_specs=vmem,
        out_shape=f32(9, nx, half, nz),
        scratch_shapes=[pltpu.VMEM((9 * nx * half, nz), jnp.float32)],
        compiler_params=params,
        name="level_own",
    )(approx, *halo[2:], table)
    sends = ((2, half, lanes), (2, half, lanes), (mx, 2, lanes), (mx, 2, lanes))
    out = [f32(9, mx, half, lanes), f32(6, mx, half, lanes)] + [f32(9, *s) for s in sends]
    return pl.pallas_call(
        lambda *refs: level_approx_kernel(nz, *refs),
        in_specs=[vmem] * 6,
        out_specs=[vmem] * len(out),
        out_shape=out,
        scratch_shapes=[
            pltpu.VMEM((9 * 4 * half, nz), jnp.float32),
            pltpu.VMEM((9 * 4 * half, nz), jnp.float32),
            pltpu.VMEM((3, mx, half, lanes), jnp.float32),
        ],
        compiler_params=params,
        name="level_approx",
    )(own, *halo, table)


def level_details(approx, halo, last):
    _, nx, ny, nz = approx.shape
    mx, half, lanes = nx // 2, ny // 2, nz // 2
    f32 = lambda *shape: jax.ShapeDtypeStruct(shape, jnp.float32)
    out = [f32(7, 9, mx, half, lanes)]
    if last:
        out += [f32(6, mx, half, lanes), f32(3, mx, half, lanes)]
    return level_call(lambda *refs: level_detail_kernel(nz, last, *refs), approx, halo, out, ny)


def halo_rows(before, after, down, up):
    rows = before.shape[2]
    cell = lambda at: jnp.concatenate([before[:, :, at : at + 1], after[:, :, at : at + 1]], axis=1)
    p, q = parts_for_next([cell(rows - 4 + i) for i in range(4)])
    down = jnp.concatenate([down, jnp.concatenate([q, p], axis=2)], axis=1)
    head = jnp.concatenate(parts_for_previous([cell(i) for i in range(3)]), axis=2)
    up = jnp.concatenate([up, head], axis=1)
    return shifted(down, "gy", 1), shifted(up, "gy", -1)


def exchange(to_next, to_prev, edge_next, edge_prev, down, up, meanwhile):
    from_prev = shifted(edge_next, "gx", 1)
    from_next = shifted(edge_prev, "gx", -1)
    before = shifted(to_next, "gx", 1)
    after = shifted(to_prev, "gx", -1)
    from_prev, from_next, result = lax.optimization_barrier((from_prev, from_next, meanwhile()))
    down = jnp.concatenate([down, from_prev[:, :, 0:2], from_next[:, :, 0:2]], axis=1)
    up = jnp.concatenate([up, from_prev[:, :, 2:4], from_next[:, :, 2:4]], axis=1)
    return (before, after, shifted(down, "gy", 1), shifted(up, "gy", -1)), result


def body(velocity):
    _, nx, ny, nz = velocity.shape
    table = jnp.asarray(third_table(nz, nz))
    tail, head = velocity[:, nx - BEFORE :], velocity[:, :AFTER]
    edges = lambda t: jnp.concatenate([t[:, :, :8], t[:, :, ny - 8 :]], axis=2)
    edge_before = shifted(edges(tail), "gx", 1)
    edge_after = shifted(edges(head), "gx", -1)
    mid_before = shifted(tail[:, :, 8 : ny - 8], "gx", 1)
    mid_after = shifted(head[:, :, 8 : ny - 8], "gx", -1)
    own_before = shifted(velocity[:, :, ny - BEFORE :], "gy", 1)
    own_after = shifted(velocity[:, :, :AFTER], "gy", -1)
    low_one, rest_one = local_pass(velocity, own_before, own_after, table, 0)
    low_two, rest_two = local_pass(velocity, own_before, own_after, table, nx // 2)
    edge_before, edge_after, low_one, low_two = lax.optimization_barrier((edge_before, edge_after, low_one, low_two))
    down = jnp.concatenate([edge_before[:, :, 12:], edge_after[:, :, 12:]], axis=1)
    up = jnp.concatenate([edge_before[:, :, :AFTER], edge_after[:, :, :AFTER]], axis=1)
    row_before = shifted(down, "gy", 1)
    row_after = shifted(up, "gy", -1)
    low_before, rest_before = halo_pass((edge_before, mid_before, row_before, row_after), table)
    halo = (edge_after, mid_after, row_before, row_after)
    approx, high, stress_one, *sends = approx_pass((low_one, low_two), low_before, halo, table)
    details = lambda *span: detail_pass((rest_one, rest_two), rest_before, high, halo, table, *span)
    second_halo, details_one = exchange(*sends, lambda: details(0, 2))
    details_one = details(2, 3, details_one)
    approx, details_one = lax.optimization_barrier((approx, details_one))
    second = approx
    approx, stress_two, *sends = level_approx(second, second_halo)
    before = shifted(sends[0], "gx", 1)
    after = shifted(sends[1], "gx", -1)
    (details_two,) = level_details(second, second_halo, False)
    before, after, details_two = lax.optimization_barrier((before, after, details_two))
    third_halo = (before, after) + halo_rows(before, after, *sends[2:])
    details_three, stress_three, coarse = level_details(approx, third_halo, True)
    return details_one, stress_one, details_two, stress_two, details_three, stress_three, coarse


def solution(mesh):
    in_specs = (P(None, "gx", "gy", None),)
    out_specs = (
        P(None, None, "gx", "gy", None),
        P(None, "gx", "gy", None),
        P(None, None, "gx", "gy", None),
        P(None, "gx", "gy", None),
        P(None, None, "gx", "gy", None),
        P(None, "gx", "gy", None),
        P(None, "gx", "gy", None),
    )
    return jax.shard_map(body, mesh=mesh, in_specs=in_specs, out_specs=out_specs, check_vma=False)
```

```python
import jax
import jax.numpy as jnp
import numpy as np
from jax import lax
from jax.experimental import pallas as pl
from jax.experimental.pallas import tpu as pltpu
from jax.sharding import PartitionSpec as P

predict_one = -1.586134342
update_one = -0.05298011854
predict_two = 0.8829110762
update_two = 0.4435068522
scaling = 1.149604398
product_pairs = ((0, 0), (0, 1), (0, 2), (1, 1), (1, 2), (2, 2))
BEFORE = 4
AFTER = 3
GROUP = 3
MIB = 1 << 20


def shifted(block, axis, distance):
    size = lax.axis_size(axis)
    return lax.ppermute(block, axis, [(i, (i + distance) % size) for i in range(size)])


def swapped(block, axis, odd):
    size = lax.axis_size(axis)
    route = []
    for i in range(size):
        route.append((i, (i + 1) % size if i % 2 == odd else (i - 1) % size))
    return lax.ppermute(block, axis, route)


def neighbours(to_next, to_prev, axis):
    even = lax.axis_index(axis) % 2 == 0
    far = swapped(jnp.where(even, to_prev, to_next), axis, 1)
    near = swapped(jnp.where(even, to_next, to_prev), axis, 0)
    return jnp.where(even, far, near), jnp.where(even, near, far)


def third_table(length, lanes):
    eye = np.eye(length)
    e, o = eye[:, 0::2], eye[:, 1::2]
    following = lambda t: np.concatenate([t[:, 1:], t[:, -1:]], 1)
    preceding = lambda t: np.concatenate([t[:, :1], t[:, :-1]], 1)
    o = o + predict_one * (e + following(e))
    e = e + update_one * (o + preceding(o))
    o = o + predict_two * (e + following(e))
    e = e + update_two * (o + preceding(o))
    table = np.zeros((lanes, lanes))
    table[:length, : length // 2] = e * scaling
    table[:length, lanes // 2 : lanes // 2 + length // 2] = o / scaling
    return table.astype(np.float32)


def band_scale(by, bx):
    return float(scaling ** ((1 - 2 * by) + (1 - 2 * bx)))


def dot(a, b):
    a_high, b_high = a.astype(jnp.bfloat16), b.astype(jnp.bfloat16)
    a_low = (a - a_high.astype(jnp.float32)).astype(jnp.bfloat16)
    b_low = (b - b_high.astype(jnp.float32)).astype(jnp.bfloat16)
    part = lambda x, y: jnp.dot(x, y, preferred_element_type=jnp.float32)
    return part(a_high, b_high) + (part(a_high, b_low) + part(a_low, b_high))


def ring_lift(e, o):
    n = e.shape[0]
    up = lambda t: pltpu.roll(t, n - 1, 0)
    down = lambda t: pltpu.roll(t, 1, 0)
    o = o + predict_one * (e + up(e))
    e = e + update_one * (o + down(o))
    o = o + predict_two * (e + up(e))
    e = e + update_two * (o + down(o))
    return e, o


def halo_lift(e, o, p, q, r, s, following, preceding, first, last):
    o1 = o + predict_one * (e + following(e, r))
    o1_before = p + predict_one * first(e)
    e1 = e + update_one * (preceding(o1, o1_before) + o1)
    e1_before = q + update_one * o1_before
    e1_after = r + update_one * (last(o1) + s)
    o2 = o1 + predict_two * (e1 + following(e1, e1_after))
    o2_before = o1_before + predict_two * (e1_before + first(e1))
    e2 = e1 + update_two * (preceding(o2, o2_before) + o2)
    return e2, o2


def halo_lift_list(e, o, p, q, r, s):
    m = len(e)
    e = list(e) + [r]
    o1 = [p + predict_one * e[0]]
    o1 += [o[i] + predict_one * (e[i] + e[i + 1]) for i in range(m)] + [s]
    e1 = [q + update_one * o1[0]]
    e1 += [e[i] + update_one * (o1[i] + o1[i + 1]) for i in range(m + 1)]
    o2 = [o1[i] + predict_two * (e1[i] + e1[i + 1]) for i in range(m + 1)]
    e2 = [e1[i + 1] + update_two * (o2[i] + o2[i + 1]) for i in range(m)]
    return e2, o2[1:]


def sublane_lift(e, o, p, q, r, s):
    n = e.shape[0]
    row = lax.broadcasted_iota(jnp.int32, e.shape, 0)
    following = lambda t, edge: jnp.where(row == n - 1, edge, pltpu.roll(t, n - 1, 0))
    preceding = lambda t, edge: jnp.where(row == 0, edge, pltpu.roll(t, 1, 0))
    return halo_lift(e, o, p, q, r, s, following, preceding, lambda t: t[0:1], lambda t: t[n - 1 : n])


def parts_for_next(c):
    p = c[-1] + predict_one * c[-2]
    q = c[-2] + update_one * (c[-3] + predict_one * (c[-4] + c[-2]))
    return p, q


def parts_for_previous(c):
    return c[0], c[1] + predict_one * (c[0] + c[2])


def row_parts(load, rows):
    tail, head = load(rows - 8), load(0)
    row = lax.broadcasted_iota(jnp.int32, tail.shape, 0)
    inner = tail + predict_one * (pltpu.roll(tail, 1, 0) + pltpu.roll(tail, 7, 0))
    p = tail + predict_one * pltpu.roll(tail, 1, 0)
    q = tail + update_one * pltpu.roll(inner, 1, 0)
    s = head + predict_one * (pltpu.roll(head, 1, 0) + pltpu.roll(head, 7, 0))
    return jnp.where(row == 7, p, q)[6:8], jnp.where(row == 0, head, s)[0:2]


def send_layers(layers, f, at, next_ref, prev_ref):
    for part, value in enumerate(parts_for_next(layers)):
        next_ref[f, part, at : at + 8, :] = value
    for part, value in enumerate(parts_for_previous(layers)):
        prev_ref[f, part, at : at + 8, :] = value


def send_rows(ref, f, down_ref, up_ref):
    for at in range(ref.shape[1]):
        tail, head = row_parts(lambda row: ref[f, at, row : row + 8, :], ref.shape[2])
        down_ref[f, at] = tail
        up_ref[f, at] = head


def local_kernel(v_ref, before_ref, after_ref, table_ref, low_ref, rest_ref, rows_ref, stack_ref):
    ny = v_ref.shape[2]
    half = ny // 2
    lanes = v_ref.shape[3] // 2
    even, odd = [], []
    for c in range(3):
        for h in range(2):
            cut = pl.ds(h * lanes, lanes)
            rows_ref[c, h, 12:16, :] = before_ref[c, 0, :, cut]
            rows_ref[c, h, 16 : 16 + ny, :] = v_ref[c, 0, :, cut]
            rows_ref[c, h, 16 + ny : 16 + ny + AFTER, :] = after_ref[c, 0, :, cut]
    count = half + 16
    for h in range(2):
        even = [rows_ref[c, h, pl.ds(0, count, stride=2), :] for c in range(3)]
        odd = [rows_ref[c, h, pl.ds(1, count, stride=2), :] for c in range(3)]
        for f in range(9):
            if f < 3:
                e, o = even[f], odd[f]
            else:
                i, j = product_pairs[f - 3]
                e, o = even[i] * even[j], odd[i] * odd[j]
            e, o = ring_lift(e, o)
            stack_ref[f * ny : f * ny + half, h * lanes : (h + 1) * lanes] = e[8 : 8 + half]
            stack_ref[f * ny + half : (f + 1) * ny, h * lanes : (h + 1) * lanes] = o[8 : 8 + half]
    out = dot(stack_ref[...], table_ref[...])
    for f in range(9):
        low_ref[f, 0] = out[f * ny : f * ny + half, :lanes]
        rest_ref[0, f, 0] = out[f * ny + half : (f + 1) * ny, :lanes]
        rest_ref[1, f, 0] = out[f * ny : f * ny + half, lanes:]
        rest_ref[2, f, 0] = out[f * ny + half : (f + 1) * ny, lanes:]


def local_pass(velocity, before, after, table, start):
    _, nx, ny, nz = velocity.shape
    nx = nx // 2
    half, lanes = ny // 2, nz // 2
    return pl.pallas_call(
        local_kernel,
        grid=(nx,),
        in_specs=[
            pl.BlockSpec((3, 1, ny, nz), lambda i: (0, i + start, 0, 0)),
            pl.BlockSpec((3, 1, BEFORE, nz), lambda i: (0, i + start, 0, 0)),
            pl.BlockSpec((3, 1, AFTER, nz), lambda i: (0, i + start, 0, 0)),
            pl.BlockSpec((nz, nz), lambda i: (0, 0)),
        ],
        out_specs=[
            pl.BlockSpec((9, 1, half, lanes), lambda i: (0, i, 0, 0)),
            pl.BlockSpec((3, 9, 1, half, lanes), lambda i: (0, 0, i, 0, 0)),
        ],
        out_shape=[
            jax.ShapeDtypeStruct((9, nx, half, lanes), jnp.float32),
            jax.ShapeDtypeStruct((3, 9, nx, half, lanes), jnp.float32),
        ],
        scratch_shapes=[pltpu.VMEM((3, 2, ny + 32, lanes), jnp.float32), pltpu.VMEM((9 * ny, nz), jnp.float32)],
        compiler_params=pltpu.CompilerParams(vmem_limit_bytes=24 * MIB),
        cost_estimate=pl.CostEstimate(flops=9 * nx * ny * nz * 512, bytes_accessed=9 * nx * ny * nz * 6, transcendentals=0),
        name="local_pass",
    )(velocity, before, after, table)


def pair_of(f):
    k = f - 3
    one = jnp.where(k < 3, 0, jnp.where(k < 5, 1, 2))
    two = jnp.where(k < 3, k, jnp.where(k < 5, k - 2, 2))
    return jnp.where(f < 3, f, one), jnp.where(f < 3, 3, two)


def gather_rows(refs, first, rows_ref, even_ref, odd_ref):
    edge, middle, row_before, row_after = refs
    layers, mid = middle.shape[1:3]
    ny = mid + 16
    lanes = rows_ref.shape[2]
    count = ny // 2 + 16
    even_ref[3] = jnp.ones(even_ref.shape[1:], jnp.float32)
    odd_ref[3] = jnp.ones(odd_ref.shape[1:], jnp.float32)
    for c in range(3):
        for layer in range(layers):
            for h in range(2):
                cut = pl.ds(h * lanes, lanes)
                rows_ref[h, 12:16, :] = row_before[c, first + layer, :, cut]
                rows_ref[h, 16:24, :] = edge[c, layer, 0:8, cut]
                rows_ref[h, 24 : 24 + mid, :] = middle[c, layer, :, cut]
                rows_ref[h, 24 + mid : 32 + mid, :] = edge[c, layer, 8:16, cut]
                rows_ref[h, 16 + ny : 16 + ny + AFTER, :] = row_after[c, first + layer, :, cut]
                even_ref[c, layer, :, cut] = rows_ref[h, pl.ds(0, count, stride=2), :]
                odd_ref[c, layer, :, cut] = rows_ref[h, pl.ds(1, count, stride=2), :]


def lift_first(layers, halo):
    return halo_lift_list(layers[0::2], layers[1::2], *halo)


def halo_stack(pairs, both, combine, even_ref, odd_ref, part_ref, stack_ref):
    count, nz = even_ref.shape[2:]
    half, lanes = count - 16, nz // 2
    kinds = 4 if both else 2
    for n, (i, j) in enumerate(pairs):
        for h in range(2):
            cut = slice(h * lanes, (h + 1) * lanes)
            for parity, ref in enumerate((even_ref, odd_ref)):
                for r in range(0, count, 16):
                    rows = slice(r, r + 16)
                    g = [ref[i, layer, rows, cut] * ref[j, layer, rows, cut] for layer in range(ref.shape[1])]
                    for k, value in enumerate(combine(g)):
                        part_ref[parity, k, rows, :] = value
            for k in range(2):
                e, o = ring_lift(part_ref[0, k], part_ref[1, k])
                at = (kinds * n + k) * half
                stack_ref[at : at + half, cut] = e[8 : 8 + half]
                if both:
                    at += 2 * half
                    stack_ref[at : at + half, cut] = o[8 : 8 + half]


def halo_kernel(*refs):
    table_ref, low_ref, rest_ref = refs[4:7]
    rows_ref, even_ref, odd_ref, part_ref, stack_ref = refs[7:]
    half, lanes = low_ref.shape[2:]
    gather_rows(refs[:4], 0, rows_ref, even_ref, odd_ref)

    def group(g, carry):
        pairs = [pair_of(g * GROUP + n) for n in range(GROUP)]
        halo_stack(pairs, True, parts_for_next, even_ref, odd_ref, part_ref, stack_ref)
        stack_ref[...] = dot(stack_ref[...], table_ref[...])
        for n in range(GROUP):
            for k in range(2):
                low, high = (slice((4 * n + k + m) * half, (4 * n + k + m + 1) * half) for m in (0, 2))
                low_ref[g * GROUP + n, k] = stack_ref[low, :lanes]
                rest_ref[0, g * GROUP + n, k] = stack_ref[high, :lanes]
                rest_ref[1, g * GROUP + n, k] = stack_ref[low, lanes:]
                rest_ref[2, g * GROUP + n, k] = stack_ref[high, lanes:]
        return carry

    lax.fori_loop(0, 9 // GROUP, group, 0)


def halo_pass(halo, table):
    half, lanes = (halo[1].shape[2] + 16) // 2, halo[1].shape[3] // 2
    vmem = pl.BlockSpec(memory_space=pltpu.VMEM)
    return pl.pallas_call(
        halo_kernel,
        in_specs=[vmem] * 5,
        out_specs=[vmem] * 2,
        out_shape=[
            jax.ShapeDtypeStruct((9, 2, half, lanes), jnp.float32),
            jax.ShapeDtypeStruct((3, 9, 2, half, lanes), jnp.float32),
        ],
        scratch_shapes=halo_scratch(half, lanes, BEFORE, True),
        compiler_params=pltpu.CompilerParams(vmem_limit_bytes=24 * MIB),
        name="halo_pass",
    )(*halo, table)


def layer_list(refs, index, rows):
    return [ref[index + (x, rows)] for ref in refs for x in range(ref.shape[len(index)])]


def approx_kernel(*refs):
    low_refs, before_ref, table_ref = refs[:2], refs[2], refs[3]
    halo_refs = refs[4:8]
    approx_ref, high_ref, stress_ref = refs[8:11]
    next_ref, prev_ref, next_edge_ref, prev_edge_ref, down_ref, up_ref = refs[11:17]
    rows_ref, even_ref, odd_ref, part_ref, stack_ref, kept_ref, out_ref = refs[17:]
    f = pl.program_id(0)
    half, lanes = low_refs[0].shape[2:]
    mx = approx_ref.shape[1]

    @pl.when(f == 0)
    def _():
        gather_rows(halo_refs, BEFORE, rows_ref, even_ref, odd_ref)

    pairs = [pair_of(f * GROUP + n) for n in range(GROUP)]
    halo_stack(pairs, False, parts_for_previous, even_ref, odd_ref, part_ref, stack_ref)
    out_ref[...] = dot(stack_ref[...], table_ref[:, :lanes])
    for n in range(GROUP):
        for r in range(0, half, 8):
            rows = slice(r, r + 8)
            halo = [before_ref[n, k, rows, :] for k in range(2)]
            halo += [out_ref[(2 * n + k) * half + r : (2 * n + k) * half + r + 8, :] for k in range(2)]
            e, o = lift_first(layer_list(low_refs, (n,), rows), halo)
            e = [t * band_scale(0, 0) for t in e]
            for x in range(mx):
                approx_ref[n, x, rows, :] = e[x]
                high_ref[n, x, rows, :] = o[x] * band_scale(0, 1)
            send_layers(e, n, r, next_ref, prev_ref)
        send_rows(approx_ref, n, down_ref, up_ref)
        for ref, edge_ref in ((next_ref, next_edge_ref), (prev_ref, prev_edge_ref)):
            for part in range(2):
                tail, head = row_parts(lambda row: ref[n, part, row : row + 8, :], half)
                edge_ref[n, part, 0:2, :] = tail
                edge_ref[n, part, 2:4, :] = head

    @pl.when(f == 0)
    def _():
        kept_ref[...] = approx_ref[...]

    @pl.when(f > 0)
    def _():
        for n, (i, j) in enumerate(pairs):
            for x in range(mx):
                stress_ref[n, x] = approx_ref[n, x] - kept_ref[i, x] * kept_ref[j, x]


def whole(shape):
    return pl.BlockSpec(shape, lambda f: (0,) * len(shape))


def per_field(shape):
    return pl.BlockSpec((GROUP,) + shape, lambda f: (f,) + (0,) * len(shape))


def approx_pass(lows, before, halo, table):
    _, nx, half, lanes = lows[0].shape
    nz, mx = 2 * lanes, nx
    f32 = lambda *shape: jax.ShapeDtypeStruct(shape, jnp.float32)
    sends = [(2, half, lanes), (2, half, lanes), (2, 4, lanes), (2, 4, lanes), (mx, 2, lanes), (mx, 2, lanes)]
    return pl.pallas_call(
        approx_kernel,
        grid=(9 // GROUP,),
        in_specs=[per_field((nx, half, lanes))] * 2
        + [per_field((2, half, lanes)), whole((nz, nz))]
        + [whole(h.shape) for h in halo],
        out_specs=[
            per_field((mx, half, lanes)),
            per_field((mx, half, lanes)),
            pl.BlockSpec((GROUP, mx, half, lanes), lambda f: (jnp.maximum(f - 1, 0), 0, 0, 0)),
        ]
        + [per_field(s) for s in sends],
        out_shape=[f32(9, mx, half, lanes), f32(9, mx, half, lanes), f32(6, mx, half, lanes)] + [f32(9, *s) for s in sends],
        scratch_shapes=halo_scratch(half, lanes, AFTER, False)
        + [
            pltpu.VMEM((3, mx, half, lanes), jnp.float32),
            pltpu.VMEM((GROUP * 2 * half, lanes), jnp.float32),
        ],
        compiler_params=pltpu.CompilerParams(vmem_limit_bytes=24 * MIB),
        name="approx_pass",
    )(*lows, before, table, *halo)


def halo_scratch(half, lanes, layers, both):
    return [
        pltpu.VMEM((2, 2 * half + 32, lanes), jnp.float32),
        pltpu.VMEM((4, layers, half + 16, 2 * lanes), jnp.float32),
        pltpu.VMEM((4, layers, half + 16, 2 * lanes), jnp.float32),
        pltpu.VMEM((2, 2, half + 16, lanes), jnp.float32),
        pltpu.VMEM((GROUP * (4 if both else 2) * half, 2 * lanes), jnp.float32),
    ]


def detail_kernel(start, *refs):
    if start:
        refs = refs[:9] + refs[10:]
    rest_refs, before_ref, high_ref, table_ref = refs[:2], refs[2], refs[3], refs[4]
    halo_refs = refs[5:9]
    out_ref, rows_ref, even_ref, odd_ref, part_ref, stack_ref = refs[9:]
    f = pl.program_id(0)
    half, lanes = high_ref.shape[2:]
    mx = high_ref.shape[1]

    @pl.when(f == 0)
    def _():
        gather_rows(halo_refs, BEFORE, rows_ref, even_ref, odd_ref)

    pairs = [pair_of((f + start) * GROUP + n) for n in range(GROUP)]
    halo_stack(pairs, True, parts_for_previous, even_ref, odd_ref, part_ref, stack_ref)
    stack_ref[...] = dot(stack_ref[...], table_ref[...])
    for n in range(GROUP):
        for x in range(mx):
            out_ref[0, n, x] = high_ref[n, x]
        for band, (bz, by) in enumerate(((0, 1), (1, 0), (1, 1))):
            plane = 4 * bz + 2 * by - 1
            for r in range(0, half, 8):
                rows = slice(r, r + 8)
                halo = [before_ref[band, n, k, rows, :] for k in range(2)]
                for k in range(2):
                    at = (4 * n + 2 * by + k) * half + r
                    halo.append(stack_ref[at : at + 8, bz * lanes : (bz + 1) * lanes])
                e, o = lift_first(layer_list(rest_refs, (band, n), rows), halo)
                for x in range(mx):
                    out_ref[plane, n, x, rows, :] = e[x] * band_scale(by, 0)
                    out_ref[plane + 1, n, x, rows, :] = o[x] * band_scale(by, 1)


def detail_pass(rests, before, high, halo, table, start, stop, details=None):
    _, mx, half, lanes = high.shape
    nz = 2 * lanes
    aliased = [] if details is None else [details]
    band = lambda count, *shape: pl.BlockSpec((count, GROUP) + shape, lambda f: (0, f + start) + (0,) * len(shape))
    return pl.pallas_call(
        lambda *refs: detail_kernel(start, *refs),
        grid=(stop - start,),
        in_specs=[band(3, mx, half, lanes)] * 2
        + [
            band(3, 2, half, lanes),
            pl.BlockSpec((GROUP, mx, half, lanes), lambda f: (f + start, 0, 0, 0)),
            whole((nz, nz)),
        ]
        + [whole(h.shape) for h in halo]
        + [pl.BlockSpec(memory_space=pl.ANY)] * len(aliased),
        out_specs=band(7, mx, half, lanes),
        out_shape=jax.ShapeDtypeStruct((7, 9, mx, half, lanes), jnp.float32),
        input_output_aliases={9: 0} if aliased else {},
        scratch_shapes=halo_scratch(half, lanes, AFTER, True),
        compiler_params=pltpu.CompilerParams(vmem_limit_bytes=24 * MIB),
        cost_estimate=pl.CostEstimate(
            flops=2 * (stop - start) * GROUP * mx * half * nz * 200,
            bytes_accessed=2 * (stop - start) * GROUP * mx * half * nz * 16,
            transcendentals=0,
        ),
        name="detail_pass",
    )(*rests, before, high, table, *halo, *aliased)


def level_rows(refs, nz, nx, span, lows, pad_ref, stack_ref):
    a_ref, before_ref, after_ref, down_ref, up_ref = refs
    ny = (before_ref if a_ref is None else a_ref).shape[2]
    half = ny // 2
    wide = stack_ref.shape[1]
    kept = half if lows else ny
    if nz < wide:
        pad_ref[...] = jnp.zeros_like(pad_ref)
    for f in range(9):
        for step, layer in enumerate(span):
            if layer < nx:
                source, at = a_ref, layer
            elif layer < nx + 2:
                source, at = before_ref, layer - nx
            else:
                source, at = after_ref, layer - nx - 2
            if nz < wide:
                pad_ref[f, layer, :, :nz] = source[f, at]
                source, at = pad_ref, layer
            e = source[f, at, pl.ds(0, half, stride=2), :]
            o = source[f, at, pl.ds(1, half, stride=2), :]
            rows = [down_ref[f, layer, 1:2, :], down_ref[f, layer, 0:1, :], up_ref[f, layer, 0:1, :], up_ref[f, layer, 1:2, :]]
            if nz < wide:
                rows = [jnp.concatenate([row, jnp.zeros((1, wide - nz), jnp.float32)], axis=1) for row in rows]
            e, o = sublane_lift(e, o, *rows)
            at = (f * len(span) + step) * kept
            stack_ref[at : at + half, :] = e
            if not lows:
                stack_ref[at + half : at + ny, :] = o


def level_own_kernel(nz, a_ref, down_ref, up_ref, table_ref, own_ref, stack_ref):
    nx, _ = a_ref.shape[1:3]
    level_rows((a_ref, None, None, down_ref, up_ref), nz, nx, range(nx), True, None, stack_ref)
    own_ref[...] = dot(stack_ref[...], table_ref[...]).reshape(own_ref.shape)


def level_approx_kernel(nz, *refs):
    own_ref, table_ref, approx_ref, stress_ref = refs[0], refs[5], refs[6], refs[7]
    sends, (stack_ref, out_ref, kept_ref) = refs[8:-3], refs[-3:]
    nx, half = own_ref.shape[1:3]
    lanes = nz // 2
    level_rows((None,) + refs[1:5], nz, nx, range(nx, nx + 4), True, None, stack_ref)
    out_ref[...] = dot(stack_ref[...], table_ref[...])
    mx = nx // 2
    for f in range(9):
        for r in range(0, half, 8):
            rows = slice(r, r + 8)
            halo = []
            for k in range(4):
                at = (f * 4 + k) * half + r
                halo.append(out_ref[at : at + 8, :])
            low, _ = lift_first([own_ref[f, x, rows, :] for x in range(nx)], halo)
            approx = [(t * band_scale(0, 0))[:, :lanes] for t in low]
            for x in range(mx):
                if f < 3:
                    kept_ref[f, x, rows, :] = approx[x]
                else:
                    i, j = product_pairs[f - 3]
                    stress_ref[f - 3, x, rows, :] = approx[x] - kept_ref[i, x, rows, :] * kept_ref[j, x, rows, :]
                approx_ref[f, x, rows, :] = approx[x]
            send_layers(approx, f, r, sends[0], sends[1])
        send_rows(approx_ref, f, sends[2], sends[3])


def level_detail_kernel(nz, last, *refs):
    table_ref, detail_ref = refs[5:7]
    pad_ref, stack_ref, out_ref, kept_ref = refs[-4:]
    nx, ny = refs[0].shape[1:3]
    half, lanes = ny // 2, nz // 2
    wide = stack_ref.shape[1]
    level_rows(refs[:5], nz, nx, range(nx + 4), False, pad_ref, stack_ref)
    out_ref[...] = dot(stack_ref[...], table_ref[...])
    for f in range(9):
        for by in range(2):
            for r in range(0, half, 8):
                rows = slice(r, r + 8)
                layers = []
                for layer in range(nx + 4):
                    at = (f * (nx + 4) + layer) * ny + by * half + r
                    layers.append(out_ref[at : at + 8, :])
                low, high = lift_first(layers[:nx], layers[nx:])
                for x in range(nx // 2):
                    for bx, value in enumerate((low[x], high[x])):
                        t = value * band_scale(by, bx)
                        for bz in range(2):
                            band = 4 * bz + 2 * by + bx
                            piece = t[:, bz * (wide // 2) : bz * (wide // 2) + lanes]
                            if band:
                                detail_ref[band - 1, f, x, rows, :] = piece
                            elif last:
                                stress_ref, approx_ref = refs[7:9]
                                if f < 3:
                                    kept_ref[f, x, rows, :] = piece
                                    approx_ref[f, x, rows, :] = piece
                                else:
                                    i, j = product_pairs[f - 3]
                                    stress_ref[f - 3, x, rows, :] = piece - kept_ref[i, x, rows, :] * kept_ref[j, x, rows, :]


def level_call(kernel, approx, halo, out, kept):
    _, nx, ny, nz = approx.shape
    wide = max(nz, 128)
    vmem = pl.BlockSpec(memory_space=pltpu.VMEM)
    return pl.pallas_call(
        kernel,
        in_specs=[vmem] * 6,
        out_specs=[vmem] * len(out),
        out_shape=out,
        scratch_shapes=[
            pltpu.VMEM((9, nx + 4, ny, wide), jnp.float32),
            pltpu.VMEM((9 * (nx + 4) * kept, wide), jnp.float32),
            pltpu.VMEM((9 * (nx + 4) * kept, wide), jnp.float32),
            pltpu.VMEM((3, nx // 2, ny // 2, nz // 2), jnp.float32),
        ],
        compiler_params=pltpu.CompilerParams(vmem_limit_bytes=24 * MIB),
    )(approx, *halo, jnp.asarray(third_table(nz, wide)))


def level_approx(approx, halo):
    _, nx, ny, nz = approx.shape
    mx, half, lanes = nx // 2, ny // 2, nz // 2
    f32 = lambda *shape: jax.ShapeDtypeStruct(shape, jnp.float32)
    vmem = pl.BlockSpec(memory_space=pltpu.VMEM)
    params = pltpu.CompilerParams(vmem_limit_bytes=24 * MIB)
    table = jnp.asarray(third_table(nz, nz))
    own = pl.pallas_call(
        lambda *refs: level_own_kernel(nz, *refs),
        in_specs=[vmem] * 4,
        out_specs=vmem,
        out_shape=f32(9, nx, half, nz),
        scratch_shapes=[pltpu.VMEM((9 * nx * half, nz), jnp.float32)],
        compiler_params=params,
        name="level_own",
    )(approx, *halo[2:], table)
    sends = ((2, half, lanes), (2, half, lanes), (mx, 2, lanes), (mx, 2, lanes))
    out = [f32(9, mx, half, lanes), f32(6, mx, half, lanes)] + [f32(9, *s) for s in sends]
    return pl.pallas_call(
        lambda *refs: level_approx_kernel(nz, *refs),
        in_specs=[vmem] * 6,
        out_specs=[vmem] * len(out),
        out_shape=out,
        scratch_shapes=[
            pltpu.VMEM((9 * 4 * half, nz), jnp.float32),
            pltpu.VMEM((9 * 4 * half, nz), jnp.float32),
            pltpu.VMEM((3, mx, half, lanes), jnp.float32),
        ],
        compiler_params=params,
        name="level_approx",
    )(own, *halo, table)


def level_details(approx, halo, last):
    _, nx, ny, nz = approx.shape
    mx, half, lanes = nx // 2, ny // 2, nz // 2
    f32 = lambda *shape: jax.ShapeDtypeStruct(shape, jnp.float32)
    out = [f32(7, 9, mx, half, lanes)]
    if last:
        out += [f32(6, mx, half, lanes), f32(3, mx, half, lanes)]
    return level_call(lambda *refs: level_detail_kernel(nz, last, *refs), approx, halo, out, ny)


def halo_rows(before, after, down, up):
    rows = before.shape[2]
    cell = lambda at: jnp.concatenate([before[:, :, at : at + 1], after[:, :, at : at + 1]], axis=1)
    p, q = parts_for_next([cell(rows - 4 + i) for i in range(4)])
    down = jnp.concatenate([down, jnp.concatenate([q, p], axis=2)], axis=1)
    head = jnp.concatenate(parts_for_previous([cell(i) for i in range(3)]), axis=2)
    up = jnp.concatenate([up, head], axis=1)
    return shifted(down, "gy", 1), shifted(up, "gy", -1)


def exchange(to_next, to_prev, edge_next, edge_prev, down, up, meanwhile):
    from_prev, from_next = neighbours(edge_next, edge_prev, "gx")
    before, after = neighbours(to_next, to_prev, "gx")
    from_prev, from_next, result = lax.optimization_barrier((from_prev, from_next, meanwhile()))
    down = jnp.concatenate([down, from_prev[:, :, 0:2], from_next[:, :, 0:2]], axis=1)
    up = jnp.concatenate([up, from_prev[:, :, 2:4], from_next[:, :, 2:4]], axis=1)
    return (before, after, shifted(down, "gy", 1), shifted(up, "gy", -1)), result


def body(velocity):
    _, nx, ny, nz = velocity.shape
    table = jnp.asarray(third_table(nz, nz))
    tail, head = velocity[:, nx - BEFORE :], velocity[:, :AFTER]
    edges = lambda t: jnp.concatenate([t[:, :, :8], t[:, :, ny - 8 :]], axis=2)
    edge_before = shifted(edges(tail), "gx", 1)
    edge_after = shifted(edges(head), "gx", -1)
    mid_before = shifted(tail[:, :, 8 : ny - 8], "gx", 1)
    mid_after = shifted(head[:, :, 8 : ny - 8], "gx", -1)
    own_before = shifted(velocity[:, :, ny - BEFORE :], "gy", 1)
    own_after = shifted(velocity[:, :, :AFTER], "gy", -1)
    low_one, rest_one = local_pass(velocity, own_before, own_after, table, 0)
    low_two, rest_two = local_pass(velocity, own_before, own_after, table, nx // 2)
    edge_before, edge_after, low_one, low_two = lax.optimization_barrier((edge_before, edge_after, low_one, low_two))
    down = jnp.concatenate([edge_before[:, :, 12:], edge_after[:, :, 12:]], axis=1)
    up = jnp.concatenate([edge_before[:, :, :AFTER], edge_after[:, :, :AFTER]], axis=1)
    row_before = shifted(down, "gy", 1)
    row_after = shifted(up, "gy", -1)
    low_before, rest_before = halo_pass((edge_before, mid_before, row_before, row_after), table)
    halo = (edge_after, mid_after, row_before, row_after)
    approx, high, stress_one, *sends = approx_pass((low_one, low_two), low_before, halo, table)
    details = lambda *span: detail_pass((rest_one, rest_two), rest_before, high, halo, table, *span)
    second_halo, details_one = exchange(*sends, lambda: details(0, 2))
    details_one = details(2, 3, details_one)
    approx, details_one = lax.optimization_barrier((approx, details_one))
    second = approx
    approx, stress_two, *sends = level_approx(second, second_halo)
    before, after = neighbours(sends[0], sends[1], "gx")
    (details_two,) = level_details(second, second_halo, False)
    before, after, details_two = lax.optimization_barrier((before, after, details_two))
    third_halo = (before, after) + halo_rows(before, after, *sends[2:])
    details_three, stress_three, coarse = level_details(approx, third_halo, True)
    return details_one, stress_one, details_two, stress_two, details_three, stress_three, coarse


def solution(mesh):
    in_specs = (P(None, "gx", "gy", None),)
    out_specs = (
        P(None, None, "gx", "gy", None),
        P(None, "gx", "gy", None),
        P(None, None, "gx", "gy", None),
        P(None, "gx", "gy", None),
        P(None, None, "gx", "gy", None),
        P(None, "gx", "gy", None),
        P(None, "gx", "gy", None),
    )
    return jax.shard_map(body, mesh=mesh, in_specs=in_specs, out_specs=out_specs, check_vma=False)
```
